32 devices in a mesh: dp: 8 (over z, y), mp: 4 (over x, core).
Axes of the slice: x: 2, y: 2, z: 4, core: 2. Of those that a mesh axis runs over, the one named last changes fastest.
Arguments:
- clean_latent: float32 [64, 1024, 512], P(('dp', 'mp')), may hold values from -6 to 6
- noise_latent: float32 [64, 1024, 512], P(('dp', 'mp')), may hold values from -6 to 6
- codec_tokens: bfloat16 [64, 512, 768], P(('dp', 'mp')), may hold values from -6 to 6
- codec_mask: int32 [64, 512], P(('dp', 'mp')), may hold values from 0 to 1, as said below
- frames: int32 [64], P(('dp', 'mp')), may hold values from 25 to 128, as said below
- timesteps: int32 [64], P(('dp', 'mp')), may hold values from 0 to 999
- out_cotangent: float32 [64, 1024, 512], P(('dp', 'mp')), may hold values from -6 to 6
- master_blocks: float32 [240, 128, 128], P('mp', 'dp'), may hold values from -6 to 6
- norm_params: float32 [6, 512], P(None, ('dp', 'mp'))
- owned_block: int32 [240], replicated, may hold values from 0 to 239, each once
- left_stats: float32 [240, 128, 128], P('mp', 'dp')
- right_stats: float32 [240, 128, 128], P('mp', 'dp')
- left_root: float32 [240, 128, 128], P('mp')
- right_root: float32 [240, 128, 128], P('mp')
Outputs:
- block_output: float32 [64, 1024, 512], P(('dp', 'mp'))
- input_grad: float32 [64, 1024, 512], P(('dp', 'mp'))
- owned_grad: float32 [240, 128, 128], P('mp', 'dp')
- new_left: float32 [240, 128, 128], P('mp', 'dp')
- new_right: float32 [240, 128, 128], P('mp', 'dp')
- new_master: float32 [240, 128, 128], P('mp', 'dp')
- master_copy: bfloat16 [240, 128, 128], P('mp', 'dp')
- norm_grads: float32 [6, 512], P(None, ('dp', 'mp'))
- new_norm: float32 [6, 512], P(None, ('dp', 'mp'))
The draws below stay inside these ranges and needn't reach their ends.
Inputs may be any that keep to these rules, and one draw needn't show every extreme that they name: frames[c] counts the clip's valid latent frames; cells of later frames are padding. codec_mask[c, l] is 1 only where l < 4 * frames[c], and codec_mask[c, 0] is 1. A permutation: slot s holds block owned_block[s]; slots s of mp index s // (240 / number of mp devices).
All inputs are finite; a program needn't handle non-finite values.
Results may differ from the reference program's by a relative error of at most 0.0095.
The reference program's roundings to bfloat16 on the way count: a program that leaves them out, or rounds other values in their place, can miss the bound.
Values may be sent and summed in bfloat16 or wider, within the bound.
No kernel may reach another device: no remote copies, remote signals or barrier semaphores. Data moves between devices by JAX's collectives and lax.ppermute only.
A program may use at most 256 MiB of HBM per device.

```python
import math
import jax
import jax.numpy as jnp
from jax import lax

LATENT_CHANNELS = 512
GROUPS = 32
HEADS = 8
HEADDIM = 64
CTX = 768
BINS = 8
MAXF = 128
MINF = 25
TSTEPS = 1000
BS = 128
POS = 1024
CTXLEN = 512
NBLK = 240
CLIPS = 64


def clip_lengths(key):
    base_key = jax.random.fold_in(key, 11)
    key_len, key_where = jax.random.split(base_key)
    lengths = jax.random.randint(key_len, (CLIPS,), MINF, MAXF + 1)
    chosen = jax.random.randint(key_where, (), 0, CLIPS)
    indices = jnp.arange(CLIPS)
    lengths = jnp.where(indices == chosen, MAXF, lengths)
    lengths = jnp.where(indices == (chosen + 1) % CLIPS, MINF, lengths)
    return lengths.astype(jnp.int32)


def draw_frames(key, part):
    return clip_lengths(key)


def draw_codec_mask(key, part):
    lengths = clip_lengths(key)
    holes = jax.random.randint(jax.random.fold_in(key, 12), (CLIPS, CTXLEN), 0, 8)
    places = jnp.arange(CTXLEN)[None, :]
    keep_slot = (holes != 0) | (places == 0)
    valid = (places < 4 * lengths[:, None]) & keep_slot
    return valid.astype(jnp.int32)


def draw_norm_params(key, part):
    key_gain, key_shift = jax.random.split(jax.random.fold_in(key, 41))
    gains = 1.0 + 0.3 * jax.random.uniform(key_gain, (2, LATENT_CHANNELS), minval=-1.0, maxval=1.0)
    shifts = 0.5 * jax.random.normal(key_shift, (4, LATENT_CHANNELS))
    return jnp.stack([gains[0], shifts[0], shifts[1], gains[1], shifts[2], shifts[3]]).astype(jnp.float32)


def symmetric_part(key, lowest, highest_diag):
    key_noise, key_diag = jax.random.split(key)
    noise = jax.random.normal(key_noise, (NBLK, BS, BS))
    sym_noise = (noise + jnp.swapaxes(noise, 1, 2)) * (1.0 / math.sqrt(2.0))
    diag_vals = jax.random.uniform(key_diag, (NBLK, BS), minval=lowest, maxval=highest_diag)
    return jnp.eye(BS)[None] * diag_vals[:, :, None] + 0.3 * sym_noise / math.sqrt(BS)


def statistics(key):
    key_level = jax.random.fold_in(key, 5)
    shape_part = symmetric_part(key, 0.5, 2.0)
    level = jax.random.uniform(key_level, (NBLK, 1, 1), minval=1.0, maxval=4.0)
    grad_square = 0.09 * BS * CLIPS * POS / LATENT_CHANNELS
    return (level * grad_square * shape_part).astype(jnp.float32)


def roots(key):
    key_level = jax.random.fold_in(key, 6)
    shape_part = symmetric_part(key, 0.5, 2.0)
    level = jnp.exp(jax.random.uniform(key_level, (NBLK, 1, 1), minval=math.log(0.5), maxval=math.log(2.0)))
    return (level * shape_part).astype(jnp.float32)


def draw_left_stats(key, part):
    return statistics(jax.random.fold_in(key, 21))


def draw_right_stats(key, part):
    return statistics(jax.random.fold_in(key, 22))


def draw_left_root(key, part):
    return roots(jax.random.fold_in(key, 31))


def draw_right_root(key, part):
    return roots(jax.random.fold_in(key, 32))


def place_ends(values, rng, smallest, high):
    longest = values.shape.index(max(values.shape))
    spots = []
    for shift in (0, 1):
        where = [jax.random.randint(jax.random.fold_in(rng, axis), (), 0, length) for axis, length in enumerate(values.shape)]
        where[longest] = (where[longest] + shift) % values.shape[longest]
        spots.append(tuple(where))
    return values.at[spots[0]].set(smallest).at[spots[1]].set(high)


def level_of(key, dims, pieces, low, high):
    loudness, own = 1.0, jax.random.fold_in(key, 6)
    for dim, parts in pieces:
        draws = jnp.exp(jax.random.uniform(jax.random.fold_in(own, dim), (parts,), jnp.float32, low / len(pieces), high / len(pieces)))
        loudness = loudness * jnp.repeat(draws, dims[dim] // parts).reshape([-1 if axis == dim else 1 for axis in range(len(dims))])
    return loudness


def normal_values(rng, dims, spread, limit, shards=(), kind=jnp.bfloat16):
    array = jax.random.normal(rng, dims, jnp.float32) * spread
    if len(shards) > 0:
        array = level_of(rng, dims, shards, -0.22, 0.18) * array
    return jnp.clip(array, min=-limit, max=limit).astype(kind)


def setup_inputs(seed: int = 0) -> dict:
    keys = jax.random.split(jax.random.key(seed), 15)
    clean_latent = normal_values(keys[0], (CLIPS, POS, LATENT_CHANNELS), 1.0, 6.0, ((0, 32),), jnp.float32)
    noise_latent = normal_values(keys[1], (CLIPS, POS, LATENT_CHANNELS), 1.0, 6.0, ((0, 32),), jnp.float32)
    codec_tokens = normal_values(keys[2], (CLIPS, CTXLEN, CTX), 1.0, 6.0, ((0, 32),))
    codec_mask = draw_codec_mask(jax.random.fold_in(keys[14], 71), 0)
    frames = draw_frames(jax.random.fold_in(keys[14], 71), 0)
    timesteps = place_ends(jax.random.randint(keys[5], (CLIPS,), 0, TSTEPS), jax.random.fold_in(keys[5], 1), 0, TSTEPS - 1).astype(jnp.int32)
    out_cotangent = normal_values(keys[6], (CLIPS, POS, LATENT_CHANNELS), 1.0, 6.0, ((0, 32),), jnp.float32)
    master_blocks = normal_values(keys[7], (NBLK, BS, BS), 1.0, 6.0, ((0, 4), (1, 8)), jnp.float32)
    norm_params = draw_norm_params(jax.random.fold_in(keys[14], 71), 0)
    owned_block = jax.random.permutation(keys[9], NBLK).astype(jnp.int32)
    left_stats = draw_left_stats(jax.random.fold_in(keys[14], 71), 0)
    right_stats = draw_right_stats(jax.random.fold_in(keys[14], 71), 0)
    left_root = draw_left_root(jax.random.fold_in(keys[14], 71), 0)
    right_root = draw_right_root(jax.random.fold_in(keys[14], 71), 0)
    return {"clean_latent": clean_latent, "noise_latent": noise_latent, "codec_tokens": codec_tokens, "codec_mask": codec_mask, "frames": frames, "timesteps": timesteps, "out_cotangent": out_cotangent, "master_blocks": master_blocks, "norm_params": norm_params, "owned_block": owned_block, "left_stats": left_stats, "right_stats": right_stats, "left_root": left_root, "right_root": right_root}


@jax.custom_vjp
def low(v):
    return lax.optimization_barrier(v.astype(jnp.bfloat16)).astype(jnp.float32)

@jax.custom_vjp
def low_back(v):
    return v

def low_keep(v):
    return (low(v), None)

def low_pass(kept, grad):
    return (grad,)

def back_keep(v):
    return (v, None)

def back_low(kept, grad):
    return (low(grad),)
low.defvjp(low_keep, low_pass)
low_back.defvjp(back_keep, back_low)
highest = lax.Precision.HIGHEST
learn_rate = 0.5
out_gain = 8.0

def unblock(blocks, first_block, row_count, col_count):
    amount = row_count // BS * (col_count // BS)
    block_part = blocks[first_block:first_block + amount]
    return block_part.reshape(row_count // BS, col_count // BS, BS, BS).transpose(0, 2, 1, 3).reshape(row_count, col_count)

def matrices(blocks):
    square = LATENT_CHANNELS // BS * (LATENT_CHANNELS // BS)
    conv_taps = jnp.stack([unblock(blocks, tap_index * square, LATENT_CHANNELS, LATENT_CHANNELS) for tap_index in range(9)])
    offset = 9 * square
    temb_w = unblock(blocks, offset, LATENT_CHANNELS, LATENT_CHANNELS)
    query_w = unblock(blocks, offset + square, LATENT_CHANNELS, LATENT_CHANNELS)
    out_w = unblock(blocks, offset + 2 * square, LATENT_CHANNELS, LATENT_CHANNELS)
    key_w = unblock(blocks, offset + 3 * square, CTX, LATENT_CHANNELS)
    value_w = unblock(blocks, offset + 3 * square + CTX // BS * (LATENT_CHANNELS // BS), CTX, LATENT_CHANNELS)
    return (conv_taps, temb_w, query_w, out_w, key_w, value_w)

def group_norm(values, frame_mask, gain_row, shift_row):
    group_width = LATENT_CHANNELS // GROUPS
    grouped = values.reshape(values.shape[:-1] + (GROUPS, group_width))
    mask_wide = frame_mask[..., None, None]
    counted = lax.optimization_barrier(jnp.sum(frame_mask, axis=-1)) * group_width
    group_mean = lax.optimization_barrier(jnp.sum(grouped * mask_wide, axis=(-3, -1))) / counted[..., None]
    centred = grouped - group_mean[..., None, :, None]
    group_var = lax.optimization_barrier(jnp.sum(centred * centred * mask_wide, axis=(-3, -1))) / counted[..., None]
    normed = centred * lax.rsqrt(group_var + 1e-05)[..., None, :, None]
    return normed.reshape(values.shape) * gain_row + shift_row

def sinusoid(timesteps):
    half_width = LATENT_CHANNELS // 2
    freqs = jnp.exp(-math.log(10000.0) * jnp.arange(half_width, dtype=jnp.float32) / half_width)
    angles = timesteps.astype(jnp.float32)[:, None] * freqs[None, :]
    return jnp.concatenate([jnp.sin(angles), jnp.cos(angles)], axis=-1)

def convolve(acts, conv_taps):
    padded = jnp.pad(acts.reshape(MAXF, BINS, LATENT_CHANNELS), ((1, 1), (1, 1), (0, 0)))
    summed = jnp.zeros((POS, LATENT_CHANNELS), jnp.float32)
    for tap_index in range(9):
        frame_off, bin_off = divmod(tap_index, 3)
        window = padded[frame_off:frame_off + MAXF, bin_off:bin_off + BINS].reshape(POS, LATENT_CHANNELS)
        summed = summed + jnp.dot(window, conv_taps[tap_index], precision=highest)
    return summed

def clip_block(matrix_set, params, latents, frame_mask, context, key_mask, embedding):
    conv_taps, temb_w, query_w, out_w, key_w, value_w = matrix_set
    first = group_norm(latents, frame_mask, params[0], params[1])
    acts = low(jax.nn.silu(first) * frame_mask[:, None])
    conv_out = low_back(convolve(acts, conv_taps) * (1.0 / math.sqrt(9 * LATENT_CHANNELS)))
    step_emb = low_back(jnp.dot(embedding[None, :], temb_w, precision=highest) * (1.0 / math.sqrt(LATENT_CHANNELS)))
    residual = latents + conv_out + step_emb + params[2]
    normed = low(group_norm(residual, frame_mask, params[3], params[4]))
    queries = low(low_back(jnp.dot(normed, query_w, precision=highest) * (1.0 / math.sqrt(LATENT_CHANNELS))))
    key_rows = low(low_back(jnp.dot(context, key_w, precision=highest) * (1.0 / math.sqrt(CTX))))
    value_rows = low(low_back(jnp.dot(context, value_w, precision=highest) * (1.0 / math.sqrt(CTX))))
    query_heads = queries.reshape(POS, HEADS, HEADDIM)
    key_heads = key_rows.reshape(CTXLEN, HEADS, HEADDIM)
    value_heads = value_rows.reshape(CTXLEN, HEADS, HEADDIM)
    scores = low_back(jnp.einsum('phd,lhd->hpl', query_heads, key_heads, precision=highest) * (1.0 / math.sqrt(HEADDIM)))
    scores = jnp.where(key_mask[None, None, :] > 0, scores, -1000000000.0)
    attn_probs = low(jax.nn.softmax(scores, axis=-1))
    mixed = low(low_back(jnp.einsum('hpl,lhd->phd', attn_probs, value_heads, precision=highest).reshape(POS, LATENT_CHANNELS)))
    projected = low_back(jnp.dot(mixed, out_w, precision=highest) * (out_gain / math.sqrt(LATENT_CHANNELS))) + params[5]
    return frame_mask[:, None] * (residual + projected)

def reference(clean_latent, noise_latent, codec_tokens, codec_mask, frames, timesteps, out_cotangent, master_blocks, norm_params, owned_block, left_stats, right_stats, left_root, right_root):
    frame_of = jnp.arange(POS, dtype=jnp.int32) // BINS
    frame_mask = (frame_of[None, :] < frames[:, None]).astype(jnp.float32)
    phases = timesteps.astype(jnp.float32) * (0.5 * math.pi / TSTEPS)
    inputs = frame_mask[:, :, None] * (jnp.cos(phases)[:, None, None] * clean_latent + jnp.sin(phases)[:, None, None] * noise_latent)
    embedding = low(jax.nn.silu(sinusoid(timesteps)))
    contexts = codec_tokens.astype(jnp.float32)
    key_mask = codec_mask.astype(jnp.float32)

    def forward(blocks, params, latents):
        matrix_set = matrices(low(blocks))
        params_low = low(params)
        checked = jax.checkpoint(clip_block)

        def one_clip(clip_item):
            return checked(matrix_set, params_low, clip_item[0], clip_item[1], clip_item[2], clip_item[3], clip_item[4])
        return lax.map(one_clip, (latents, frame_mask, contexts, key_mask, embedding))
    outputs, pullback = jax.vjp(forward, master_blocks, norm_params, inputs)
    grad_blocks, grad_params, grad_inputs = pullback(out_cotangent)
    owned = grad_blocks[owned_block]
    new_left = 0.5 * left_stats + 0.5 * jnp.einsum('srk,stk->srt', owned, owned, precision=highest)
    new_right = 0.5 * right_stats + 0.5 * jnp.einsum('skr,skt->srt', owned, owned, precision=highest)
    left_side = jnp.einsum('srk,skt->srt', left_root, owned, precision=highest)
    update = jnp.einsum('srk,skt->srt', left_side, right_root, precision=highest)
    update_step = learn_rate * update * lax.rsqrt(lax.optimization_barrier(jnp.mean(update * update, axis=(1, 2), keepdims=True)) + 1e-06)
    new_master = master_blocks.at[owned_block].add(-update_step)
    small_rate = 0.5 / math.sqrt(CLIPS * POS)
    new_norm = norm_params - small_rate * grad_params
    return (outputs, grad_inputs, owned, new_left, new_right, new_master, new_master.astype(jnp.bfloat16), grad_params, new_norm)
```

```python
import functools
import math

import jax
import jax.numpy as jnp
from jax import lax
from jax.experimental import pallas as pl
from jax.experimental.pallas import tpu as pltpu
from jax.sharding import PartitionSpec as P

LATENT_CHANNELS = 512
GROUPS = 32
HEADS = 8
HEADDIM = 64
CTX = 768
BINS = 8
TSTEPS = 1000
BS = 128
POS = 1024
CH = LATENT_CHANNELS

highest = lax.Precision.HIGHEST
learn_rate = 0.5
out_gain = 8.0
eps = 1e-05

CONV_SCALE = 1.0 / math.sqrt(9 * CH)
INV_WIDTH = 1.0 / math.sqrt(CH)
INV_CTX = 1.0 / math.sqrt(CTX)
OUT_SCALE = out_gain / math.sqrt(CH)
ATT_SCALE = 1.0 / math.sqrt(HEADDIM)

SQ = (CH // BS) * (CH // BS)
KV = (CTX // BS) * (CH // BS)
TEMB0 = 9 * SQ
QUERY0 = TEMB0 + SQ
OUT0 = QUERY0 + SQ
KEY0 = OUT0 + SQ
VALUE0 = KEY0 + KV
NBLK = VALUE0 + KV

F32 = jnp.float32
BF16 = jnp.bfloat16
VMEM_LIMIT = 60 * 1024 * 1024


def nt(a, b):
    return lax.dot_general(a, b, (((1,), (1,)), ((), ())), preferred_element_type=F32)


def nn(a, b):
    return lax.dot_general(a, b, (((1,), (0,)), ((), ())), preferred_element_type=F32)


def mat(ref, base, nr, nc):
    rows = [jnp.concatenate([ref[base + a * nc + b] for b in range(nc)], axis=1) for a in range(nr)]
    return jnp.concatenate(rows, axis=0)


def row_iota(start, count):
    return lax.broadcasted_iota(jnp.int32, (count, 1), 0) + start


def fold8(x):
    return jnp.sum(x.reshape(-1, 8, x.shape[-1]), axis=0)


def group_sums(rows8, gmat):
    total = jnp.broadcast_to(jnp.sum(rows8, axis=0, keepdims=True), (8, CH))
    return lax.dot_general(
        total, gmat, (((1,), (0,)), ((), ())), preferred_element_type=F32, precision=highest
    )[0:1]


def group_matrix():
    i = lax.broadcasted_iota(jnp.int32, (CH, CH), 0) // (CH // GROUPS)
    j = lax.broadcasted_iota(jnp.int32, (CH, CH), 1) // (CH // GROUPS)
    return (i == j).astype(F32)


def shift_bins(tile, step):
    if step == 0:
        return tile
    t = tile.reshape(-1, 8, tile.shape[-1])
    rolled = pltpu.roll(t, (8 - step) % 8, 1)
    b = lax.broadcasted_iota(jnp.int32, (1, 8, 1), 1) + step
    keep = (b >= 0) & (b < 8)
    return jnp.where(keep, rolled, 0.0).reshape(tile.shape)


def write_windows(pad, e_ref, o_ref, sign):
    T = 64

    def body(i, carry):
        r = pl.multiple_of(i * T, T)
        mid = pad[pl.ds(r + 8, T), :]
        low = pad[pl.ds(r, T), :]
        for d in range(3):
            step = sign * (d - 1)
            e_ref[0, d, pl.ds(r, T), :] = shift_bins(mid, step).astype(BF16)
            o_ref[0, d, pl.ds(r, T), :] = shift_bins(low, step).astype(BF16)
        return carry

    lax.fori_loop(0, POS // T, body, 0)
    last = pad[POS : POS + 16, :]
    for d in range(3):
        o_ref[0, d, POS : POS + 16, :] = shift_bins(last, sign * (d - 1)).astype(BF16)


def window(e_ref, o_ref, df, db, r, n, lead=(0,)):
    if df == 1:
        return e_ref[lead + (db, pl.ds(r, n), slice(None))]
    off = 0 if df == 0 else 16
    return o_ref[lead + (db, pl.ds(pl.multiple_of(r + off, 16), n), slice(None))]


def pre_kernel(frames_s, trig_s, clean, noise, cot, inp, outlow, stats, obias):
    c = pl.program_id(0)
    rows = frames_s[c] * BINS
    cs, sn = trig_s[0, c], trig_s[1, c]
    T = 64
    zero = jnp.zeros((8, CH), F32)
    gmat = group_matrix()
    inv_n = 1.0 / (rows * (CH // GROUPS)).astype(F32)

    def first(i, carry):
        s0, s1 = carry
        r = pl.multiple_of(i * T, T)
        m = row_iota(r, T) < rows
        x = jnp.where(m, cs * clean[0, pl.ds(r, T), :] + sn * noise[0, pl.ds(r, T), :], 0.0)
        inp[0, pl.ds(r, T), :] = x
        g = jnp.where(m, cot[0, pl.ds(r, T), :], 0.0)
        outlow[0, pl.ds(r, T), :] = g.astype(BF16)
        return (s0 + fold8(x), s1 + fold8(g))

    s0, s1 = lax.fori_loop(0, POS // T, first, (zero, zero))
    mean = group_sums(s0, gmat) * inv_n

    def second(i, s):
        r = pl.multiple_of(i * T, T)
        m = row_iota(r, T) < rows
        d = jnp.where(m, inp[0, pl.ds(r, T), :] - mean, 0.0)
        return s + fold8(d * d)

    s2 = lax.fori_loop(0, POS // T, second, zero)
    rstd = lax.rsqrt(group_sums(s2, gmat) * inv_n + eps)
    stats[0] = jnp.concatenate([mean, rstd, jnp.zeros((6, CH), F32)], axis=0)
    obias[0] = s1


def pre(frames, trig, clean, noise, cot):
    n = clean.shape[0]
    big = pl.BlockSpec((1, POS, CH), lambda c, *_: (c, 0, 0))
    small = pl.BlockSpec((1, 8, CH), lambda c, *_: (c, 0, 0))
    return pl.pallas_call(
        pre_kernel,
        out_shape=(
            jax.ShapeDtypeStruct((n, POS, CH), F32),
            jax.ShapeDtypeStruct((n, POS, CH), BF16),
            jax.ShapeDtypeStruct((n, 8, CH), F32),
            jax.ShapeDtypeStruct((n, 8, CH), F32),
        ),
        grid_spec=pltpu.PrefetchScalarGridSpec(
            num_scalar_prefetch=2, grid=(n,), in_specs=[big, big, big], out_specs=[big, big, small, small]
        ),
        compiler_params=pltpu.CompilerParams(vmem_limit_bytes=VMEM_LIMIT),
        cost_estimate=pl.CostEstimate(flops=n * POS * CH * 20, bytes_accessed=n * POS * CH * 18, transcendentals=0),
        name="inputs_stats",
    )(frames, trig, clean, noise, cot)


def acts_kernel(frames_s, inp, stats, params, e_ref, o_ref, pad):
    c = pl.program_id(0)
    rows = frames_s[c] * BINS
    T = 64
    mean, rstd = stats[0, 0:1], stats[0, 1:2]
    scale = rstd * params[0:1]
    shift = params[1:2]
    pad[0:8, :] = jnp.zeros((8, CH), F32)
    pad[8 + POS :, :] = jnp.zeros((8, CH), F32)

    def body(i, carry):
        r = pl.multiple_of(i * T, T)
        m = row_iota(r, T) < rows
        y = (inp[0, pl.ds(r, T), :] - mean) * scale + shift
        a = jnp.where(m, y * jax.nn.sigmoid(y), 0.0)
        pad[pl.ds(r + 8, T), :] = a
        return carry

    lax.fori_loop(0, POS // T, body, 0)
    write_windows(pad, e_ref, o_ref, 1)


def acts_windows(frames, inp, stats, params):
    n = inp.shape[0]
    return pl.pallas_call(
        acts_kernel,
        out_shape=(
            jax.ShapeDtypeStruct((n, 3, POS, CH), BF16),
            jax.ShapeDtypeStruct((n, 3, POS + 16, CH), BF16),
        ),
        grid_spec=pltpu.PrefetchScalarGridSpec(
            num_scalar_prefetch=1,
            grid=(n,),
            in_specs=[
                pl.BlockSpec((1, POS, CH), lambda c, *_: (c, 0, 0)),
                pl.BlockSpec((1, 8, CH), lambda c, *_: (c, 0, 0)),
                pl.BlockSpec((8, CH), lambda c, *_: (0, 0)),
            ],
            out_specs=[
                pl.BlockSpec((1, 3, POS, CH), lambda c, *_: (c, 0, 0, 0)),
                pl.BlockSpec((1, 3, POS + 16, CH), lambda c, *_: (c, 0, 0, 0)),
            ],
            scratch_shapes=[pltpu.VMEM((POS + 16, CH), F32)],
        ),
        compiler_params=pltpu.CompilerParams(vmem_limit_bytes=VMEM_LIMIT),
        cost_estimate=pl.CostEstimate(
            flops=n * POS * CH * 30, bytes_accessed=n * POS * CH * 16, transcendentals=n * POS * CH
        ),
        name="acts",
    )(frames, inp, stats, params)


def conv_kernel(frames_s, e_ref, o_ref, inp, emb, params, w, res, normed, stats):
    c = pl.program_id(0)
    rows = frames_s[c] * BINS
    R = 256
    T = 64
    zero = jnp.zeros((8, CH), F32)
    gmat = group_matrix()
    inv_n = 1.0 / (rows * (CH // GROUPS)).astype(F32)
    temb = nn(emb[0], mat(w, TEMB0, 4, 4))[0:1] * INV_WIDTH
    add = temb + params[2:3]

    def tile(i, s):
        r = pl.multiple_of(i * R, R)
        acc = jnp.zeros((R, CH), F32)
        for t in range(9):
            df, db = divmod(t, 3)
            acc = acc + nn(window(e_ref, o_ref, df, db, r, R), mat(w, t * SQ, 4, 4))
        v = inp[0, pl.ds(r, R), :] + acc * CONV_SCALE + add
        res[0, pl.ds(r, R), :] = v
        return s + fold8(jnp.where(row_iota(r, R) < rows, v, 0.0))

    s = lax.fori_loop(0, POS // R, tile, zero)
    mean = group_sums(s, gmat) * inv_n

    def second(i, s):
        r = pl.multiple_of(i * T, T)
        d = jnp.where(row_iota(r, T) < rows, res[0, pl.ds(r, T), :] - mean, 0.0)
        return s + fold8(d * d)

    s2 = lax.fori_loop(0, POS // T, second, zero)
    rstd = lax.rsqrt(group_sums(s2, gmat) * inv_n + eps)
    scale = rstd * params[3:4]
    shift = params[4:5]

    def third(i, carry):
        r = pl.multiple_of(i * T, T)
        normed[0, pl.ds(r, T), :] = ((res[0, pl.ds(r, T), :] - mean) * scale + shift).astype(BF16)
        return carry

    lax.fori_loop(0, POS // T, third, 0)
    stats[0] = jnp.concatenate([mean, rstd, jnp.zeros((6, CH), F32)], axis=0)


def whole(shape):
    return pl.BlockSpec(shape, lambda *_: (0,) * len(shape), pipeline_mode=pl.Buffered(1))


def per_clip(shape):
    return pl.BlockSpec((1,) + shape, lambda c, *_: (c,) + (0,) * len(shape))


def conv_forward(frames, e, o, inp, emb, params, w):
    n = inp.shape[0]
    return pl.pallas_call(
        conv_kernel,
        out_shape=(
            jax.ShapeDtypeStruct((n, POS, CH), F32),
            jax.ShapeDtypeStruct((n, POS, CH), BF16),
            jax.ShapeDtypeStruct((n, 8, CH), F32),
        ),
        grid_spec=pltpu.PrefetchScalarGridSpec(
            num_scalar_prefetch=1,
            grid=(n,),
            in_specs=[
                per_clip((3, POS, CH)),
                per_clip((3, POS + 16, CH)),
                per_clip((POS, CH)),
                per_clip((16, CH)),
                whole((8, CH)),
                pl.BlockSpec((QUERY0, BS, BS), lambda *_: (0, 0, 0), pipeline_mode=pl.Buffered(1)),
            ],
            out_specs=[per_clip((POS, CH)), per_clip((POS, CH)), per_clip((8, CH))],
        ),
        compiler_params=pltpu.CompilerParams(vmem_limit_bytes=VMEM_LIMIT),
        cost_estimate=pl.CostEstimate(
            flops=n * POS * CH * CH * 18, bytes_accessed=n * POS * CH * 22 + 5000000, transcendentals=0
        ),
        name="conv_forward",
    )(frames, e, o, inp, emb, params, w)


def attn_kernel(
    frames_s, normed, tokens, tok_t, kmask, outlow, res, params, w,
    block_out, dq_ref, dw_ref,
    q_s, do_s, kv_s, qt_s, dot_s, mixed_s, dkt_s, dvt_s, dkv_acc,
):
    c = pl.program_id(0)
    rows = frames_s[c] * BINS
    R = 256
    query_w = mat(w, 0, 4, 4)
    out_w = mat(w, SQ, 4, 4)
    key_w = mat(w, 2 * SQ, CTX // BS, 4)
    value_w = mat(w, 2 * SQ + KV, CTX // BS, 4)

    def project(i, carry):
        r = pl.multiple_of(i * R, R)
        q = (nn(normed[0, pl.ds(r, R), :], query_w) * INV_WIDTH).astype(BF16)
        q_s[pl.ds(r, R), :] = q
        qt_s[:, pl.ds(r, R)] = q.T
        d = (nt(outlow[0, pl.ds(r, R), :], out_w) * OUT_SCALE).astype(BF16)
        do_s[pl.ds(r, R), :] = d
        dot_s[:, pl.ds(r, R)] = d.T
        return carry

    lax.fori_loop(0, POS // R, project, 0)
    kv_s[0] = ((nn(tokens[0], key_w) * INV_CTX).astype(BF16).astype(F32) * ATT_SCALE).astype(BF16)
    kv_s[1] = (nn(tokens[0], value_w) * INV_CTX).astype(BF16)
    valid = kmask[0, 0:1, :] > 0.0
    lane = lax.broadcasted_iota(jnp.int32, (1, BS), 1)
    first = lane < HEADDIM

    for slab in range(HEADS // 2):
        cols = slice(slab * BS, (slab + 1) * BS)
        k2, v2 = kv_s[0, :, cols], kv_s[1, :, cols]
        none = jnp.zeros_like(k2)
        ks = (jnp.where(first, k2, none), jnp.where(first, none, k2))
        vs = (jnp.where(first, v2, none), jnp.where(first, none, v2))
        dkv_acc[...] = jnp.zeros_like(dkv_acc)

        def tile(i, carry):
            r = pl.multiple_of(i * R, R)
            q = q_s[pl.ds(r, R), cols]
            d = do_s[pl.ds(r, R), cols]
            o = jnp.zeros((R, BS), F32)
            dq = jnp.zeros((R, BS), F32)
            for h in range(2):
                s = jnp.where(valid, nt(q, ks[h]), -1000000000.0)
                e = jnp.exp(s - jnp.max(s, axis=-1, keepdims=True))
                p = e * (1.0 / jnp.sum(e, axis=-1, keepdims=True))
                pb = p.astype(BF16)
                dp = nt(d, vs[h])
                delta = jnp.sum(p * dp, axis=-1, keepdims=True)
                ds = (p * (dp - delta)).astype(BF16)
                o = o + nn(pb, vs[h])
                dq = dq + nn(ds, ks[h])
                half = slice(slab * BS + h * HEADDIM, slab * BS + (h + 1) * HEADDIM)
                mine = slice(h * HEADDIM, (h + 1) * HEADDIM)
                dkv_acc[0, mine, :] += nn(qt_s[half, pl.ds(r, R)], ds)
                dkv_acc[1, mine, :] += nn(dot_s[half, pl.ds(r, R)], pb)
            mixed_s[pl.ds(r, R), cols] = o.astype(BF16)
            dq_ref[0, pl.ds(r, R), cols] = dq.astype(BF16)
            return carry

        lax.fori_loop(0, POS // R, tile, 0)
        dkt_s[cols, :] = (dkv_acc[0] * ATT_SCALE).astype(BF16)
        dvt_s[cols, :] = dkv_acc[1].astype(BF16)

    def project_out(i, carry):
        r = pl.multiple_of(i * R, R)
        proj = nn(mixed_s[pl.ds(r, R), :], out_w) * OUT_SCALE + params[5:6]
        m = row_iota(r, R) < rows
        block_out[0, pl.ds(r, R), :] = jnp.where(m, res[0, pl.ds(r, R), :] + proj, 0.0)
        return carry

    lax.fori_loop(0, POS // R, project_out, 0)

    @pl.when(c == 0)
    def _():
        dw_ref[...] = jnp.zeros_like(dw_ref)

    dw_ref[0:CH, :] += nn(normed[0].T, dq_ref[0])
    dw_ref[CH : 2 * CH, :] += nn(mixed_s[...].T, outlow[0])
    dw_ref[2 * CH : 2 * CH + CTX, :] += nt(tok_t[0], dkt_s[...])
    dw_ref[2 * CH + CTX :, :] += nt(tok_t[0], dvt_s[...])


def attention(frames, normed, tokens, tok_t, kmask, outlow, res, params, w):
    n = normed.shape[0]
    ctx_len = tokens.shape[1]
    amount = 2 * SQ + 2 * KV
    return pl.pallas_call(
        attn_kernel,
        out_shape=(
            jax.ShapeDtypeStruct((n, POS, CH), F32),
            jax.ShapeDtypeStruct((n, POS, CH), BF16),
            jax.ShapeDtypeStruct((2 * CH + 2 * CTX, CH), F32),
        ),
        grid_spec=pltpu.PrefetchScalarGridSpec(
            num_scalar_prefetch=1,
            grid=(n,),
            in_specs=[
                per_clip((POS, CH)),
                per_clip((ctx_len, CTX)),
                per_clip((CTX, ctx_len)),
                per_clip((8, ctx_len)),
                per_clip((POS, CH)),
                per_clip((POS, CH)),
                whole((8, CH)),
                whole((amount, BS, BS)),
            ],
            out_specs=[
                per_clip((POS, CH)),
                per_clip((POS, CH)),
                pl.BlockSpec((2 * CH + 2 * CTX, CH), lambda *_: (0, 0)),
            ],
            scratch_shapes=[
                pltpu.VMEM((POS, CH), BF16),
                pltpu.VMEM((POS, CH), BF16),
                pltpu.VMEM((2, ctx_len, CH), BF16),
                pltpu.VMEM((CH, POS), BF16),
                pltpu.VMEM((CH, POS), BF16),
                pltpu.VMEM((POS, CH), BF16),
                pltpu.VMEM((CH, ctx_len), BF16),
                pltpu.VMEM((CH, ctx_len), BF16),
                pltpu.VMEM((2, BS, ctx_len), F32),
            ],
        ),
        compiler_params=pltpu.CompilerParams(vmem_limit_bytes=VMEM_LIMIT),
        cost_estimate=pl.CostEstimate(
            flops=n * POS * CH * (6 * CH * 2 + 24 * ctx_len),
            bytes_accessed=n * POS * CH * 16,
            transcendentals=n * POS * HEADS * ctx_len,
        ),
        name="attention",
    )(frames, normed, tokens, tok_t, kmask, outlow, res, params, w)


def norm2_kernel(frames_s, dq_ref, res, stats, cot, params, w, rgrad, e_ref, o_ref, sums, ng_s, pad):
    c = pl.program_id(0)
    rows = frames_s[c] * BINS
    R = 256
    T = 64
    zero = jnp.zeros((8, CH), F32)
    gmat = group_matrix()
    inv_n = 1.0 / (rows * (CH // GROUPS)).astype(F32)
    mean, rstd = stats[0, 0:1], stats[0, 1:2]
    gain = params[3:4]
    query_w = mat(w, 0, 4, 4)

    def first(i, carry):
        s0, s1 = carry
        r = pl.multiple_of(i * R, R)
        ng = nt(dq_ref[0, pl.ds(r, R), :], query_w) * INV_WIDTH
        m = row_iota(r, R) < rows
        ng = jnp.where(m, ng, 0.0)
        ng_s[pl.ds(r, R), :] = ng
        x = jnp.where(m, (res[0, pl.ds(r, R), :] - mean) * rstd, 0.0)
        return (s0 + fold8(ng), s1 + fold8(ng * x))

    s0, s1 = lax.fori_loop(0, POS // R, first, (zero, zero))
    mh = group_sums(s0 * gain, gmat) * inv_n
    mhx = group_sums(s1 * gain, gmat) * inv_n
    pad[0:8, :] = zero
    pad[8 + POS :, :] = zero

    def second(i, s):
        r = pl.multiple_of(i * T, T)
        m = row_iota(r, T) < rows
        x = (res[0, pl.ds(r, T), :] - mean) * rstd
        d = rstd * (gain * ng_s[pl.ds(r, T), :] - mh - x * mhx)
        g = jnp.where(m, cot[0, pl.ds(r, T), :] + d, 0.0)
        rgrad[0, pl.ds(r, T), :] = g
        pad[pl.ds(r + 8, T), :] = g
        return s + fold8(g)

    s2 = lax.fori_loop(0, POS // T, second, zero)
    sums[0, 0:8] = s2
    sums[0, 8:16] = s1
    sums[0, 16:24] = s0
    write_windows(pad, e_ref, o_ref, -1)


def norm2_backward(frames, dq, res, stats, cot, params, w):
    n = dq.shape[0]
    return pl.pallas_call(
        norm2_kernel,
        out_shape=(
            jax.ShapeDtypeStruct((n, POS, CH), F32),
            jax.ShapeDtypeStruct((n, 3, POS, CH), BF16),
            jax.ShapeDtypeStruct((n, 3, POS + 16, CH), BF16),
            jax.ShapeDtypeStruct((n, 24, CH), F32),
        ),
        grid_spec=pltpu.PrefetchScalarGridSpec(
            num_scalar_prefetch=1,
            grid=(n,),
            in_specs=[
                per_clip((POS, CH)),
                per_clip((POS, CH)),
                per_clip((8, CH)),
                per_clip((POS, CH)),
                whole((8, CH)),
                whole((SQ, BS, BS)),
            ],
            out_specs=[
                per_clip((POS, CH)),
                per_clip((3, POS, CH)),
                per_clip((3, POS + 16, CH)),
                per_clip((24, CH)),
            ],
            scratch_shapes=[pltpu.VMEM((POS, CH), F32), pltpu.VMEM((POS + 16, CH), F32)],
        ),
        compiler_params=pltpu.CompilerParams(vmem_limit_bytes=VMEM_LIMIT),
        cost_estimate=pl.CostEstimate(
            flops=n * POS * CH * CH * 2, bytes_accessed=n * POS * CH * 26, transcendentals=0
        ),
        name="norm2_backward",
    )(frames, dq, res, stats, cot, params, w)


def tap_kernel(at, e_ref, o_ref, out):
    n = e_ref.shape[0]
    for df in range(3):
        acc = None
        for c in range(n):
            g = window(e_ref, o_ref, 2 - df, 0, 0, POS, (c,))
            part = nn(at[:, c * POS : (c + 1) * POS], g)
            acc = part if acc is None else acc + part
        acc = (acc * CONV_SCALE).astype(BF16)
        for a in range(4):
            for b in range(4):
                out[df, 0, a * 4 + b] = acc[a * BS : (a + 1) * BS, b * BS : (b + 1) * BS]


def tap_gradients(at, e, o):
    n = e.shape[0]
    return pl.pallas_call(
        tap_kernel,
        out_shape=jax.ShapeDtypeStruct((3, 3, SQ, BS, BS), BF16),
        grid_spec=pltpu.PrefetchScalarGridSpec(
            num_scalar_prefetch=0,
            grid=(3,),
            in_specs=[
                whole((CH, n * POS)),
                pl.BlockSpec((n, 1, POS, CH), lambda d: (0, d, 0, 0)),
                pl.BlockSpec((n, 1, POS + 16, CH), lambda d: (0, d, 0, 0)),
            ],
            out_specs=pl.BlockSpec((3, 1, SQ, BS, BS), lambda d: (0, d, 0, 0, 0)),
        ),
        compiler_params=pltpu.CompilerParams(vmem_limit_bytes=VMEM_LIMIT),
        cost_estimate=pl.CostEstimate(
            flops=n * POS * CH * CH * 18, bytes_accessed=n * POS * CH * 14 + 5000000, transcendentals=0
        ),
        name="tap_gradients",
    )(at, e, o)


def input_kernel(frames_s, e_ref, o_ref, inp, stats, rgrad, params, w, out, sums, ag_s):
    c = pl.program_id(0)
    rows = frames_s[c] * BINS
    R = 256
    T = 64
    zero = jnp.zeros((8, CH), F32)
    gmat = group_matrix()
    inv_n = 1.0 / (rows * (CH // GROUPS)).astype(F32)
    mean, rstd = stats[0, 0:1], stats[0, 1:2]
    gain, shift = params[0:1], params[1:2]

    def conv(i, carry):
        r = pl.multiple_of(i * R, R)
        acc = jnp.zeros((R, CH), F32)
        for t in range(9):
            df, db = divmod(t, 3)
            acc = acc + nt(window(e_ref, o_ref, 2 - df, db, r, R), mat(w, t * SQ, 4, 4))
        ag_s[pl.ds(r, R), :] = acc * CONV_SCALE
        return carry

    lax.fori_loop(0, POS // R, conv, 0)

    def first(i, carry):
        s0, s1 = carry
        r = pl.multiple_of(i * T, T)
        m = row_iota(r, T) < rows
        x = (inp[0, pl.ds(r, T), :] - mean) * rstd
        y = x * gain + shift
        sg = jax.nn.sigmoid(y)
        dy = jnp.where(m, ag_s[pl.ds(r, T), :] * (sg * (1.0 + y * (1.0 - sg))), 0.0)
        ag_s[pl.ds(r, T), :] = dy
        return (s0 + fold8(dy), s1 + fold8(dy * x))

    s0, s1 = lax.fori_loop(0, POS // T, first, (zero, zero))
    mh = group_sums(s0 * gain, gmat) * inv_n
    mhx = group_sums(s1 * gain, gmat) * inv_n

    def second(i, carry):
        r = pl.multiple_of(i * T, T)
        m = row_iota(r, T) < rows
        x = (inp[0, pl.ds(r, T), :] - mean) * rstd
        d = rstd * (gain * ag_s[pl.ds(r, T), :] - mh - x * mhx)
        out[0, pl.ds(r, T), :] = jnp.where(m, rgrad[0, pl.ds(r, T), :] + d, 0.0)
        return carry

    lax.fori_loop(0, POS // T, second, 0)
    sums[0, 0:8] = s1
    sums[0, 8:16] = s0


def input_backward(frames, e, o, inp, stats, rgrad, params, w):
    n = inp.shape[0]
    return pl.pallas_call(
        input_kernel,
        out_shape=(
            jax.ShapeDtypeStruct((n, POS, CH), F32),
            jax.ShapeDtypeStruct((n, 16, CH), F32),
        ),
        grid_spec=pltpu.PrefetchScalarGridSpec(
            num_scalar_prefetch=1,
            grid=(n,),
            in_specs=[
                per_clip((3, POS, CH)),
                per_clip((3, POS + 16, CH)),
                per_clip((POS, CH)),
                per_clip((8, CH)),
                per_clip((POS, CH)),
                whole((8, CH)),
                pl.BlockSpec((TEMB0, BS, BS), lambda *_: (0, 0, 0), pipeline_mode=pl.Buffered(1)),
            ],
            out_specs=[per_clip((POS, CH)), per_clip((16, CH))],
            scratch_shapes=[pltpu.VMEM((POS, CH), F32)],
        ),
        compiler_params=pltpu.CompilerParams(vmem_limit_bytes=VMEM_LIMIT),
        cost_estimate=pl.CostEstimate(
            flops=n * POS * CH * CH * 18, bytes_accessed=n * POS * CH * 24, transcendentals=n * POS * CH
        ),
        name="input_backward",
    )(frames, e, o, inp, stats, rgrad, params, w)


def to_blocks(matrix):
    r, k = matrix.shape
    return matrix.reshape(r // BS, BS, k // BS, BS).transpose(0, 2, 1, 3).reshape(-1, BS, BS)


def sinusoid(timesteps):
    half_width = CH // 2
    freqs = jnp.exp(-math.log(10000.0) * jnp.arange(half_width, dtype=F32) / half_width)
    angles = timesteps.astype(F32)[:, None] * freqs[None, :]
    return jnp.concatenate([jnp.sin(angles), jnp.cos(angles)], axis=-1)


def body(
    clean_latent, noise_latent, codec_tokens, codec_mask, frames, timesteps, out_cotangent,
    master_blocks, norm_params, owned_block, left_stats, right_stats, left_root, right_root,
):
    n_data = lax.axis_size("dp")
    n_model = lax.axis_size("mp")
    total_devices = n_data * n_model
    clip_count = clean_latent.shape[0]
    ctx_len = codec_tokens.shape[1]
    slot_count, row_share = (master_blocks.shape[0], master_blocks.shape[1])
    master_low = master_blocks.astype(BF16)[None]
    params_low = norm_params.astype(BF16)[None]
    gathered = lax.all_gather(master_low, ("dp", "mp"), axis=0, tiled=True)
    gathered_params = lax.all_gather(params_low, ("dp", "mp"), axis=0, tiled=True)
    params = gathered_params.transpose(1, 0, 2).reshape(gathered_params.shape[1], -1).astype(F32)
    params = jnp.pad(params, ((0, 2), (0, 0)))
    blocks = (
        gathered.reshape(n_data, n_model, slot_count, row_share, BS)
        .transpose(1, 2, 0, 3, 4)
        .reshape(n_model * slot_count, BS, BS)
    )

    phases = timesteps.astype(F32) * (0.5 * math.pi / TSTEPS)
    trig = jnp.stack([jnp.cos(phases), jnp.sin(phases)])
    embedding = jax.nn.silu(sinusoid(timesteps)).astype(BF16)
    emb_rows = jnp.broadcast_to(embedding[:, None, :], (clip_count, 16, CH))
    kmask = jnp.broadcast_to(codec_mask.astype(F32)[:, None, :], (clip_count, 8, ctx_len))
    tok_t = codec_tokens.transpose(0, 2, 1)

    inp, outlow, stats1, obias = pre(frames, trig, clean_latent, noise_latent, out_cotangent)
    e1, o1 = acts_windows(frames, inp, stats1, params)
    at = e1[:, 1].reshape(-1, CH).T
    res, normed, stats2 = conv_forward(frames, e1, o1, inp, emb_rows, params, blocks)
    block_output, dq, dw_att = attention(
        frames, normed, codec_tokens, tok_t, kmask, outlow, res, params, blocks[QUERY0:]
    )
    rgrad, e2, o2, sums2 = norm2_backward(frames, dq, res, stats2, out_cotangent, params, blocks[QUERY0:OUT0])
    dtaps = tap_gradients(at, e2, o2)
    input_grad, sums1 = input_backward(frames, e2, o2, inp, stats1, rgrad, params, blocks)

    clip_sums = jnp.sum(sums2[:, 0:8], axis=1)
    temb_grad = clip_sums.astype(BF16)
    dtemb = jnp.einsum("nc,nd->cd", embedding, temb_grad, preferred_element_type=F32) * INV_WIDTH
    att_scales = jnp.concatenate(
        [jnp.full((CH, 1), INV_WIDTH), jnp.full((CH, 1), OUT_SCALE), jnp.full((2 * CTX, 1), INV_CTX)]
    ).astype(F32)
    dw_att = (dw_att * att_scales).astype(BF16)
    local_blocks = jnp.concatenate(
        [
            dtaps.reshape(TEMB0, BS, BS),
            to_blocks(dtemb.astype(BF16)),
            to_blocks(dw_att),
        ],
        axis=0,
    )
    param_grads = jnp.stack(
        [
            jnp.sum(sums1[:, 0:8], axis=(0, 1)),
            jnp.sum(sums1[:, 8:16], axis=(0, 1)),
            jnp.sum(clip_sums, axis=0),
            jnp.sum(sums2[:, 8:16], axis=(0, 1)),
            jnp.sum(sums2[:, 16:24], axis=(0, 1)),
            jnp.sum(obias, axis=(0, 1)),
        ]
    )
    permuted = jnp.take(local_blocks, owned_block, axis=0)
    arranged = (
        permuted.reshape(n_model, slot_count, n_data, row_share, BS)
        .transpose(2, 0, 1, 3, 4)
        .reshape(-1, row_share, BS)
    )
    param_rows = param_grads.shape[0]
    param_arranged = (
        param_grads.reshape(param_rows, total_devices, -1)
        .transpose(1, 0, 2)
        .reshape(total_devices * param_rows, -1)
    )
    owned_low = lax.psum_scatter(arranged, ("dp", "mp"), scatter_dimension=0, tiled=True)
    norm_grads = lax.psum_scatter(param_arranged, ("dp", "mp"), scatter_dimension=0, tiled=True)
    owned_rows = owned_low.astype(F32)
    full_grad = lax.all_gather(owned_low, "dp", axis=1, tiled=True).astype(F32)
    row_start = lax.axis_index("dp") * row_share
    my_columns = lax.dynamic_slice_in_dim(full_grad, row_start, row_share, 2)
    new_left = 0.5 * left_stats + 0.5 * jnp.einsum("srk,stk->srt", owned_rows, full_grad)
    new_right = 0.5 * right_stats + 0.5 * jnp.einsum("skr,skt->srt", my_columns, full_grad)
    left_side = jnp.einsum("srk,skt->srt", left_root, full_grad)
    update = jnp.einsum("srk,skt->srt", left_side, right_root)
    update_step = (
        learn_rate * update * lax.rsqrt(jnp.mean(update * update, axis=(1, 2), keepdims=True) + 1e-06)
    )
    step_rows = lax.dynamic_slice_in_dim(update_step, row_start, row_share, 1)
    all_steps = lax.all_gather(step_rows, "mp", axis=0, tiled=True)
    natural = jnp.zeros_like(all_steps).at[owned_block].set(all_steps)
    my_steps = lax.dynamic_slice_in_dim(natural, lax.axis_index("mp") * slot_count, slot_count, 0)
    new_master = master_blocks - my_steps
    small_rate = 0.5 / math.sqrt(clip_count * total_devices * POS)
    new_norm = norm_params - small_rate * norm_grads
    return (
        block_output, input_grad, owned_rows, new_left, new_right, new_master,
        new_master.astype(BF16), norm_grads, new_norm,
    )


def solution(mesh):
    cells = P(("dp", "mp"), None, None)
    rows = P("mp", "dp", None)
    in_specs = (
        cells, cells, cells, P(("dp", "mp"), None), P(("dp", "mp")), P(("dp", "mp")), cells,
        rows, P(None, ("dp", "mp")), P(), rows, rows, P("mp", None, None), P("mp", None, None),
    )
    out_specs = (
        cells, cells, rows, rows, rows, rows, rows, P(None, ("dp", "mp")), P(None, ("dp", "mp")),
    )
    return jax.shard_map(body, mesh=mesh, in_specs=in_specs, out_specs=out_specs, check_vma=False)
```

```python
import functools
import math

import jax
import jax.numpy as jnp
from jax import lax
from jax.experimental import pallas as pl
from jax.experimental.pallas import tpu as pltpu
from jax.sharding import PartitionSpec as P

LATENT_CHANNELS = 512
GROUPS = 32
HEADS = 8
HEADDIM = 64
CTX = 768
BINS = 8
TSTEPS = 1000
BS = 128
POS = 1024
CH = LATENT_CHANNELS

highest = lax.Precision.HIGHEST
learn_rate = 0.5
out_gain = 8.0
eps = 1e-05

CONV_SCALE = 1.0 / math.sqrt(9 * CH)
INV_WIDTH = 1.0 / math.sqrt(CH)
INV_CTX = 1.0 / math.sqrt(CTX)
OUT_SCALE = out_gain / math.sqrt(CH)
ATT_SCALE = 1.0 / math.sqrt(HEADDIM)

SQ = (CH // BS) * (CH // BS)
KV = (CTX // BS) * (CH // BS)
TEMB0 = 9 * SQ
QUERY0 = TEMB0 + SQ
OUT0 = QUERY0 + SQ
KEY0 = OUT0 + SQ
VALUE0 = KEY0 + KV
NBLK = VALUE0 + KV

F32 = jnp.float32
BF16 = jnp.bfloat16
VMEM_LIMIT = 60 * 1024 * 1024


def nt(a, b):
    return lax.dot_general(a, b, (((1,), (1,)), ((), ())), preferred_element_type=F32)


def nn(a, b):
    return lax.dot_general(a, b, (((1,), (0,)), ((), ())), preferred_element_type=F32)


def mat(ref, base, nr, nc):
    rows = [jnp.concatenate([ref[base + a * nc + b] for b in range(nc)], axis=1) for a in range(nr)]
    return jnp.concatenate(rows, axis=0)


def row_iota(start, count):
    return lax.broadcasted_iota(jnp.int32, (count, 1), 0) + start


def fold8(x):
    return jnp.sum(x.reshape(-1, 8, x.shape[-1]), axis=0)


def group_sums(rows8, gmat):
    total = jnp.broadcast_to(jnp.sum(rows8, axis=0, keepdims=True), (8, CH))
    return lax.dot_general(
        total, gmat, (((1,), (0,)), ((), ())), preferred_element_type=F32, precision=highest
    )[0:1]


def group_matrix():
    i = lax.broadcasted_iota(jnp.int32, (CH, CH), 0) // (CH // GROUPS)
    j = lax.broadcasted_iota(jnp.int32, (CH, CH), 1) // (CH // GROUPS)
    return (i == j).astype(F32)


def shift_bins(tile, step):
    if step == 0:
        return tile
    t = tile.reshape(-1, 8, tile.shape[-1])
    rolled = pltpu.roll(t, (8 - step) % 8, 1)
    b = lax.broadcasted_iota(jnp.int32, (1, 8, 1), 1) + step
    keep = (b >= 0) & (b < 8)
    return jnp.where(keep, rolled, 0.0).reshape(tile.shape)


def write_windows(pad, e_ref, o_ref, sign):
    T = 64

    def body(i, carry):
        r = pl.multiple_of(i * T, T)
        mid = pad[pl.ds(r + 8, T), :]
        low = pad[pl.ds(r, T), :]
        for d in range(3):
            step = sign * (d - 1)
            e_ref[0, d, pl.ds(r, T), :] = shift_bins(mid, step).astype(BF16)
            o_ref[0, d, pl.ds(r, T), :] = shift_bins(low, step).astype(BF16)
        return carry

    lax.fori_loop(0, POS // T, body, 0)
    last = pad[POS : POS + 16, :]
    for d in range(3):
        o_ref[0, d, POS : POS + 16, :] = shift_bins(last, sign * (d - 1)).astype(BF16)


def window(e_ref, o_ref, df, db, r, n, lead=(0,)):
    if df == 1:
        return e_ref[lead + (db, pl.ds(r, n), slice(None))]
    off = 0 if df == 0 else 16
    return o_ref[lead + (db, pl.ds(pl.multiple_of(r + off, 16), n), slice(None))]


def pre_kernel(frames_s, trig_s, clean, noise, cot, inp, outlow, stats, obias):
    c = pl.program_id(0)
    rows = frames_s[c] * BINS
    cs, sn = trig_s[0, c], trig_s[1, c]
    T = 64
    zero = jnp.zeros((8, CH), F32)
    gmat = group_matrix()
    inv_n = 1.0 / (rows * (CH // GROUPS)).astype(F32)

    def first(i, carry):
        s0, s1 = carry
        r = pl.multiple_of(i * T, T)
        m = row_iota(r, T) < rows
        x = jnp.where(m, cs * clean[0, pl.ds(r, T), :] + sn * noise[0, pl.ds(r, T), :], 0.0)
        inp[0, pl.ds(r, T), :] = x
        g = jnp.where(m, cot[0, pl.ds(r, T), :], 0.0)
        outlow[0, pl.ds(r, T), :] = g.astype(BF16)
        return (s0 + fold8(x), s1 + fold8(g))

    s0, s1 = lax.fori_loop(0, POS // T, first, (zero, zero))
    mean = group_sums(s0, gmat) * inv_n

    def second(i, s):
        r = pl.multiple_of(i * T, T)
        m = row_iota(r, T) < rows
        d = jnp.where(m, inp[0, pl.ds(r, T), :] - mean, 0.0)
        return s + fold8(d * d)

    s2 = lax.fori_loop(0, POS // T, second, zero)
    rstd = lax.rsqrt(group_sums(s2, gmat) * inv_n + eps)
    stats[0] = jnp.concatenate([mean, rstd, jnp.zeros((6, CH), F32)], axis=0)
    obias[0] = s1


def pre(frames, trig, clean, noise, cot):
    n = clean.shape[0]
    big = pl.BlockSpec((1, POS, CH), lambda c, *_: (c, 0, 0))
    small = pl.BlockSpec((1, 8, CH), lambda c, *_: (c, 0, 0))
    return pl.pallas_call(
        pre_kernel,
        out_shape=(
            jax.ShapeDtypeStruct((n, POS, CH), F32),
            jax.ShapeDtypeStruct((n, POS, CH), BF16),
            jax.ShapeDtypeStruct((n, 8, CH), F32),
            jax.ShapeDtypeStruct((n, 8, CH), F32),
        ),
        grid_spec=pltpu.PrefetchScalarGridSpec(
            num_scalar_prefetch=2, grid=(n,), in_specs=[big, big, big], out_specs=[big, big, small, small]
        ),
        compiler_params=pltpu.CompilerParams(vmem_limit_bytes=VMEM_LIMIT),
        cost_estimate=pl.CostEstimate(flops=n * POS * CH * 20, bytes_accessed=n * POS * CH * 18, transcendentals=0),
        name="inputs_stats",
    )(frames, trig, clean, noise, cot)


def acts_kernel(frames_s, inp, stats, *refs):
    pieces, (e_ref, o_ref, params_ref, pad) = refs[:-4], refs[-4:]
    c = pl.program_id(0)
    rows = frames_s[c] * BINS
    T = 64
    total = None
    for piece in pieces:
        for j in range(piece.shape[0]):
            got = piece[j].astype(F32).reshape(CH // BS, 8, BS)
            total = got if total is None else total + got
    params = jnp.concatenate([total[j] for j in range(CH // BS)], axis=1)
    params_ref[...] = params
    mean, rstd = stats[0, 0:1], stats[0, 1:2]
    scale = rstd * params[0:1]
    shift = params[1:2]
    pad[0:8, :] = jnp.zeros((8, CH), F32)
    pad[8 + POS :, :] = jnp.zeros((8, CH), F32)

    def body(i, carry):
        r = pl.multiple_of(i * T, T)
        m = row_iota(r, T) < rows
        y = (inp[0, pl.ds(r, T), :] - mean) * scale + shift
        a = jnp.where(m, y * jax.nn.sigmoid(y), 0.0)
        pad[pl.ds(r + 8, T), :] = a
        return carry

    lax.fori_loop(0, POS // T, body, 0)
    write_windows(pad, e_ref, o_ref, 1)


def acts_windows(frames, inp, stats, pieces):
    n = inp.shape[0]
    row_share = pieces[0].shape[2]
    slots = CH // BS * 8 // row_share
    return pl.pallas_call(
        acts_kernel,
        out_shape=(
            jax.ShapeDtypeStruct((n, 3, POS, CH), BF16),
            jax.ShapeDtypeStruct((n, 3, POS + 16, CH), BF16),
            jax.ShapeDtypeStruct((8, CH), F32),
        ),
        grid_spec=pltpu.PrefetchScalarGridSpec(
            num_scalar_prefetch=1,
            grid=(n,),
            in_specs=[
                pl.BlockSpec((1, POS, CH), lambda c, *_: (c, 0, 0)),
                pl.BlockSpec((1, 8, CH), lambda c, *_: (c, 0, 0)),
            ]
            + [
                pl.BlockSpec((p.shape[0], slots, row_share, BS), lambda c, *_: (0, 0, 0, 0))
                for p in pieces
            ],
            out_specs=[
                pl.BlockSpec((1, 3, POS, CH), lambda c, *_: (c, 0, 0, 0)),
                pl.BlockSpec((1, 3, POS + 16, CH), lambda c, *_: (c, 0, 0, 0)),
                pl.BlockSpec((8, CH), lambda c, *_: (0, 0)),
            ],
            scratch_shapes=[pltpu.VMEM((POS + 16, CH), F32)],
        ),
        compiler_params=pltpu.CompilerParams(vmem_limit_bytes=VMEM_LIMIT),
        cost_estimate=pl.CostEstimate(
            flops=n * POS * CH * 30, bytes_accessed=n * POS * CH * 16, transcendentals=n * POS * CH
        ),
        name="acts",
    )(frames, inp, stats, *pieces)


def conv_kernel(chunks, frames_s, dest_s, e_ref, o_ref, inp, emb, params, *refs):
    pieces, (res, normed, stats, w_out, w, sem, sem_out) = refs[: -7], refs[-7:]
    c = pl.program_id(0)
    per_chunk = len(pieces) // len(chunks)
    row_share = pieces[0].shape[2]

    @pl.when(c == 0)
    def _():
        copies = []
        for j, (skip, start, count) in enumerate(chunks):
            for a in range(per_chunk):
                ref = pieces[j * per_chunk + a]
                for p in range(ref.shape[0]):
                    i = a * ref.shape[0] + p
                    first = dest_s[0, i] + start
                    row = pl.multiple_of(dest_s[1, i], row_share)
                    copies.append(
                        pltpu.make_async_copy(
                            ref.at[p, pl.ds(skip, count)],
                            w.at[pl.ds(first, count), pl.ds(row, row_share), :],
                            sem.at[len(copies)],
                        )
                    )
        for copy in copies:
            copy.start()
        for copy in copies:
            copy.wait()
        pltpu.make_async_copy(w, w_out, sem_out).start()

    rows = frames_s[c] * BINS
    R = 256
    T = 64
    zero = jnp.zeros((8, CH), F32)
    gmat = group_matrix()
    inv_n = 1.0 / (rows * (CH // GROUPS)).astype(F32)
    temb = nn(emb[0], mat(w, TEMB0, 4, 4))[0:1] * INV_WIDTH
    add = temb + params[2:3]

    def tile(i, s):
        r = pl.multiple_of(i * R, R)
        acc = jnp.zeros((R, CH), F32)
        for t in range(9):
            df, db = divmod(t, 3)
            acc = acc + nn(window(e_ref, o_ref, df, db, r, R), mat(w, t * SQ, 4, 4))
        v = inp[0, pl.ds(r, R), :] + acc * CONV_SCALE + add
        res[0, pl.ds(r, R), :] = v
        return s + fold8(jnp.where(row_iota(r, R) < rows, v, 0.0))

    s = lax.fori_loop(0, POS // R, tile, zero)
    mean = group_sums(s, gmat) * inv_n

    def second(i, s):
        r = pl.multiple_of(i * T, T)
        d = jnp.where(row_iota(r, T) < rows, res[0, pl.ds(r, T), :] - mean, 0.0)
        return s + fold8(d * d)

    s2 = lax.fori_loop(0, POS // T, second, zero)
    rstd = lax.rsqrt(group_sums(s2, gmat) * inv_n + eps)
    scale = rstd * params[3:4]
    shift = params[4:5]

    def third(i, carry):
        r = pl.multiple_of(i * T, T)
        normed[0, pl.ds(r, T), :] = ((res[0, pl.ds(r, T), :] - mean) * scale + shift).astype(BF16)
        return carry

    lax.fori_loop(0, POS // T, third, 0)
    stats[0] = jnp.concatenate([mean, rstd, jnp.zeros((6, CH), F32)], axis=0)

    @pl.when(c == pl.num_programs(0) - 1)
    def _():
        pltpu.make_async_copy(w, w_out, sem_out).wait()


def whole(shape):
    return pl.BlockSpec(shape, lambda *_: (0,) * len(shape), pipeline_mode=pl.Buffered(1))


def per_clip(shape):
    return pl.BlockSpec((1,) + shape, lambda c, *_: (c,) + (0,) * len(shape))


def conv_forward(frames, dest, e, o, inp, emb, params, pieces, chunks):
    n = inp.shape[0]
    copies = sum(p.shape[0] for p in pieces)
    return pl.pallas_call(
        functools.partial(conv_kernel, chunks),
        out_shape=(
            jax.ShapeDtypeStruct((n, POS, CH), F32),
            jax.ShapeDtypeStruct((n, POS, CH), BF16),
            jax.ShapeDtypeStruct((n, 8, CH), F32),
            jax.ShapeDtypeStruct((NBLK, BS, BS), BF16),
        ),
        grid_spec=pltpu.PrefetchScalarGridSpec(
            num_scalar_prefetch=2,
            grid=(n,),
            in_specs=[
                per_clip((3, POS, CH)),
                per_clip((3, POS + 16, CH)),
                per_clip((POS, CH)),
                per_clip((16, CH)),
                whole((8, CH)),
            ]
            + [pl.BlockSpec(memory_space=pl.ANY)] * len(pieces),
            out_specs=[
                per_clip((POS, CH)),
                per_clip((POS, CH)),
                per_clip((8, CH)),
                pl.BlockSpec(memory_space=pl.ANY),
            ],
            scratch_shapes=[
                pltpu.VMEM((NBLK, BS, BS), BF16),
                pltpu.SemaphoreType.DMA((copies,)),
                pltpu.SemaphoreType.DMA(()),
            ],
        ),
        compiler_params=pltpu.CompilerParams(vmem_limit_bytes=VMEM_LIMIT),
        cost_estimate=pl.CostEstimate(
            flops=n * POS * CH * CH * 18, bytes_accessed=n * POS * CH * 22 + 5000000, transcendentals=0
        ),
        name="conv_forward",
    )(frames, dest, e, o, inp, emb, params, *pieces)


def attn_kernel(
    frames_s, normed, tokens, tok_t, kmask, outlow, res, params, w,
    block_out, dq_ref, dw_ref,
    q_s, do_s, kv_s, qt_s, dot_s, mixed_s, dkt_s, dvt_s, dkv_acc,
):
    c = pl.program_id(0)
    rows = frames_s[c] * BINS
    R = 256
    query_w = mat(w, SQ, 4, 4)
    out_w = mat(w, 2 * SQ, 4, 4)
    key_w = mat(w, 3 * SQ, CTX // BS, 4)
    value_w = mat(w, 3 * SQ + KV, CTX // BS, 4)

    def project(i, carry):
        r = pl.multiple_of(i * R, R)
        q = (nn(normed[0, pl.ds(r, R), :], query_w) * INV_WIDTH).astype(BF16)
        q_s[pl.ds(r, R), :] = q
        qt_s[:, pl.ds(r, R)] = q.T
        d = (nt(outlow[0, pl.ds(r, R), :], out_w) * OUT_SCALE).astype(BF16)
        do_s[pl.ds(r, R), :] = d
        dot_s[:, pl.ds(r, R)] = d.T
        return carry

    lax.fori_loop(0, POS // R, project, 0)
    kv_s[0] = ((nn(tokens[0], key_w) * INV_CTX).astype(BF16).astype(F32) * ATT_SCALE).astype(BF16)
    kv_s[1] = (nn(tokens[0], value_w) * INV_CTX).astype(BF16)
    valid = kmask[0, 0:1, :] > 0.0
    lane = lax.broadcasted_iota(jnp.int32, (1, BS), 1)
    first = lane < HEADDIM

    for slab in range(HEADS // 2):
        cols = slice(slab * BS, (slab + 1) * BS)
        k2, v2 = kv_s[0, :, cols], kv_s[1, :, cols]
        none = jnp.zeros_like(k2)
        ks = (jnp.where(first, k2, none), jnp.where(first, none, k2))
        vs = (jnp.where(first, v2, none), jnp.where(first, none, v2))
        dkv_acc[...] = jnp.zeros_like(dkv_acc)

        def tile(i, carry):
            r = pl.multiple_of(i * R, R)
            q = q_s[pl.ds(r, R), cols]
            d = do_s[pl.ds(r, R), cols]
            o = jnp.zeros((R, BS), F32)
            dq = jnp.zeros((R, BS), F32)
            for h in range(2):
                s = jnp.where(valid, nt(q, ks[h]), -1000000000.0)
                e = jnp.exp(s - jnp.max(s, axis=-1, keepdims=True))
                p = e * (1.0 / jnp.sum(e, axis=-1, keepdims=True))
                pb = p.astype(BF16)
                dp = nt(d, vs[h])
                delta = jnp.sum(p * dp, axis=-1, keepdims=True)
                ds = (p * (dp - delta)).astype(BF16)
                o = o + nn(pb, vs[h])
                dq = dq + nn(ds, ks[h])
                half = slice(slab * BS + h * HEADDIM, slab * BS + (h + 1) * HEADDIM)
                mine = slice(h * HEADDIM, (h + 1) * HEADDIM)
                dkv_acc[0, mine, :] += nn(qt_s[half, pl.ds(r, R)], ds)
                dkv_acc[1, mine, :] += nn(dot_s[half, pl.ds(r, R)], pb)
            mixed_s[pl.ds(r, R), cols] = o.astype(BF16)
            dq_ref[0, pl.ds(r, R), cols] = dq.astype(BF16)
            return carry

        lax.fori_loop(0, POS // R, tile, 0)
        dkt_s[cols, :] = (dkv_acc[0] * ATT_SCALE).astype(BF16)
        dvt_s[cols, :] = dkv_acc[1].astype(BF16)

    def project_out(i, carry):
        r = pl.multiple_of(i * R, R)
        proj = nn(mixed_s[pl.ds(r, R), :], out_w) * OUT_SCALE + params[5:6]
        m = row_iota(r, R) < rows
        block_out[0, pl.ds(r, R), :] = jnp.where(m, res[0, pl.ds(r, R), :] + proj, 0.0)
        return carry

    lax.fori_loop(0, POS // R, project_out, 0)

    @pl.when(c == 0)
    def _():
        dw_ref[...] = jnp.zeros_like(dw_ref)

    dw_ref[0:CH, :] += nn(normed[0].T, dq_ref[0])
    dw_ref[CH : 2 * CH, :] += nn(mixed_s[...].T, outlow[0])
    dw_ref[2 * CH : 2 * CH + CTX, :] += nt(tok_t[0], dkt_s[...])
    dw_ref[2 * CH + CTX :, :] += nt(tok_t[0], dvt_s[...])


def attention(frames, normed, tokens, tok_t, kmask, outlow, res, params, w):
    n = normed.shape[0]
    ctx_len = tokens.shape[1]
    amount = SQ + SQ + SQ + KV + KV
    return pl.pallas_call(
        attn_kernel,
        out_shape=(
            jax.ShapeDtypeStruct((n, POS, CH), F32),
            jax.ShapeDtypeStruct((n, POS, CH), BF16),
            jax.ShapeDtypeStruct((2 * CH + 2 * CTX, CH), F32),
        ),
        grid_spec=pltpu.PrefetchScalarGridSpec(
            num_scalar_prefetch=1,
            grid=(n,),
            in_specs=[
                per_clip((POS, CH)),
                per_clip((ctx_len, CTX)),
                per_clip((CTX, ctx_len)),
                per_clip((8, ctx_len)),
                per_clip((POS, CH)),
                per_clip((POS, CH)),
                whole((8, CH)),
                pl.BlockSpec(
                    (pl.Element(amount), pl.Element(BS), pl.Element(BS)),
                    lambda *_: (TEMB0, 0, 0),
                    pipeline_mode=pl.Buffered(1),
                ),
            ],
            out_specs=[
                per_clip((POS, CH)),
                per_clip((POS, CH)),
                pl.BlockSpec((2 * CH + 2 * CTX, CH), lambda *_: (0, 0)),
            ],
            scratch_shapes=[
                pltpu.VMEM((POS, CH), BF16),
                pltpu.VMEM((POS, CH), BF16),
                pltpu.VMEM((2, ctx_len, CH), BF16),
                pltpu.VMEM((CH, POS), BF16),
                pltpu.VMEM((CH, POS), BF16),
                pltpu.VMEM((POS, CH), BF16),
                pltpu.VMEM((CH, ctx_len), BF16),
                pltpu.VMEM((CH, ctx_len), BF16),
                pltpu.VMEM((2, BS, ctx_len), F32),
            ],
        ),
        compiler_params=pltpu.CompilerParams(vmem_limit_bytes=VMEM_LIMIT),
        cost_estimate=pl.CostEstimate(
            flops=n * POS * CH * (6 * CH * 2 + 24 * ctx_len),
            bytes_accessed=n * POS * CH * 16,
            transcendentals=n * POS * HEADS * ctx_len,
        ),
        name="attention",
    )(frames, normed, tokens, tok_t, kmask, outlow, res, params, w)


def norm2_kernel(frames_s, dq_ref, res, stats, cot, params, w, rgrad, e_ref, o_ref, sums, ng_s, pad):
    c = pl.program_id(0)
    rows = frames_s[c] * BINS
    R = 256
    T = 64
    zero = jnp.zeros((8, CH), F32)
    gmat = group_matrix()
    inv_n = 1.0 / (rows * (CH // GROUPS)).astype(F32)
    mean, rstd = stats[0, 0:1], stats[0, 1:2]
    gain = params[3:4]
    query_w = mat(w, 0, 4, 4)

    def first(i, carry):
        s0, s1 = carry
        r = pl.multiple_of(i * R, R)
        ng = nt(dq_ref[0, pl.ds(r, R), :], query_w) * INV_WIDTH
        m = row_iota(r, R) < rows
        ng = jnp.where(m, ng, 0.0)
        ng_s[pl.ds(r, R), :] = ng
        x = jnp.where(m, (res[0, pl.ds(r, R), :] - mean) * rstd, 0.0)
        return (s0 + fold8(ng), s1 + fold8(ng * x))

    s0, s1 = lax.fori_loop(0, POS // R, first, (zero, zero))
    mh = group_sums(s0 * gain, gmat) * inv_n
    mhx = group_sums(s1 * gain, gmat) * inv_n
    pad[0:8, :] = zero
    pad[8 + POS :, :] = zero

    def second(i, s):
        r = pl.multiple_of(i * T, T)
        m = row_iota(r, T) < rows
        x = (res[0, pl.ds(r, T), :] - mean) * rstd
        d = rstd * (gain * ng_s[pl.ds(r, T), :] - mh - x * mhx)
        g = jnp.where(m, cot[0, pl.ds(r, T), :] + d, 0.0)
        rgrad[0, pl.ds(r, T), :] = g
        pad[pl.ds(r + 8, T), :] = g
        return s + fold8(g)

    s2 = lax.fori_loop(0, POS // T, second, zero)
    sums[0, 0:8] = s2
    sums[0, 8:16] = s1
    sums[0, 16:24] = s0
    write_windows(pad, e_ref, o_ref, -1)


def norm2_backward(frames, dq, res, stats, cot, params, w):
    n = dq.shape[0]
    return pl.pallas_call(
        norm2_kernel,
        out_shape=(
            jax.ShapeDtypeStruct((n, POS, CH), F32),
            jax.ShapeDtypeStruct((n, 3, POS, CH), BF16),
            jax.ShapeDtypeStruct((n, 3, POS + 16, CH), BF16),
            jax.ShapeDtypeStruct((n, 24, CH), F32),
        ),
        grid_spec=pltpu.PrefetchScalarGridSpec(
            num_scalar_prefetch=1,
            grid=(n,),
            in_specs=[
                per_clip((POS, CH)),
                per_clip((POS, CH)),
                per_clip((8, CH)),
                per_clip((POS, CH)),
                whole((8, CH)),
                pl.BlockSpec((SQ, BS, BS), lambda *_: (QUERY0 // SQ, 0, 0), pipeline_mode=pl.Buffered(1)),
            ],
            out_specs=[
                per_clip((POS, CH)),
                per_clip((3, POS, CH)),
                per_clip((3, POS + 16, CH)),
                per_clip((24, CH)),
            ],
            scratch_shapes=[pltpu.VMEM((POS, CH), F32), pltpu.VMEM((POS + 16, CH), F32)],
        ),
        compiler_params=pltpu.CompilerParams(vmem_limit_bytes=VMEM_LIMIT),
        cost_estimate=pl.CostEstimate(
            flops=n * POS * CH * CH * 2, bytes_accessed=n * POS * CH * 26, transcendentals=0
        ),
        name="norm2_backward",
    )(frames, dq, res, stats, cot, params, w)


def tap_kernel(parts, table_s, at, emb, sums, dw_att, e_ref, o_ref, *refs):
    outs, (blocks, sem) = refs[: 2 * parts], refs[2 * parts :]
    n = e_ref.shape[0]
    d = pl.program_id(0)
    entries = table_s.shape[1]

    def cut(value, first, stride):
        low = value.astype(BF16)
        for a in range(value.shape[0] // BS):
            for b in range(4):
                blocks[first + a * 4 + b] = low[a * BS : (a + 1) * BS, b * BS : (b + 1) * BS]

    def send(lo, hi):
        def one(i, carry):
            for q in range(2 * parts):
                @pl.when(table_s[0, i] == q)
                def _():
                    src = blocks.at[jnp.minimum(i, NBLK)]
                    pltpu.make_async_copy(src, outs[q].at[table_s[1, i]], sem).start()

            return carry

        lax.fori_loop(lo, hi, one, 0)

    for df in range(3):
        acc = None
        for c in range(n):
            g = window(e_ref, o_ref, 2 - df, 0, 0, POS, (c,))
            part = nn(at[:, c * POS : (c + 1) * POS], g)
            acc = part if acc is None else acc + part
        cut(acc * CONV_SCALE, (3 * df + d) * SQ, 4)
        send((3 * df + d) * SQ, (3 * df + d + 1) * SQ)

    @pl.when(d == 0)
    def _():
        rows = [jnp.sum(sums[c, 0:8], axis=0, keepdims=True) for c in range(n)]
        grad = jnp.concatenate(rows + [jnp.zeros((16 - n, CH), F32)], axis=0).astype(BF16)
        outer = lax.dot_general(emb[...], grad, (((0,), (0,)), ((), ())), preferred_element_type=F32)
        cut(outer * INV_WIDTH, TEMB0, 4)
        blocks[NBLK] = jnp.zeros((BS, BS), BF16)
        cut(dw_att[0:CH] * INV_WIDTH, QUERY0, 4)
        cut(dw_att[CH : 2 * CH] * OUT_SCALE, OUT0, 4)
        cut(dw_att[2 * CH :] * INV_CTX, KEY0, 4)
        send(TEMB0, entries)

    @pl.when(d == pl.num_programs(0) - 1)
    def _():
        for out in outs:
            pltpu.make_async_copy(out, out, sem).wait()


def tap_gradients(table, at, emb, sums, dw_att, e, o, sizes):
    n = e.shape[0]
    parts = len(sizes) // 2
    return pl.pallas_call(
        functools.partial(tap_kernel, parts),
        out_shape=tuple(jax.ShapeDtypeStruct((s, BS, BS), BF16) for s in sizes),
        grid_spec=pltpu.PrefetchScalarGridSpec(
            num_scalar_prefetch=1,
            grid=(3,),
            in_specs=[
                whole((CH, n * POS)),
                whole((16, CH)),
                whole(sums.shape),
                whole(dw_att.shape),
                pl.BlockSpec((n, 1, POS, CH), lambda d, *_: (0, d, 0, 0)),
                pl.BlockSpec((n, 1, POS + 16, CH), lambda d, *_: (0, d, 0, 0)),
            ],
            out_specs=[pl.BlockSpec(memory_space=pl.ANY)] * len(sizes),
            scratch_shapes=[pltpu.VMEM((NBLK + 1, BS, BS), BF16), pltpu.SemaphoreType.DMA(())],
        ),
        compiler_params=pltpu.CompilerParams(vmem_limit_bytes=VMEM_LIMIT),
        cost_estimate=pl.CostEstimate(
            flops=n * POS * CH * CH * 18, bytes_accessed=n * POS * CH * 14 + 20000000, transcendentals=0
        ),
        name="tap_gradients",
    )(table, at, emb, sums, dw_att, e, o)


def input_kernel(clip, frames_s, e_ref, o_ref, inp, stats, rgrad, params, w, *refs):
    out, sums, ag_s = refs[-3:]
    c = clip
    rows = frames_s[c] * BINS
    R = 256
    T = 64
    zero = jnp.zeros((8, CH), F32)
    gmat = group_matrix()
    inv_n = 1.0 / (rows * (CH // GROUPS)).astype(F32)
    mean, rstd = stats[0, 0:1], stats[0, 1:2]
    gain, shift = params[0:1], params[1:2]

    def conv(i, carry):
        r = pl.multiple_of(i * R, R)
        acc = jnp.zeros((R, CH), F32)
        for t in range(9):
            df, db = divmod(t, 3)
            acc = acc + nt(window(e_ref, o_ref, 2 - df, db, r, R), mat(w, t * SQ, 4, 4))
        ag_s[pl.ds(r, R), :] = acc * CONV_SCALE
        return carry

    lax.fori_loop(0, POS // R, conv, 0)

    def first(i, carry):
        s0, s1 = carry
        r = pl.multiple_of(i * T, T)
        m = row_iota(r, T) < rows
        x = (inp[0, pl.ds(r, T), :] - mean) * rstd
        y = x * gain + shift
        sg = jax.nn.sigmoid(y)
        dy = jnp.where(m, ag_s[pl.ds(r, T), :] * (sg * (1.0 + y * (1.0 - sg))), 0.0)
        ag_s[pl.ds(r, T), :] = dy
        return (s0 + fold8(dy), s1 + fold8(dy * x))

    s0, s1 = lax.fori_loop(0, POS // T, first, (zero, zero))
    mh = group_sums(s0 * gain, gmat) * inv_n
    mhx = group_sums(s1 * gain, gmat) * inv_n

    def second(i, carry):
        r = pl.multiple_of(i * T, T)
        m = row_iota(r, T) < rows
        x = (inp[0, pl.ds(r, T), :] - mean) * rstd
        d = rstd * (gain * ag_s[pl.ds(r, T), :] - mh - x * mhx)
        out[0, pl.ds(r, T), :] = jnp.where(m, rgrad[0, pl.ds(r, T), :] + d, 0.0)
        return carry

    lax.fori_loop(0, POS // T, second, 0)
    sums[0, 0:8] = s1
    sums[0, 8:16] = s0


def input_backward(clip, frames, e, o, inp, stats, rgrad, params, w, before=None):
    n = inp.shape[0]

    def of_clip(shape):
        return pl.BlockSpec((1,) + shape, lambda i, *_: (clip,) + (0,) * len(shape))

    before = () if before is None else (before,)
    return pl.pallas_call(
        functools.partial(input_kernel, clip),
        out_shape=(
            jax.ShapeDtypeStruct((n, POS, CH), F32),
            jax.ShapeDtypeStruct((1, 16, CH), F32),
        ),
        grid_spec=pltpu.PrefetchScalarGridSpec(
            num_scalar_prefetch=1,
            grid=(1,),
            in_specs=[
                of_clip((3, POS, CH)),
                of_clip((3, POS + 16, CH)),
                of_clip((POS, CH)),
                of_clip((8, CH)),
                of_clip((POS, CH)),
                whole((8, CH)),
                pl.BlockSpec((TEMB0, BS, BS), lambda *_: (0, 0, 0), pipeline_mode=pl.Buffered(1)),
            ]
            + [pl.BlockSpec(memory_space=pl.ANY)] * len(before),
            out_specs=[of_clip((POS, CH)), pl.BlockSpec((1, 16, CH), lambda *_: (0, 0, 0))],
            scratch_shapes=[pltpu.VMEM((POS, CH), F32)],
        ),
        input_output_aliases={8: 0} if before else {},
        compiler_params=pltpu.CompilerParams(vmem_limit_bytes=VMEM_LIMIT),
        cost_estimate=pl.CostEstimate(
            flops=POS * CH * CH * 18, bytes_accessed=POS * CH * 24, transcendentals=POS * CH
        ),
        name="input_backward",
    )(frames, e, o, inp, stats, rgrad, params, w, *before)


def pad_kernel(n_data, table_s, obias, sums2, *refs):
    sums1, (_, _, keep, send, blocks, sem) = refs[:-6], refs[-6:]
    n_model = table_s.shape[1]
    row_share = BS // n_data
    width = CH // (n_data * n_model)
    total = lambda v: jnp.sum(v, axis=0, keepdims=True)
    first = sums1[0][0]
    for v in sums1[1:]:
        first = first + v[0]
    second, bias = sums2[0], obias[0]
    for i in range(1, sums2.shape[0]):
        second, bias = second + sums2[i], bias + obias[i]
    grads = jnp.concatenate(
        [
            total(first[0:8]), total(first[8:16]), total(second[0:8]), total(second[8:16]),
            total(second[16:24]), total(bias), jnp.zeros((2, CH), F32),
        ],
        axis=0,
    )
    lane = lax.broadcasted_iota(jnp.int32, (8, BS), 1)
    copies = []
    for m in range(n_model):
        tiles = []
        for d in range(n_data):
            at = (d * n_model + m) * width
            tile = grads[:, at // BS * BS : (at // BS + 1) * BS]
            tile = pltpu.roll(tile, (BS - at % BS) % BS, 1)
            tiles.append(jnp.where(lane < width, tile, 0.0))
            if row_share > 8:
                tiles.append(jnp.zeros((row_share - 8, BS), F32))
        blocks[m] = jnp.concatenate(tiles, axis=0).astype(BF16)
    for m in range(n_model):
        for q, out in enumerate((keep, send)):
            @pl.when(table_s[0, m] == q)
            def _():
                pltpu.make_async_copy(blocks.at[m], out.at[table_s[1, m]], sem).start()

    pltpu.make_async_copy(blocks, blocks, sem).wait()


def add_norm_grads(table, n_data, obias, sums2, sums1, keep, send):
    vm = pl.BlockSpec(memory_space=pltpu.VMEM)
    any_space = pl.BlockSpec(memory_space=pl.ANY)
    n = 3 + len(sums1)
    return pl.pallas_call(
        functools.partial(pad_kernel, n_data),
        out_shape=(
            jax.ShapeDtypeStruct(keep.shape, BF16),
            jax.ShapeDtypeStruct(send.shape, BF16),
        ),
        in_specs=[pl.BlockSpec(memory_space=pltpu.SMEM)] + [vm] * (n - 1) + [any_space] * 2,
        out_specs=[any_space] * 2,
        scratch_shapes=[pltpu.VMEM((table.shape[1], BS, BS), BF16), pltpu.SemaphoreType.DMA(())],
        input_output_aliases={n: 0, n + 1: 1},
        name="norm_grads",
    )(table, obias, sums2, *sums1, keep, send)


def sinusoid(timesteps):
    half_width = CH // 2
    freqs = jnp.exp(-math.log(10000.0) * jnp.arange(half_width, dtype=F32) / half_width)
    angles = timesteps.astype(F32)[:, None] * freqs[None, :]
    return jnp.concatenate([jnp.sin(angles), jnp.cos(angles)], axis=-1)


def step_kernel(dp_s, grad, left_root, right_root, step, stats):
    g = grad[0]
    low = g.astype(BF16)
    n_data, row_share = step.shape[0], step.shape[2]
    left = nt(low, low)
    right = lax.dot_general(low, low, (((0,), (0,)), ((), ())), preferred_element_type=F32)
    side = nn(left_root[0].astype(BF16), low)
    update = nn(side.astype(BF16), right_root[0].astype(BF16))
    rate = learn_rate * lax.rsqrt(jnp.sum(update * update, keepdims=True) * (1.0 / (BS * BS)) + 1e-06)
    step[:, 0] = (update * rate).reshape(n_data, row_share, BS).astype(BF16)
    stats[:, 0, 0] = g.reshape(n_data, row_share, BS).astype(BF16)
    stats[:, 0, 1] = left.reshape(n_data, row_share, BS).astype(BF16)
    stats[:, 0, 2] = right.reshape(n_data, row_share, BS).astype(BF16)


def owner_step(dp, grad, left_root, right_root, n_data, row_share):
    k = grad.shape[0]
    last = left_root.shape[0] - 1
    root = pl.BlockSpec((1, BS, BS), lambda i, dp: (jnp.minimum(dp[0] * k + i, last), 0, 0))
    return pl.pallas_call(
        step_kernel,
        out_shape=(
            jax.ShapeDtypeStruct((n_data, k, row_share, BS), BF16),
            jax.ShapeDtypeStruct((n_data, k, 3, row_share, BS), BF16),
        ),
        grid_spec=pltpu.PrefetchScalarGridSpec(
            num_scalar_prefetch=1,
            grid=(k,),
            in_specs=[pl.BlockSpec((1, BS, BS), lambda i, dp: (i, 0, 0)), root, root],
            out_specs=[
                pl.BlockSpec((n_data, 1, row_share, BS), lambda i, dp: (0, i, 0, 0)),
                pl.BlockSpec((n_data, 1, 3, row_share, BS), lambda i, dp: (0, i, 0, 0, 0)),
            ],
        ),
        cost_estimate=pl.CostEstimate(flops=k * 8 * BS**3, bytes_accessed=k * BS * BS * 20, transcendentals=0),
        name="owner_step",
    )(dp, grad, left_root, right_root)


def master_kernel(where_s, master, near, far, new, low, steps):
    half = near.shape[0]
    steps[0:half] = near[...].astype(F32)
    steps[half:] = far[...].astype(F32)

    def one(j, carry):
        value = master[j] - steps[where_s[j]]
        new[j] = value
        low[j] = value.astype(BF16)
        return carry

    lax.fori_loop(0, master.shape[0], one, 0)


def update_master(where, master, near, far):
    vm = pl.BlockSpec(memory_space=pltpu.VMEM)
    return pl.pallas_call(
        master_kernel,
        out_shape=(
            jax.ShapeDtypeStruct(master.shape, F32),
            jax.ShapeDtypeStruct(master.shape, BF16),
        ),
        in_specs=[pl.BlockSpec(memory_space=pltpu.SMEM), vm, vm, vm],
        out_specs=[vm, vm],
        scratch_shapes=[pltpu.VMEM((2 * near.shape[0],) + near.shape[1:], F32)],
        name="update_master",
    )(where, master, near, far)


class Grid:
    def __init__(self, n_data, n_model):
        self.nd, self.nm = n_data, n_model
        self.nx = n_model // 2
        self.ny = 1
        while self.ny * self.ny * 4 <= n_data:
            self.ny *= 2
        self.nz = n_data // self.ny
        self.split = self.nx == self.ny
        self.sizes = (self.ny, self.ny) if self.split else (self.ny, self.nx)
        dp, mp = lax.axis_index("dp"), lax.axis_index("mp")
        self.z, self.y, self.x, self.c = dp // self.ny, dp % self.ny, mp // 2, mp % 2

    def permute(self, value, fn):
        pairs = []
        for src in range(self.nd * self.nm):
            dp, mp = divmod(src, self.nm)
            z, y, x, c = fn(dp // self.ny, dp % self.ny, mp // 2, mp % 2)
            dst = ((z % self.nz) * self.ny + y % self.ny) * self.nm + (x % self.nx) * 2 + c % 2
            pairs.append((src, dst))
        return lax.ppermute(value, ("dp", "mp"), pairs)

    def along_z(self, value, d):
        return self.permute(value, lambda z, y, x, c: (z + d, y, x, c))

    def along_plane(self, value, stage, d):
        def fn(z, y, x, c):
            on_y = (stage == 0) != (self.split and c == 1)
            return (z, y + d, x, c) if on_y else (z, y, x + d, c)

        return self.permute(value, fn)

    def along_core(self, value):
        return self.permute(value, lambda z, y, x, c: (z, y, x, c + 1))

    def place(self, core, d0, d1, dz):
        swap = (core == 1) if self.split else jnp.zeros_like(core == 1)
        dy, dx = jnp.where(swap, d1, d0), jnp.where(swap, d0, d1)
        zz, yy, xx = (self.z + dz) % self.nz, (self.y + dy) % self.ny, (self.x + dx) % self.nx
        return zz * self.ny + yy, xx * 2 + core


def after(value, *others):
    return lax.optimization_barrier((value,) + others)[0]


def gather_z(grid, shard):
    return [shard] + [grid.along_z(shard, -d) for d in range(1, grid.nz)]


def gather_plane(grid, stack):
    got = [stack] + [grid.along_plane(stack, 0, -d) for d in range(1, grid.sizes[0])]
    stack = jnp.concatenate(got)
    got = [stack] + [grid.along_plane(stack, 1, -d) for d in range(1, grid.sizes[1])]
    return got + [grid.along_core(v) for v in got]


def gather_places(grid):
    dps, mps = [], []
    for rel in range(2):
        core = (grid.c + rel) % 2
        for d1 in range(grid.sizes[1]):
            for d0 in range(grid.sizes[0]):
                for dz in range(grid.nz):
                    dp, mp = grid.place(core, d0, d1, dz)
                    dps.append(dp)
                    mps.append(mp)
    return jnp.stack(dps), jnp.stack(mps)


def add_low(*parts):
    total = parts[0].astype(F32)
    for p in parts[1:]:
        total = total + p.astype(F32)
    return total


def scatter_core(grid, keep, send):
    return add_low(keep, grid.along_core(send)).astype(BF16)


def scatter_plane(grid, value, stage):
    size = grid.sizes[stage]
    value = value.reshape(size, -1, BS, BS)
    got = [grid.along_plane(value[d], stage, d) for d in range(1, size)]
    return add_low(value[0], *got).astype(BF16)


def scatter_z(grid, value):
    value = value.reshape(grid.nz, -1, BS, BS)
    got = [grid.along_z(value[d], d) for d in range(1, grid.nz)]
    return add_low(value[0], *got)


def body(
    clean_latent, noise_latent, codec_tokens, codec_mask, frames, timesteps, out_cotangent,
    master_blocks, norm_params, owned_block, left_stats, right_stats, left_root, right_root,
):
    n_data = lax.axis_size("dp")
    n_model = lax.axis_size("mp")
    total_devices = n_data * n_model
    clip_count = clean_latent.shape[0]
    ctx_len = codec_tokens.shape[1]
    slot_count, row_share = (master_blocks.shape[0], master_blocks.shape[1])
    param_rows, width = norm_params.shape
    grid = Grid(n_data, n_model)
    dp, mp = lax.axis_index("dp"), lax.axis_index("mp")
    me = dp * n_model + mp

    own_params = lax.dynamic_update_slice(
        jnp.zeros((8, CH), BF16), norm_params.astype(BF16), (0, me * width)
    )
    param_tiles = own_params.reshape(8, CH // BS, BS).transpose(1, 0, 2).reshape(-1, row_share, BS)
    skip = param_tiles.shape[0]
    master_low = master_blocks.astype(BF16)
    cut = slot_count // 2
    chunks = ((skip, 0, cut), (0, cut, slot_count - cut))
    ring0 = gather_z(grid, jnp.concatenate([param_tiles, master_low[:cut]]))
    ring1 = gather_z(grid, master_low[cut:])
    place_dp, place_mp = gather_places(grid)
    dest = jnp.stack([place_mp * slot_count, place_dp * row_share])

    phases = timesteps.astype(F32) * (0.5 * math.pi / TSTEPS)
    trig = jnp.stack([jnp.cos(phases), jnp.sin(phases)])
    embedding = jax.nn.silu(sinusoid(timesteps)).astype(BF16)
    emb_rows = jnp.broadcast_to(embedding[:, None, :], (clip_count, 16, CH))
    emb_pad = jnp.pad(embedding, ((0, 16 - clip_count), (0, 0)))
    kmask = jnp.broadcast_to(codec_mask.astype(F32)[:, None, :], (clip_count, 8, ctx_len))
    tok_t = codec_tokens.transpose(0, 2, 1)

    k = slot_count // n_data + 1
    padded = n_data * k
    k0 = k // 2

    def route(to_mp, to_slot):
        to_dp, to_k = to_slot // k, to_slot % k
        to_core = to_mp % 2
        rel_core = (to_core + grid.c) % 2
        dz = (to_dp // grid.ny - grid.z) % grid.nz
        dy = (to_dp % grid.ny - grid.y) % grid.ny
        dx = (to_mp // 2 - grid.x) % grid.nx
        swap = (to_core == 1) if grid.split else jnp.zeros_like(to_core == 1)
        d0, d1 = jnp.where(swap, dx, dy), jnp.where(swap, dy, dx)
        part = (to_k >= k0).astype(jnp.int32)
        k_part = jnp.where(part == 1, k - k0, k0)
        index = ((d1 * grid.sizes[0] + d0) * grid.nz + dz) * k_part + to_k - part * k0
        return rel_core * 2 + part, index

    block_ids = jnp.arange(NBLK, dtype=jnp.int32)
    slot_of_block = jnp.sum(
        jnp.where(owned_block[None, :] == block_ids[:, None], block_ids[None, :], 0), axis=1
    )
    pad_ids = jnp.arange(n_model * (padded - slot_count), dtype=jnp.int32)
    per = padded - slot_count
    block_mp = jnp.concatenate([slot_of_block // slot_count, pad_ids // per])
    block_slot = jnp.concatenate([slot_of_block % slot_count, pad_ids % per + slot_count])
    table = jnp.stack(route(block_mp, block_slot))
    model_ids = jnp.arange(n_model, dtype=jnp.int32)
    pad_quarter, pad_index = route(model_ids, jnp.full((n_model,), padded - 1, jnp.int32))
    pad_table = jnp.stack([pad_quarter // 2, pad_index])
    half = n_model * padded // 2
    sizes = tuple(half // k * kk for _ in range(2) for kk in (k0, k - k0))
    my_slots = lax.dynamic_slice_in_dim(slot_of_block, mp * slot_count, slot_count)
    from_mp = my_slots // slot_count
    where = (
        ((from_mp + grid.c) % 2 * grid.nx + (from_mp // 2 - grid.x) % grid.nx) * padded + my_slots % slot_count
    )

    inp, outlow, stats1, obias = pre(frames, trig, clean_latent, noise_latent, out_cotangent)
    stack0 = after(jnp.stack(ring0), stats1)
    pieces = gather_plane(grid, stack0)
    stack1 = after(jnp.stack(ring1), table, pad_table, where, dest, kmask, emb_rows, emb_pad, tok_t)
    later = gather_plane(grid, stack1)
    e1, o1, params = acts_windows(frames, inp, stats1, pieces)
    at = e1[:, 1].reshape(-1, CH).T
    e1 = after(e1, at)
    res, normed, stats2, blocks = conv_forward(
        frames, dest, e1, o1, inp, emb_rows, params, pieces + later, chunks
    )
    block_output, dq, dw_att = attention(
        frames, normed, codec_tokens, tok_t, kmask, outlow, res, params, blocks
    )
    rgrad, e2, o2, sums2 = norm2_backward(frames, dq, res, stats2, out_cotangent, params, blocks)
    keep0, keep1, send0, send1 = tap_gradients(table, at, emb_pad, sums2, dw_att, e2, o2, sizes)

    sums1, input_grad = [], None
    value0 = keep0
    for clip in range(clip_count):
        if clip == 1:
            value0 = scatter_core(grid, keep0, send0)
        input_grad, part = input_backward(
            clip, frames, after(e2, value0), o2, inp, stats1, rgrad, params, blocks, input_grad
        )
        sums1.append(part)
    value0 = scatter_plane(grid, value0, 1)
    keep1, send1 = add_norm_grads(pad_table, n_data, obias, sums2, sums1, keep1, send1)
    value1 = scatter_core(grid, keep1, send1)
    value0 = scatter_plane(grid, value0, 0)
    value1 = scatter_plane(grid, value1, 1)
    grad0 = scatter_z(grid, value0)
    value1 = scatter_plane(grid, value1, 0)
    grad1 = scatter_z(grid, value1)
    full_grad = jnp.concatenate([grad0, grad1])

    step, stats = owner_step(dp[None], full_grad, left_root, right_root, n_data, row_share)
    step = lax.all_to_all(step, "dp", 0, 0, tiled=True).reshape(padded, row_share, BS)
    near = jnp.concatenate(
        [step] + [grid.permute(step, lambda z, y, x, c, d=d: (z, y, x - d, c)) for d in range(1, grid.nx)]
    )
    far = grid.along_core(near)
    stats = lax.all_to_all(stats, "dp", 0, 0, tiled=True).reshape(padded, 3, row_share, BS)
    new_master, master_copy = update_master(where, master_blocks, near, far)
    owned_rows = stats[:slot_count, 0].astype(F32)
    new_left = 0.5 * left_stats + 0.5 * stats[:slot_count, 1].astype(F32)
    new_right = 0.5 * right_stats + 0.5 * stats[:slot_count, 2].astype(F32)
    norm_grads = stats[padded - 1, 0, :param_rows, :width].astype(F32)
    small_rate = 0.5 / math.sqrt(clip_count * total_devices * POS)
    new_norm = norm_params - small_rate * norm_grads
    return (
        block_output, input_grad, owned_rows, new_left, new_right, new_master, master_copy,
        norm_grads, new_norm,
    )


def solution(mesh):
    cells = P(("dp", "mp"), None, None)
    rows = P("mp", "dp", None)
    in_specs = (
        cells, cells, cells, P(("dp", "mp"), None), P(("dp", "mp")), P(("dp", "mp")), cells,
        rows, P(None, ("dp", "mp")), P(), rows, rows, P("mp", None, None), P("mp", None, None),
    )
    out_specs = (
        cells, cells, rows, rows, rows, rows, rows, P(None, ("dp", "mp")), P(None, ("dp", "mp")),
    )
    return jax.shard_map(body, mesh=mesh, in_specs=in_specs, out_specs=out_specs, check_vma=False)
```

```python
import functools
import math

import jax
import jax.numpy as jnp
from jax import lax
from jax.experimental import pallas as pl
from jax.experimental.pallas import tpu as pltpu
from jax.sharding import PartitionSpec as P

LATENT_CHANNELS = 512
GROUPS = 32
HEADS = 8
HEADDIM = 64
CTX = 768
BINS = 8
TSTEPS = 1000
BS = 128
POS = 1024
CH = LATENT_CHANNELS

highest = lax.Precision.HIGHEST
learn_rate = 0.5
out_gain = 8.0
eps = 1e-05

CONV_SCALE = 1.0 / math.sqrt(9 * CH)
INV_WIDTH = 1.0 / math.sqrt(CH)
INV_CTX = 1.0 / math.sqrt(CTX)
OUT_SCALE = out_gain / math.sqrt(CH)
ATT_SCALE = 1.0 / math.sqrt(HEADDIM)

SQ = (CH // BS) * (CH // BS)
KV = (CTX // BS) * (CH // BS)
TEMB0 = 9 * SQ
QUERY0 = TEMB0 + SQ
OUT0 = QUERY0 + SQ
KEY0 = OUT0 + SQ
VALUE0 = KEY0 + KV
NBLK = VALUE0 + KV

F32 = jnp.float32
BF16 = jnp.bfloat16
VMEM_LIMIT = 60 * 1024 * 1024


def nt(a, b):
    return lax.dot_general(a, b, (((1,), (1,)), ((), ())), preferred_element_type=F32)


def nn(a, b):
    return lax.dot_general(a, b, (((1,), (0,)), ((), ())), preferred_element_type=F32)


def mat(ref, base, nr, nc):
    rows = [jnp.concatenate([ref[base + a * nc + b] for b in range(nc)], axis=1) for a in range(nr)]
    return jnp.concatenate(rows, axis=0)


def row_iota(start, count):
    return lax.broadcasted_iota(jnp.int32, (count, 1), 0) + start


def fold8(x):
    return jnp.sum(x.reshape(-1, 8, x.shape[-1]), axis=0)


def group_sums(*partials):
    i = lax.broadcasted_iota(jnp.int32, (CH, CH), 0) // (CH // GROUPS)
    j = lax.broadcasted_iota(jnp.int32, (CH, CH), 1) // (CH // GROUPS)
    gmat = jnp.where(i == j, 1.0, 0.0).astype(BF16)
    row = lax.broadcasted_iota(jnp.int32, (16, CH), 0)
    stack = jnp.zeros((16, CH), F32)
    for k, rows8 in enumerate(partials):
        rest = jnp.sum(rows8, axis=0, keepdims=True)
        for t in range(3):
            term = rest.astype(BF16).astype(F32)
            stack = jnp.where(row == 3 * k + t, term, stack)
            rest = rest - term
    out = nn(stack.astype(BF16), gmat)
    sums = [out[3 * k : 3 * k + 1] + out[3 * k + 1 : 3 * k + 2] + out[3 * k + 2 : 3 * k + 3] for k in range(len(partials))]
    return sums[0] if len(sums) == 1 else sums


def shift_bins(tile, step):
    if step == 0:
        return tile
    t = tile.reshape(-1, 8, tile.shape[-1])
    rolled = pltpu.roll(t, (8 - step) % 8, 1)
    b = lax.broadcasted_iota(jnp.int32, (1, 8, 1), 1) + step
    keep = (b >= 0) & (b < 8)
    return jnp.where(keep, rolled, 0.0).reshape(tile.shape)


def write_windows(pad, e_ref, o_ref, sign, lead=0):
    T = 64

    def body(i, carry):
        r = pl.multiple_of(i * T, T)
        mid = pad[pl.ds(r + 8, T), :]
        low = pad[pl.ds(r, T), :]
        for d in range(3):
            step = sign * (d - 1)
            e_ref[lead, d, pl.ds(r, T), :] = shift_bins(mid, step).astype(BF16)
            o_ref[lead, d, pl.ds(r, T), :] = shift_bins(low, step).astype(BF16)
        return carry

    lax.fori_loop(0, POS // T, body, 0)
    last = pad[POS : POS + 16, :]
    for d in range(3):
        o_ref[lead, d, POS : POS + 16, :] = shift_bins(last, sign * (d - 1)).astype(BF16)


def window(e_ref, o_ref, df, db, r, n, lead=(0,)):
    if df == 1:
        return e_ref[lead + (db, pl.ds(r, n), slice(None))]
    off = 0 if df == 0 else 16
    return o_ref[lead + (db, pl.ds(pl.multiple_of(r + off, 16), n), slice(None))]


def pre_kernel(frames_s, trig_s, clean, noise, cot, inp, outlow, stats, obias):
    c = pl.program_id(0)
    rows = frames_s[c] * BINS
    cs, sn = trig_s[0, c], trig_s[1, c]
    T = 64
    zero = jnp.zeros((8, CH), F32)
    inv_n = 1.0 / (rows * (CH // GROUPS)).astype(F32)

    def first(i, carry):
        s0, s1 = carry
        r = pl.multiple_of(i * T, T)
        m = row_iota(r, T) < rows
        x = jnp.where(m, cs * clean[0, pl.ds(r, T), :] + sn * noise[0, pl.ds(r, T), :], 0.0)
        inp[0, pl.ds(r, T), :] = x
        g = jnp.where(m, cot[0, pl.ds(r, T), :], 0.0)
        outlow[0, pl.ds(r, T), :] = g.astype(BF16)
        return (s0 + fold8(x), s1 + fold8(g))

    s0, s1 = lax.fori_loop(0, POS // T, first, (zero, zero))
    mean = group_sums(s0) * inv_n

    def second(i, s):
        r = pl.multiple_of(i * T, T)
        m = row_iota(r, T) < rows
        d = jnp.where(m, inp[0, pl.ds(r, T), :] - mean, 0.0)
        return s + fold8(d * d)

    s2 = lax.fori_loop(0, POS // T, second, zero)
    rstd = lax.rsqrt(group_sums(s2) * inv_n + eps)
    stats[0] = jnp.concatenate([mean, rstd, jnp.zeros((6, CH), F32)], axis=0)
    obias[0] = s1


def pre(frames, trig, clean, noise, cot):
    n = clean.shape[0]
    big = pl.BlockSpec((1, POS, CH), lambda c, *_: (c, 0, 0))
    small = pl.BlockSpec((1, 8, CH), lambda c, *_: (c, 0, 0))
    return pl.pallas_call(
        pre_kernel,
        out_shape=(
            jax.ShapeDtypeStruct((n, POS, CH), F32),
            jax.ShapeDtypeStruct((n, POS, CH), BF16),
            jax.ShapeDtypeStruct((n, 8, CH), F32),
            jax.ShapeDtypeStruct((n, 8, CH), F32),
        ),
        grid_spec=pltpu.PrefetchScalarGridSpec(
            num_scalar_prefetch=2, grid=(n,), in_specs=[big, big, big], out_specs=[big, big, small, small]
        ),
        compiler_params=pltpu.CompilerParams(vmem_limit_bytes=VMEM_LIMIT),
        cost_estimate=pl.CostEstimate(flops=n * POS * CH * 20, bytes_accessed=n * POS * CH * 18, transcendentals=0),
        name="inputs_stats",
    )(frames, trig, clean, noise, cot)


def acts_kernel(frames_s, inp, stats, *refs):
    pieces, (e_ref, o_ref, params_ref, pad) = refs[:-4], refs[-4:]
    c = pl.program_id(0)
    rows = frames_s[c] * BINS
    T = 64
    total = None
    for piece in pieces:
        for j in range(piece.shape[0]):
            got = piece[j].astype(F32).reshape(CH // BS, 8, BS)
            total = got if total is None else total + got
    params = jnp.concatenate([total[j] for j in range(CH // BS)], axis=1)
    params_ref[...] = params
    mean, rstd = stats[0, 0:1], stats[0, 1:2]
    scale = rstd * params[0:1]
    shift = params[1:2]
    pad[0:8, :] = jnp.zeros((8, CH), F32)
    pad[8 + POS :, :] = jnp.zeros((8, CH), F32)

    def body(i, carry):
        r = pl.multiple_of(i * T, T)
        m = row_iota(r, T) < rows
        y = (inp[0, pl.ds(r, T), :] - mean) * scale + shift
        a = jnp.where(m, y * jax.nn.sigmoid(y), 0.0)
        pad[pl.ds(r + 8, T), :] = a
        return carry

    lax.fori_loop(0, POS // T, body, 0)
    write_windows(pad, e_ref, o_ref, 1)


def acts_windows(frames, inp, stats, pieces):
    n = inp.shape[0]
    row_share = pieces[0].shape[2]
    slots = CH // BS * 8 // row_share
    return pl.pallas_call(
        acts_kernel,
        out_shape=(
            jax.ShapeDtypeStruct((n, 3, POS, CH), BF16),
            jax.ShapeDtypeStruct((n, 3, POS + 16, CH), BF16),
            jax.ShapeDtypeStruct((8, CH), F32),
        ),
        grid_spec=pltpu.PrefetchScalarGridSpec(
            num_scalar_prefetch=1,
            grid=(n,),
            in_specs=[
                pl.BlockSpec((1, POS, CH), lambda c, *_: (c, 0, 0)),
                pl.BlockSpec((1, 8, CH), lambda c, *_: (c, 0, 0)),
            ]
            + [
                pl.BlockSpec((p.shape[0], slots, row_share, BS), lambda c, *_: (0, 0, 0, 0))
                for p in pieces
            ],
            out_specs=[
                pl.BlockSpec((1, 3, POS, CH), lambda c, *_: (c, 0, 0, 0)),
                pl.BlockSpec((1, 3, POS + 16, CH), lambda c, *_: (c, 0, 0, 0)),
                pl.BlockSpec((8, CH), lambda c, *_: (0, 0)),
            ],
            scratch_shapes=[pltpu.VMEM((POS + 16, CH), F32)],
        ),
        compiler_params=pltpu.CompilerParams(vmem_limit_bytes=VMEM_LIMIT),
        cost_estimate=pl.CostEstimate(
            flops=n * POS * CH * 30, bytes_accessed=n * POS * CH * 16, transcendentals=n * POS * CH
        ),
        name="acts",
    )(frames, inp, stats, *pieces)


def conv_kernel(chunks, frames_s, dest_s, e_ref, o_ref, inp, emb, params, *refs):
    pieces, (res, normed, stats, w_out, w, sem, sem_out) = refs[: -7], refs[-7:]
    c = pl.program_id(0)
    per_chunk = len(pieces) // len(chunks)
    row_share = pieces[0].shape[2]

    @pl.when(c == 0)
    def _():
        copies = []
        for j, (skip, start, count) in enumerate(chunks):
            for a in range(per_chunk):
                ref = pieces[j * per_chunk + a]
                for p in range(ref.shape[0]):
                    i = a * ref.shape[0] + p
                    first = dest_s[0, i] + start
                    row = pl.multiple_of(dest_s[1, i], row_share)
                    copies.append(
                        pltpu.make_async_copy(
                            ref.at[p, pl.ds(skip, count)],
                            w.at[pl.ds(first, count), pl.ds(row, row_share), :],
                            sem.at[len(copies)],
                        )
                    )
        for copy in copies:
            copy.start()
        for copy in copies:
            copy.wait()
        pltpu.make_async_copy(w, w_out, sem_out).start()

    rows = frames_s[c] * BINS
    R = 256
    T = 64
    zero = jnp.zeros((8, CH), F32)
    inv_n = 1.0 / (rows * (CH // GROUPS)).astype(F32)
    temb = nn(emb[0], mat(w, TEMB0, 4, 4))[0:1] * INV_WIDTH
    add = temb + params[2:3]

    def tile(i, s):
        r = pl.multiple_of(i * R, R)
        acc = jnp.zeros((R, CH), F32)
        for t in range(9):
            df, db = divmod(t, 3)
            acc = acc + nn(window(e_ref, o_ref, df, db, r, R), mat(w, t * SQ, 4, 4))
        v = inp[0, pl.ds(r, R), :] + acc * CONV_SCALE + add
        res[0, pl.ds(r, R), :] = v
        return s + fold8(jnp.where(row_iota(r, R) < rows, v, 0.0))

    s = lax.fori_loop(0, POS // R, tile, zero)
    mean = group_sums(s) * inv_n

    def second(i, s):
        r = pl.multiple_of(i * T, T)
        d = jnp.where(row_iota(r, T) < rows, res[0, pl.ds(r, T), :] - mean, 0.0)
        return s + fold8(d * d)

    s2 = lax.fori_loop(0, POS // T, second, zero)
    rstd = lax.rsqrt(group_sums(s2) * inv_n + eps)
    scale = rstd * params[3:4]
    shift = params[4:5]

    def third(i, carry):
        r = pl.multiple_of(i * T, T)
        normed[0, pl.ds(r, T), :] = ((res[0, pl.ds(r, T), :] - mean) * scale + shift).astype(BF16)
        return carry

    lax.fori_loop(0, POS // T, third, 0)
    stats[0] = jnp.concatenate([mean, rstd, jnp.zeros((6, CH), F32)], axis=0)

    @pl.when(c == pl.num_programs(0) - 1)
    def _():
        pltpu.make_async_copy(w, w_out, sem_out).wait()


def whole(shape):
    return pl.BlockSpec(shape, lambda *_: (0,) * len(shape), pipeline_mode=pl.Buffered(1))


def per_clip(shape):
    return pl.BlockSpec((1,) + shape, lambda c, *_: (c,) + (0,) * len(shape))


def conv_forward(frames, dest, e, o, inp, emb, params, pieces, chunks):
    n = inp.shape[0]
    copies = sum(p.shape[0] for p in pieces)
    return pl.pallas_call(
        functools.partial(conv_kernel, chunks),
        out_shape=(
            jax.ShapeDtypeStruct((n, POS, CH), F32),
            jax.ShapeDtypeStruct((n, POS, CH), BF16),
            jax.ShapeDtypeStruct((n, 8, CH), F32),
            jax.ShapeDtypeStruct((NBLK, BS, BS), BF16),
        ),
        grid_spec=pltpu.PrefetchScalarGridSpec(
            num_scalar_prefetch=2,
            grid=(n,),
            in_specs=[
                per_clip((3, POS, CH)),
                per_clip((3, POS + 16, CH)),
                per_clip((POS, CH)),
                per_clip((16, CH)),
                whole((8, CH)),
            ]
            + [pl.BlockSpec(memory_space=pl.ANY)] * len(pieces),
            out_specs=[
                per_clip((POS, CH)),
                per_clip((POS, CH)),
                per_clip((8, CH)),
                pl.BlockSpec(memory_space=pl.ANY),
            ],
            scratch_shapes=[
                pltpu.VMEM((NBLK, BS, BS), BF16),
                pltpu.SemaphoreType.DMA((copies,)),
                pltpu.SemaphoreType.DMA(()),
            ],
        ),
        compiler_params=pltpu.CompilerParams(vmem_limit_bytes=VMEM_LIMIT),
        cost_estimate=pl.CostEstimate(
            flops=n * POS * CH * CH * 18, bytes_accessed=n * POS * CH * 22 + 5000000, transcendentals=0
        ),
        name="conv_forward",
    )(frames, dest, e, o, inp, emb, params, *pieces)


def attn_kernel(
    frames_s, normed, tokens, tok_t, kmask, outlow, res, params, w,
    block_out, dq_ref, dw_ref,
    q_s, do_s, qt_s, dot_s, mixed_s, dkt_s, dvt_s, dkv_acc, km_s, s_s, dp_s, pb_s, ds_s, odq_s, dw_s,
):
    c = pl.program_id(0)
    rows = frames_s[c] * BINS
    R = 256
    C = 32
    def project(i, carry):
        r = pl.multiple_of(i * R, R)
        q = (nn(normed[0, pl.ds(r, R), :], mat(w, SQ, 4, 4)) * INV_WIDTH).astype(BF16)
        q_s[pl.ds(r, R), :] = q
        qt_s[:, pl.ds(r, R)] = q.T
        d = (nt(outlow[0, pl.ds(r, R), :], mat(w, 2 * SQ, 4, 4)) * OUT_SCALE).astype(BF16)
        do_s[pl.ds(r, R), :] = d
        dot_s[:, pl.ds(r, R)] = d.T
        return carry

    lax.fori_loop(0, POS // R, project, 0)
    lane = lax.broadcasted_iota(jnp.int32, (1, BS), 1)
    first = lane < HEADDIM
    keys = ((nn(tokens[0], mat(w, 3 * SQ, CTX // BS, 4)) * INV_CTX).astype(BF16).astype(F32) * ATT_SCALE).astype(BF16)
    values = (nn(tokens[0], mat(w, 3 * SQ + KV, CTX // BS, 4)) * INV_CTX).astype(BF16)
    for slab in range(HEADS // 2):
        for j, side in enumerate((keys, values)):
            two = side[:, slab * BS : (slab + 1) * BS]
            none = jnp.zeros_like(two)
            km_s[slab, 2 * j] = jnp.where(first, two, none)
            km_s[slab, 2 * j + 1] = jnp.where(first, none, two)
    dkv_acc[...] = jnp.zeros_like(dkv_acc)
    pb_s[1] = jnp.zeros(pb_s.shape[1:], BF16)
    ds_s[1] = jnp.zeros(ds_s.shape[1:], BF16)
    valid = kmask[0, 0:1, :] > 0.0
    RA = s_s.shape[1]
    tiles = POS // RA
    steps = HEADS // 2 * tiles

    def place(i):
        slab = i // tiles
        return slab, pl.ds(pl.multiple_of(slab * BS, BS), BS), pl.ds(pl.multiple_of(i % tiles * RA, RA), RA)

    def scores(i, h):
        slab, cols, at = place(i)
        s_s[h] = nt(q_s[at, cols], km_s[slab, h])
        dp_s[h] = nt(do_s[at, cols], km_s[slab, 2 + h])

    def soften(h):
        for j in range(RA // C):
            part = slice(j * C, (j + 1) * C)
            s = jnp.where(valid, s_s[h, part, :], -1000000000.0)
            e = jnp.exp(s - jnp.max(s, axis=-1, keepdims=True))
            p = e * (1.0 / jnp.sum(e, axis=-1, keepdims=True))
            pb_s[h, part, :] = p.astype(BF16)
            dp = dp_s[h, part, :]
            delta = jnp.sum(p * dp, axis=-1, keepdims=True)
            ds_s[h, part, :] = (p * (dp - delta)).astype(BF16)

    def back(i, h):
        slab, cols, at = place(i)
        half = pl.ds(pl.multiple_of(slab * BS + h * HEADDIM, HEADDIM), HEADDIM)
        mine = slice(h * HEADDIM, (h + 1) * HEADDIM)
        pb, ds = pb_s[h], ds_s[h]
        dkv_acc[slab, 0, mine, :] += nn(qt_s[half, at], ds)
        dkv_acc[slab, 1, mine, :] += nn(dot_s[half, at], pb)
        o, dq = nn(pb, km_s[slab, 2 + h]), nn(ds, km_s[slab, h])
        if h == 0:
            odq_s[0] = o
            odq_s[1] = dq
        else:
            mixed_s[at, cols] = (odq_s[0] + o).astype(BF16)
            dq_ref[0, at, cols] = (odq_s[1] + dq).astype(BF16)

    scores(0, 0)

    def step(i, carry):
        back(jnp.maximum(i - 1, 0), 1)
        scores(i, 1)
        soften(0)
        back(i, 0)
        scores(jnp.minimum(i + 1, steps - 1), 0)
        soften(1)
        return carry

    odq_s[...] = jnp.zeros_like(odq_s)
    lax.fori_loop(0, steps, step, 0)
    back(steps - 1, 1)
    for slab in range(HEADS // 2):
        cols = slice(slab * BS, (slab + 1) * BS)
        dkt_s[cols, :] = (dkv_acc[slab, 0] * ATT_SCALE).astype(BF16)
        dvt_s[cols, :] = dkv_acc[slab, 1].astype(BF16)

    def project_out(i, carry):
        r = pl.multiple_of(i * R, R)
        proj = nn(mixed_s[pl.ds(r, R), :], mat(w, 2 * SQ, 4, 4)) * OUT_SCALE + params[5:6]
        m = row_iota(r, R) < rows
        block_out[0, pl.ds(r, R), :] = jnp.where(m, res[0, pl.ds(r, R), :] + proj, 0.0)
        return carry

    lax.fori_loop(0, POS // R, project_out, 0)

    @pl.when(c == 0)
    def _():
        dw_s[...] = jnp.zeros_like(dw_s)

    dw_s[0:CH, :] += nn(normed[0].T, dq_ref[0])
    dw_s[CH : 2 * CH, :] += nn(mixed_s[...].T, outlow[0])
    dw_s[2 * CH : 2 * CH + CTX, :] += nt(tok_t[0], dkt_s[...])
    dw_s[2 * CH + CTX :, :] += nt(tok_t[0], dvt_s[...])

    @pl.when(c == pl.num_programs(0) - 1)
    def _():
        def cut(i, carry):
            r = pl.multiple_of(i * BS, BS)
            scale = jnp.where(i < CH // BS, INV_WIDTH, jnp.where(i < 2 * CH // BS, OUT_SCALE, INV_CTX))
            low = (dw_s[pl.ds(r, BS), :] * scale).astype(BF16)
            for b in range(CH // BS):
                dw_ref[i * (CH // BS) + b] = low[:, b * BS : (b + 1) * BS]
            return carry

        lax.fori_loop(0, dw_s.shape[0] // BS, cut, 0)


def attention(frames, normed, tokens, tok_t, kmask, outlow, res, params, w):
    n = normed.shape[0]
    ctx_len = tokens.shape[1]
    amount = SQ + SQ + SQ + KV + KV
    return pl.pallas_call(
        attn_kernel,
        out_shape=(
            jax.ShapeDtypeStruct((n, POS, CH), F32),
            jax.ShapeDtypeStruct((n, POS, CH), BF16),
            jax.ShapeDtypeStruct((NBLK - QUERY0, BS, BS), BF16),
        ),
        grid_spec=pltpu.PrefetchScalarGridSpec(
            num_scalar_prefetch=1,
            grid=(n,),
            in_specs=[
                per_clip((POS, CH)),
                per_clip((ctx_len, CTX)),
                per_clip((CTX, ctx_len)),
                per_clip((8, ctx_len)),
                per_clip((POS, CH)),
                per_clip((POS, CH)),
                whole((8, CH)),
                pl.BlockSpec(
                    (pl.Element(amount), pl.Element(BS), pl.Element(BS)),
                    lambda *_: (TEMB0, 0, 0),
                    pipeline_mode=pl.Buffered(1),
                ),
            ],
            out_specs=[
                per_clip((POS, CH)),
                per_clip((POS, CH)),
                pl.BlockSpec((NBLK - QUERY0, BS, BS), lambda *_: (0, 0, 0)),
            ],
            scratch_shapes=[
                pltpu.VMEM((POS, CH), BF16),
                pltpu.VMEM((POS, CH), BF16),
                pltpu.VMEM((CH, POS), BF16),
                pltpu.VMEM((CH, POS), BF16),
                pltpu.VMEM((POS, CH), BF16),
                pltpu.VMEM((CH, ctx_len), BF16),
                pltpu.VMEM((CH, ctx_len), BF16),
                pltpu.VMEM((HEADS // 2, 2, BS, ctx_len), F32),
                pltpu.VMEM((HEADS // 2, 4, ctx_len, BS), BF16),
                pltpu.VMEM((2, 256, ctx_len), F32),
                pltpu.VMEM((2, 256, ctx_len), F32),
                pltpu.VMEM((2, 256, ctx_len), BF16),
                pltpu.VMEM((2, 256, ctx_len), BF16),
                pltpu.VMEM((2, 256, BS), F32),
                pltpu.VMEM((2 * CH + 2 * CTX, CH), F32),
            ],
        ),
        compiler_params=pltpu.CompilerParams(vmem_limit_bytes=VMEM_LIMIT),
        cost_estimate=pl.CostEstimate(
            flops=n * POS * CH * (6 * CH * 2 + 24 * ctx_len),
            bytes_accessed=n * POS * CH * 16,
            transcendentals=n * POS * HEADS * ctx_len,
        ),
        name="attention",
    )(frames, normed, tokens, tok_t, kmask, outlow, res, params, w)


def taps_kernel(
    counts, frames_s, slots_s, owned_s, dq_ref, res, stats, cot, params, w, at, emb, dw_att,
    rgrad, sums, e_out, o_out, *refs,
):
    outs, refs = refs[: len(counts)], refs[len(counts) :]
    ng_s, pad, e_ref, o_ref, blocks, sem, sem_w = refs
    n = e_ref.shape[0]
    step = pl.program_id(0)
    T = 64

    @pl.when(step == 0)
    def _():
        blocks[NBLK] = jnp.zeros((BS, BS), BF16)
        pltpu.make_async_copy(dw_att, blocks.at[pl.ds(QUERY0, NBLK - QUERY0)], sem.at[0]).start()

    @pl.when(step < n)
    def _():
        rows = frames_s[step] * BINS
        R = 256
        zero = jnp.zeros((8, CH), F32)
        inv_n = 1.0 / (rows * (CH // GROUPS)).astype(F32)
        mean, rstd = stats[0, 0:1], stats[0, 1:2]
        gain = params[3:4]

        def first(i, carry):
            s0, s1 = carry
            r = pl.multiple_of(i * R, R)
            ng = nt(dq_ref[0, pl.ds(r, R), :], mat(w, 0, 4, 4)) * INV_WIDTH
            m = row_iota(r, R) < rows
            ng = jnp.where(m, ng, 0.0)
            ng_s[pl.ds(r, R), :] = ng
            x = jnp.where(m, (res[0, pl.ds(r, R), :] - mean) * rstd, 0.0)
            return (s0 + fold8(ng), s1 + fold8(ng * x))

        s0, s1 = lax.fori_loop(0, POS // R, first, (zero, zero))
        mh, mhx = group_sums(s0 * gain, s1 * gain)
        scale, mh, mhx = rstd * gain, rstd * mh * inv_n, rstd * mhx * inv_n
        pad[0:8, :] = zero
        pad[8 + POS :, :] = zero

        def second(i, s):
            r = pl.multiple_of(i * T, T)
            m = row_iota(r, T) < rows
            x = (res[0, pl.ds(r, T), :] - mean) * rstd
            d = scale * ng_s[pl.ds(r, T), :] - mh - x * mhx
            g = jnp.where(m, cot[0, pl.ds(r, T), :] + d, 0.0)
            rgrad[0, pl.ds(r, T), :] = g
            pad[pl.ds(r + 8, T), :] = g
            return s + fold8(g)

        s2 = lax.fori_loop(0, POS // T, second, zero)
        sums[pl.ds(step, 1)] = jnp.concatenate([s2, s1, s0], axis=0)[None]
        write_windows(pad, e_ref, o_ref, -1, step)
        pltpu.make_async_copy(e_ref.at[step], e_out.at[step], sem_w.at[2 * step]).start()
        pltpu.make_async_copy(o_ref.at[step], o_out.at[step], sem_w.at[2 * step + 1]).start()

    def cut(value, first):
        low = value.astype(BF16)
        for a in range(4):
            for b in range(4):
                blocks[first + a * 4 + b] = low[a * BS : (a + 1) * BS, b * BS : (b + 1) * BS]

    @pl.when(step >= n)
    def _():
        d = step - n
        for df in range(3):
            acc = None
            for c in range(n):
                g = window(e_ref, o_ref, 2 - df, d, 0, POS, (c,))
                part = nn(at[:, c * POS : (c + 1) * POS], g)
                acc = part if acc is None else acc + part
            cut(acc * CONV_SCALE, (3 * df + d) * SQ)

    @pl.when(step == pl.num_programs(0) - 1)
    def _():
        rows = [jnp.sum(sums[c, 0:8], axis=0, keepdims=True) for c in range(n)]
        grad = jnp.concatenate(rows + [jnp.zeros((16 - n, CH), F32)], axis=0).astype(BF16)
        outer = lax.dot_general(emb[...], grad, (((0,), (0,)), ((), ())), preferred_element_type=F32)
        cut(outer * INV_WIDTH, TEMB0)
        pltpu.make_async_copy(dw_att, blocks.at[pl.ds(QUERY0, NBLK - QUERY0)], sem.at[0]).wait()
        start = sum(counts)
        for q in reversed(range(len(counts))):
            start -= counts[q]

            def send(i, carry, q=q, start=start):
                for u in range(8):
                    t = i * 8 + u
                    src = owned_s[slots_s[start + t]]
                    pltpu.make_async_copy(blocks.at[src], outs[q].at[t], sem.at[1 + q]).start()
                return carry

            lax.fori_loop(0, counts[q] // 8, send, 0)
        for c in range(n):
            pltpu.make_async_copy(e_ref.at[c], e_out.at[c], sem_w.at[2 * c]).wait()
            pltpu.make_async_copy(o_ref.at[c], o_out.at[c], sem_w.at[2 * c + 1]).wait()
        for q, out in enumerate(outs):
            pltpu.make_async_copy(out, out, sem.at[1 + q]).wait()


def tap_gradients(frames, slots, owned, dq, res, stats, cot, params, w, at, emb, dw_att, counts):
    n = dq.shape[0]

    def of_clip(shape):
        return pl.BlockSpec((1,) + shape, lambda i, *_: (jnp.minimum(i, n - 1),) + (0,) * len(shape))

    any_space = pl.BlockSpec(memory_space=pl.ANY)
    return pl.pallas_call(
        functools.partial(taps_kernel, counts),
        out_shape=(
            jax.ShapeDtypeStruct((n, POS, CH), F32),
            jax.ShapeDtypeStruct((n, 24, CH), F32),
            jax.ShapeDtypeStruct((n, 3, POS, CH), BF16),
            jax.ShapeDtypeStruct((n, 3, POS + 16, CH), BF16),
        )
        + tuple(jax.ShapeDtypeStruct((s, BS, BS), BF16) for s in counts),
        grid_spec=pltpu.PrefetchScalarGridSpec(
            num_scalar_prefetch=3,
            grid=(n + 3,),
            in_specs=[
                of_clip((POS, CH)),
                of_clip((POS, CH)),
                of_clip((8, CH)),
                of_clip((POS, CH)),
                whole((8, CH)),
                pl.BlockSpec((SQ, BS, BS), lambda *_: (QUERY0 // SQ, 0, 0), pipeline_mode=pl.Buffered(1)),
                whole((CH, n * POS)),
                whole((16, CH)),
                any_space,
            ],
            out_specs=[of_clip((POS, CH)), pl.BlockSpec((n, 24, CH), lambda *_: (0, 0, 0)), any_space, any_space]
            + [any_space] * len(counts),
            scratch_shapes=[
                pltpu.VMEM((POS, CH), F32),
                pltpu.VMEM((POS + 16, CH), F32),
                pltpu.VMEM((n, 3, POS, CH), BF16),
                pltpu.VMEM((n, 3, POS + 16, CH), BF16),
                pltpu.VMEM((NBLK + 1, BS, BS), BF16),
                pltpu.SemaphoreType.DMA((1 + len(counts),)),
                pltpu.SemaphoreType.DMA((2 * n,)),
            ],
        ),
        compiler_params=pltpu.CompilerParams(vmem_limit_bytes=VMEM_LIMIT),
        cost_estimate=pl.CostEstimate(
            flops=n * POS * CH * CH * 20, bytes_accessed=n * POS * CH * 30 + 20000000, transcendentals=0
        ),
        name="tap_gradients",
    )(frames, slots, owned, dq, res, stats, cot, params, w, at, emb, dw_att)


def input_kernel(clip, frames_s, e_ref, o_ref, inp, stats, rgrad, params, w, *refs):
    out, sums, ag_s = refs[-3:]
    c = clip
    rows = frames_s[c] * BINS
    R = 256
    T = 64
    zero = jnp.zeros((8, CH), F32)
    inv_n = 1.0 / (rows * (CH // GROUPS)).astype(F32)
    mean, rstd = stats[0, 0:1], stats[0, 1:2]
    gain, shift = params[0:1], params[1:2]

    def conv(i, carry):
        r = pl.multiple_of(i * R, R)
        acc = jnp.zeros((R, CH), F32)
        for t in range(9):
            df, db = divmod(t, 3)
            acc = acc + nt(window(e_ref, o_ref, 2 - df, db, r, R), mat(w, t * SQ, 4, 4))
        ag_s[pl.ds(r, R), :] = acc * CONV_SCALE
        return carry

    lax.fori_loop(0, POS // R, conv, 0)

    def first(i, carry):
        s0, s1 = carry
        r = pl.multiple_of(i * T, T)
        m = row_iota(r, T) < rows
        x = (inp[0, pl.ds(r, T), :] - mean) * rstd
        y = x * gain + shift
        sg = jax.nn.sigmoid(y)
        dy = jnp.where(m, ag_s[pl.ds(r, T), :] * (sg * (1.0 + y * (1.0 - sg))), 0.0)
        ag_s[pl.ds(r, T), :] = dy
        return (s0 + fold8(dy), s1 + fold8(dy * x))

    s0, s1 = lax.fori_loop(0, POS // T, first, (zero, zero))
    mh, mhx = group_sums(s0 * gain, s1 * gain)
    mh, mhx = mh * inv_n, mhx * inv_n

    def second(i, carry):
        r = pl.multiple_of(i * T, T)
        m = row_iota(r, T) < rows
        x = (inp[0, pl.ds(r, T), :] - mean) * rstd
        d = rstd * (gain * ag_s[pl.ds(r, T), :] - mh - x * mhx)
        out[0, pl.ds(r, T), :] = jnp.where(m, rgrad[0, pl.ds(r, T), :] + d, 0.0)
        return carry

    lax.fori_loop(0, POS // T, second, 0)
    sums[0, 0:8] = s1
    sums[0, 8:16] = s0


def input_backward(clip, frames, e, o, inp, stats, rgrad, params, w, before=None):
    n = inp.shape[0]

    def of_clip(shape):
        return pl.BlockSpec((1,) + shape, lambda i, *_: (clip,) + (0,) * len(shape))

    before = () if before is None else (before,)
    return pl.pallas_call(
        functools.partial(input_kernel, clip),
        out_shape=(
            jax.ShapeDtypeStruct((n, POS, CH), F32),
            jax.ShapeDtypeStruct((1, 16, CH), F32),
        ),
        grid_spec=pltpu.PrefetchScalarGridSpec(
            num_scalar_prefetch=1,
            grid=(1,),
            in_specs=[
                of_clip((3, POS, CH)),
                of_clip((3, POS + 16, CH)),
                of_clip((POS, CH)),
                of_clip((8, CH)),
                of_clip((POS, CH)),
                whole((8, CH)),
                pl.BlockSpec((TEMB0, BS, BS), lambda *_: (0, 0, 0), pipeline_mode=pl.Buffered(1)),
            ]
            + [pl.BlockSpec(memory_space=pl.ANY)] * len(before),
            out_specs=[of_clip((POS, CH)), pl.BlockSpec((1, 16, CH), lambda *_: (0, 0, 0))],
            scratch_shapes=[pltpu.VMEM((POS, CH), F32)],
        ),
        input_output_aliases={8: 0} if before else {},
        compiler_params=pltpu.CompilerParams(vmem_limit_bytes=VMEM_LIMIT),
        cost_estimate=pl.CostEstimate(
            flops=POS * CH * CH * 18, bytes_accessed=POS * CH * 24, transcendentals=POS * CH
        ),
        name="input_backward",
    )(frames, e, o, inp, stats, rgrad, params, w, *before)


def norm_grads_kernel(obias, sums2, *refs):
    sums1, tiles = refs[:-1], refs[-1]
    count = tiles.shape[0]
    width = CH // count
    total = lambda v: jnp.sum(v, axis=0, keepdims=True)
    first = sums1[0][0]
    for v in sums1[1:]:
        first = first + v[0]
    second, bias = sums2[0], obias[0]
    for i in range(1, sums2.shape[0]):
        second, bias = second + sums2[i], bias + obias[i]
    grads = jnp.concatenate(
        [
            total(first[0:8]), total(first[8:16]), total(second[0:8]), total(second[8:16]),
            total(second[16:24]), total(bias), jnp.zeros((2, CH), F32),
        ],
        axis=0,
    )
    lane = lax.broadcasted_iota(jnp.int32, (8, BS), 1)
    for d in range(count):
        at = d * width
        tile = grads[:, at // BS * BS : (at // BS + 1) * BS]
        tile = pltpu.roll(tile, (BS - at % BS) % BS, 1)
        tiles[d] = jnp.where(lane < width, tile, 0.0)


def norm_grad_tiles(count, obias, sums2, sums1):
    vm = pl.BlockSpec(memory_space=pltpu.VMEM)
    return pl.pallas_call(
        norm_grads_kernel,
        out_shape=jax.ShapeDtypeStruct((count, 8, BS), F32),
        in_specs=[vm] * (2 + len(sums1)),
        out_specs=vm,
        cost_estimate=pl.CostEstimate(flops=100000, bytes_accessed=400000, transcendentals=0),
        name="norm_grads",
    )(obias, sums2, *sums1)


def sinusoid(timesteps):
    half_width = CH // 2
    freqs = jnp.exp(-math.log(10000.0) * jnp.arange(half_width, dtype=F32) / half_width)
    angles = timesteps.astype(F32)[:, None] * freqs[None, :]
    return jnp.concatenate([jnp.sin(angles), jnp.cos(angles)], axis=-1)


def step_kernel(dp_s, grad, left_root, right_root, step, stats):
    g = grad[0]
    low = g.astype(BF16)
    n_data, row_share = step.shape[0], step.shape[2]
    left = nt(low, low)
    right = lax.dot_general(low, low, (((0,), (0,)), ((), ())), preferred_element_type=F32)
    side = nn(left_root[0].astype(BF16), low)
    update = nn(side.astype(BF16), right_root[0].astype(BF16))
    rate = learn_rate * lax.rsqrt(jnp.sum(update * update, keepdims=True) * (1.0 / (BS * BS)) + 1e-06)
    step[:, 0] = (update * rate).reshape(n_data, row_share, BS).astype(BF16)
    stats[:, 0, 0] = g.reshape(n_data, row_share, BS).astype(BF16)
    stats[:, 0, 1] = left.reshape(n_data, row_share, BS).astype(BF16)
    stats[:, 0, 2] = right.reshape(n_data, row_share, BS).astype(BF16)


def owner_step(dp, grad, left_root, right_root, n_data, row_share):
    k = grad.shape[0]
    last = left_root.shape[0] - 1
    root = pl.BlockSpec((1, BS, BS), lambda i, dp: (jnp.minimum(dp[0] * k + i, last), 0, 0))
    return pl.pallas_call(
        step_kernel,
        out_shape=(
            jax.ShapeDtypeStruct((n_data, k, row_share, BS), BF16),
            jax.ShapeDtypeStruct((n_data, k, 3, row_share, BS), BF16),
        ),
        grid_spec=pltpu.PrefetchScalarGridSpec(
            num_scalar_prefetch=1,
            grid=(k,),
            in_specs=[pl.BlockSpec((1, BS, BS), lambda i, dp: (i, 0, 0)), root, root],
            out_specs=[
                pl.BlockSpec((n_data, 1, row_share, BS), lambda i, dp: (0, i, 0, 0)),
                pl.BlockSpec((n_data, 1, 3, row_share, BS), lambda i, dp: (0, i, 0, 0, 0)),
            ],
        ),
        cost_estimate=pl.CostEstimate(flops=k * 8 * BS**3, bytes_accessed=k * BS * BS * 20, transcendentals=0),
        name="owner_step",
    )(dp, grad, left_root, right_root)


def master_kernel(where_s, master, near, far, new, low, steps):
    half = near.shape[0]
    steps[0:half] = near[...].astype(F32)
    steps[half:] = far[...].astype(F32)

    def one(j, carry):
        value = master[j] - steps[where_s[j]]
        new[j] = value
        low[j] = value.astype(BF16)
        return carry

    lax.fori_loop(0, master.shape[0], one, 0)


def update_master(where, master, near, far):
    vm = pl.BlockSpec(memory_space=pltpu.VMEM)
    return pl.pallas_call(
        master_kernel,
        out_shape=(
            jax.ShapeDtypeStruct(master.shape, F32),
            jax.ShapeDtypeStruct(master.shape, BF16),
        ),
        in_specs=[pl.BlockSpec(memory_space=pltpu.SMEM), vm, vm, vm],
        out_specs=[vm, vm],
        scratch_shapes=[pltpu.VMEM((2 * near.shape[0],) + near.shape[1:], F32)],
        cost_estimate=pl.CostEstimate(flops=300000, bytes_accessed=3000000, transcendentals=0),
        name="update_master",
    )(where, master, near, far)


class Grid:
    def __init__(self, n_data, n_model):
        self.nd, self.nm = n_data, n_model
        self.nx = n_model // 2
        self.ny = 1
        while self.ny * self.ny * 4 <= n_data:
            self.ny *= 2
        self.nz = n_data // self.ny
        self.split = self.nx == self.ny
        self.sizes = (self.ny, self.ny) if self.split else (self.ny, self.nx)
        dp, mp = lax.axis_index("dp"), lax.axis_index("mp")
        self.z, self.y, self.x, self.c = dp // self.ny, dp % self.ny, mp // 2, mp % 2

    def permute(self, value, fn):
        pairs = []
        for src in range(self.nd * self.nm):
            dp, mp = divmod(src, self.nm)
            z, y, x, c = fn(dp // self.ny, dp % self.ny, mp // 2, mp % 2)
            dst = ((z % self.nz) * self.ny + y % self.ny) * self.nm + (x % self.nx) * 2 + c % 2
            pairs.append((src, dst))
        return lax.ppermute(value, ("dp", "mp"), pairs)

    def along_z(self, value, d):
        return self.permute(value, lambda z, y, x, c: (z + d, y, x, c))

    def along_plane(self, value, stage, d):
        def fn(z, y, x, c):
            on_y = (stage == 0) != (self.split and c == 1)
            return (z, y + d, x, c) if on_y else (z, y, x + d, c)

        return self.permute(value, fn)

    def along_core(self, value):
        return self.permute(value, lambda z, y, x, c: (z, y, x, c + 1))

    def place(self, core, d0, d1, dz):
        swap = (core == 1) if self.split else jnp.zeros_like(core == 1)
        dy, dx = jnp.where(swap, d1, d0), jnp.where(swap, d0, d1)
        zz, yy, xx = (self.z + dz) % self.nz, (self.y + dy) % self.ny, (self.x + dx) % self.nx
        return zz * self.ny + yy, xx * 2 + core


def after(value, *others):
    return lax.optimization_barrier((value,) + others)[0]


def after_all(values, *others):
    return list(lax.optimization_barrier(tuple(values) + others)[: len(values)])


def gather_z(grid, shard):
    return [shard] + [grid.along_z(shard, -d) for d in range(1, grid.nz)]


def gather_plane(grid, stack, stage):
    return [stack] + [grid.along_plane(stack, stage, -d) for d in range(1, grid.sizes[stage])]


def gather_core(grid, got):
    return got + [grid.along_core(v) for v in got]


def gather_places(grid):
    dps, mps = [], []
    for rel in range(2):
        core = (grid.c + rel) % 2
        for d1 in range(grid.sizes[1]):
            for d0 in range(grid.sizes[0]):
                for dz in range(grid.nz):
                    dp, mp = grid.place(core, d0, d1, dz)
                    dps.append(dp)
                    mps.append(mp)
    return jnp.stack(dps), jnp.stack(mps)


def add_low(*parts):
    total = parts[0].astype(F32)
    for p in parts[1:]:
        total = total + p.astype(F32)
    return total


def scatter_core(grid, keep, send):
    return add_low(keep, grid.along_core(send)).astype(BF16)


def send_plane(grid, value, stage):
    value = value.reshape(grid.sizes[stage], -1, BS, BS)
    return [value[0]] + [grid.along_plane(value[d], stage, d) for d in range(1, value.shape[0])]


def send_z(grid, value):
    value = value.reshape(grid.nz, -1, BS, BS)
    return [value[0]] + [grid.along_z(value[d], d) for d in range(1, value.shape[0])]


def body(
    clean_latent, noise_latent, codec_tokens, codec_mask, frames, timesteps, out_cotangent,
    master_blocks, norm_params, owned_block, left_stats, right_stats, left_root, right_root,
):
    n_data = lax.axis_size("dp")
    n_model = lax.axis_size("mp")
    total_devices = n_data * n_model
    clip_count = clean_latent.shape[0]
    ctx_len = codec_tokens.shape[1]
    slot_count, row_share = (master_blocks.shape[0], master_blocks.shape[1])
    param_rows, width = norm_params.shape
    grid = Grid(n_data, n_model)
    dp, mp = lax.axis_index("dp"), lax.axis_index("mp")
    me = dp * n_model + mp

    own_params = lax.dynamic_update_slice(
        jnp.zeros((8, CH), BF16), norm_params.astype(BF16), (0, me * width)
    )
    param_tiles = own_params.reshape(8, CH // BS, BS).transpose(1, 0, 2).reshape(-1, row_share, BS)
    skip = param_tiles.shape[0]
    master_low = master_blocks.astype(BF16)
    cut = slot_count * 3 // 10
    chunks = ((skip, 0, cut), (0, cut, slot_count - cut))
    ring0 = gather_z(grid, jnp.concatenate([param_tiles, master_low[:cut]]))
    ring1 = gather_z(grid, master_low[cut:])
    place_dp, place_mp = gather_places(grid)
    dest = jnp.stack([place_mp * slot_count, place_dp * row_share])

    phases = timesteps.astype(F32) * (0.5 * math.pi / TSTEPS)
    trig = jnp.stack([jnp.cos(phases), jnp.sin(phases)])
    embedding = jax.nn.silu(sinusoid(timesteps)).astype(BF16)
    emb_rows = jnp.broadcast_to(embedding[:, None, :], (clip_count, 16, CH))
    emb_pad = jnp.pad(embedding, ((0, 16 - clip_count), (0, 0)))
    kmask = jnp.broadcast_to(codec_mask.astype(F32)[:, None, :], (clip_count, 8, ctx_len))
    tok_t = codec_tokens.transpose(0, 2, 1)

    k = slot_count // n_data + 1
    padded = n_data * k
    k0 = max(1, k // 4)

    planes = grid.sizes[0] * grid.sizes[1]
    half = n_model * padded // 2
    counts, slot_list = [], []
    for rel in range(2):
        core = (grid.c + rel) % 2
        for part, kk in ((0, k0), (1, k - k0)):
            t = jnp.arange(half // k * kk, dtype=jnp.int32)
            group, k_id = t // kk, t % kk + part * k0
            if part == 1:
                plane, dz = group // grid.nz, group % grid.nz
            else:
                plane, dz = group % planes, group // planes
            to_dp, to_mp = grid.place(core, plane % grid.sizes[0], plane // grid.sizes[0], dz)
            to_slot = to_dp * k + k_id
            slot_list.append(jnp.where(to_slot < slot_count, to_mp * slot_count + to_slot, NBLK))
            counts.append(half // k * kk)
    slots = jnp.concatenate(slot_list)
    owned = jnp.concatenate([owned_block, jnp.full((1,), NBLK, jnp.int32)])
    counts = tuple(counts)
    block_ids = jnp.arange(NBLK, dtype=jnp.int32)
    slot_of_block = jnp.sum(
        jnp.where(owned_block[None, :] == block_ids[:, None], block_ids[None, :], 0), axis=1
    )
    my_slots = lax.dynamic_slice_in_dim(slot_of_block, mp * slot_count, slot_count)
    from_mp = my_slots // slot_count
    where = (
        ((from_mp + grid.c) % 2 * grid.nx + (from_mp // 2 - grid.x) % grid.nx) * padded + my_slots % slot_count
    )

    stack0 = jnp.stack(ring0)
    inp, outlow, stats1, obias = pre(after(frames, stack0), trig, clean_latent, noise_latent, out_cotangent)
    got0 = jnp.concatenate(gather_plane(grid, stack0, 0))
    stack1 = after(jnp.stack(ring1), stats1, got0)
    got0 = gather_plane(grid, got0, 1)
    pieces = gather_core(grid, got0)
    got1 = jnp.concatenate(gather_plane(grid, stack1, 0))
    got1 = after(got1, *got0[1:])
    ready = after(frames, slots, owned, where, dest, kmask, emb_rows, emb_pad, tok_t)
    e1, o1, params = acts_windows(ready, inp, stats1, pieces)
    at = e1[:, 1].reshape(-1, CH).T
    got1 = gather_plane(grid, got1, 1)
    got1 = [got1[0]] + [after(v, e1) for v in got1[1:]]
    later = gather_core(grid, got1)
    e1 = after(e1, at)
    res, normed, stats2, blocks = conv_forward(
        frames, dest, e1, o1, inp, emb_rows, params, pieces + later, chunks
    )
    block_output, dq, dw_att = attention(
        frames, normed, codec_tokens, tok_t, kmask, outlow, res, params, blocks
    )
    rgrad, sums2, e2, o2, keep0, keep1, send0, send1 = tap_gradients(
        frames, slots, owned, dq, res, stats2, out_cotangent, params, blocks, at, emb_pad, dw_att, counts
    )

    value0 = scatter_core(grid, keep0, send0)
    value1 = scatter_core(grid, keep1, send1)
    ready = after(e2, value0, value1)
    moved0 = send_z(grid, value0)
    moved1 = send_plane(grid, value1, 1)
    input_grad, part = input_backward(0, frames, ready, o2, inp, stats1, rgrad, params, blocks)
    sums1 = [part]
    moved = after_all(moved1 + moved0, part)
    moved1, moved0 = moved[: len(moved1)], moved[len(moved1) :]
    value1 = add_low(*moved1).astype(BF16)
    value1 = add_low(*send_plane(grid, value1, 0)).astype(BF16)
    moved1 = send_z(grid, value1)
    value0 = add_low(*after_all(moved0, value1)).astype(BF16)
    moved0 = send_plane(grid, value0, 1)
    ready = after(e2, value0)
    for clip in range(1, clip_count):
        input_grad, part = input_backward(
            clip, frames, ready, o2, inp, stats1, rgrad, params, blocks, input_grad
        )
        sums1.append(part)
    value0 = add_low(*after_all(moved0, part)).astype(BF16)
    grad0 = add_low(*send_plane(grid, value0, 0))
    grad1 = add_low(*after_all(moved1, part))
    full_grad = jnp.concatenate([grad0.reshape(k0, BS, BS), grad1.reshape(k - k0, BS, BS)])
    tiles = norm_grad_tiles(total_devices, obias, after(sums2, full_grad), sums1)
    tiles = lax.all_to_all(tiles, ("dp", "mp"), 0, 0, tiled=True)
    norm_grads = jnp.sum(tiles, axis=0)[:param_rows, :width]

    step, stats = owner_step(dp[None], full_grad, left_root, right_root, n_data, row_share)
    step = lax.all_to_all(step, "dp", 0, 0, tiled=True).reshape(padded, row_share, BS)
    near = jnp.concatenate(
        [step] + [grid.permute(step, lambda z, y, x, c, d=d: (z, y, x - d, c)) for d in range(1, grid.nx)]
    )
    far = grid.along_core(near)
    stats = lax.all_to_all(stats, "dp", 0, 0, tiled=True).reshape(padded, 3, row_share, BS)
    new_master, master_copy = update_master(where, master_blocks, near, far)
    owned_rows = stats[:slot_count, 0].astype(F32)
    new_left = 0.5 * left_stats + 0.5 * stats[:slot_count, 1].astype(F32)
    new_right = 0.5 * right_stats + 0.5 * stats[:slot_count, 2].astype(F32)
    small_rate = 0.5 / math.sqrt(clip_count * total_devices * POS)
    new_norm = norm_params - small_rate * norm_grads
    return (
        block_output, input_grad, owned_rows, new_left, new_right, new_master, master_copy,
        norm_grads, new_norm,
    )


def solution(mesh):
    cells = P(("dp", "mp"), None, None)
    rows = P("mp", "dp", None)
    in_specs = (
        cells, cells, cells, P(("dp", "mp"), None), P(("dp", "mp")), P(("dp", "mp")), cells,
        rows, P(None, ("dp", "mp")), P(), rows, rows, P("mp", None, None), P("mp", None, None),
    )
    out_specs = (
        cells, cells, rows, rows, rows, rows, rows, P(None, ("dp", "mp")), P(None, ("dp", "mp")),
    )
    return jax.shard_map(body, mesh=mesh, in_specs=in_specs, out_specs=out_specs, check_vma=False)
```

```python
import functools
import math

import jax
import jax.numpy as jnp
from jax import lax
from jax.experimental import pallas as pl
from jax.experimental.pallas import tpu as pltpu
from jax.sharding import PartitionSpec as P

LATENT_CHANNELS = 512
GROUPS = 32
HEADS = 8
HEADDIM = 64
CTX = 768
BINS = 8
TSTEPS = 1000
BS = 128
POS = 1024
CH = LATENT_CHANNELS

highest = lax.Precision.HIGHEST
learn_rate = 0.5
out_gain = 8.0
eps = 1e-05

CONV_SCALE = 1.0 / math.sqrt(9 * CH)
INV_WIDTH = 1.0 / math.sqrt(CH)
INV_CTX = 1.0 / math.sqrt(CTX)
OUT_SCALE = out_gain / math.sqrt(CH)
ATT_SCALE = 1.0 / math.sqrt(HEADDIM)

SQ = (CH // BS) * (CH // BS)
KV = (CTX // BS) * (CH // BS)
TEMB0 = 9 * SQ
QUERY0 = TEMB0 + SQ
OUT0 = QUERY0 + SQ
KEY0 = OUT0 + SQ
VALUE0 = KEY0 + KV
NBLK = VALUE0 + KV

F32 = jnp.float32
BF16 = jnp.bfloat16
VMEM_LIMIT = 60 * 1024 * 1024
SMALL = pl.CostEstimate(flops=1000000, bytes_accessed=1000000, transcendentals=0)


def nt(a, b):
    return lax.dot_general(a, b, (((1,), (1,)), ((), ())), preferred_element_type=F32)


def nn(a, b):
    return lax.dot_general(a, b, (((1,), (0,)), ((), ())), preferred_element_type=F32)


def mat(ref, base, nr, nc):
    rows = [jnp.concatenate([ref[base + a * nc + b] for b in range(nc)], axis=1) for a in range(nr)]
    return jnp.concatenate(rows, axis=0)


def row_iota(start, count):
    return lax.broadcasted_iota(jnp.int32, (count, 1), 0) + start


def fold8(x):
    return jnp.sum(x.reshape(-1, 8, x.shape[-1]), axis=0)


def group_sums(*partials):
    i = lax.broadcasted_iota(jnp.int32, (CH, CH), 0) // (CH // GROUPS)
    j = lax.broadcasted_iota(jnp.int32, (CH, CH), 1) // (CH // GROUPS)
    gmat = jnp.where(i == j, 1.0, 0.0).astype(BF16)
    row = lax.broadcasted_iota(jnp.int32, (16, CH), 0)
    stack = jnp.zeros((16, CH), F32)
    for k, rows8 in enumerate(partials):
        rest = jnp.sum(rows8, axis=0, keepdims=True)
        for t in range(3):
            term = rest.astype(BF16).astype(F32)
            stack = jnp.where(row == 3 * k + t, term, stack)
            rest = rest - term
    out = nn(stack.astype(BF16), gmat)
    sums = [out[3 * k : 3 * k + 1] + out[3 * k + 1 : 3 * k + 2] + out[3 * k + 2 : 3 * k + 3] for k in range(len(partials))]
    return sums[0] if len(sums) == 1 else sums


def shift_bins(tile, step):
    if step == 0:
        return tile
    t = tile.reshape(-1, 8, tile.shape[-1])
    rolled = pltpu.roll(t, (8 - step) % 8, 1)
    b = lax.broadcasted_iota(jnp.int32, (1, 8, 1), 1) + step
    keep = (b >= 0) & (b < 8)
    return jnp.where(keep, rolled, 0.0).reshape(tile.shape)


def write_windows(pad, e_ref, o_ref, sign, lead=0):
    T = 64

    def body(i, carry):
        r = pl.multiple_of(i * T, T)
        mid = pad[pl.ds(r + 8, T), :]
        low = pad[pl.ds(r, T), :]
        for d in range(3):
            step = sign * (d - 1)
            e_ref[lead, d, pl.ds(r, T), :] = shift_bins(mid, step).astype(BF16)
            o_ref[lead, d, pl.ds(r, T), :] = shift_bins(low, step).astype(BF16)
        return carry

    lax.fori_loop(0, POS // T, body, 0)
    last = pad[POS : POS + 16, :]
    for d in range(3):
        o_ref[lead, d, POS : POS + 16, :] = shift_bins(last, sign * (d - 1)).astype(BF16)


def window(e_ref, o_ref, df, db, r, n, lead=(0,)):
    if df == 1:
        return e_ref[lead + (db, pl.ds(r, n), slice(None))]
    off = 0 if df == 0 else 16
    return o_ref[lead + (db, pl.ds(pl.multiple_of(r + off, 16), n), slice(None))]


def pre_kernel(frames_s, trig_s, clean, noise, cot, inp, outlow, stats, obias):
    c = pl.program_id(0)
    rows = frames_s[c] * BINS
    cs, sn = trig_s[0, c], trig_s[1, c]
    T = 64
    zero = jnp.zeros((8, CH), F32)
    inv_n = 1.0 / (rows * (CH // GROUPS)).astype(F32)

    def first(i, carry):
        s0, s1 = carry
        r = pl.multiple_of(i * T, T)
        m = row_iota(r, T) < rows
        x = jnp.where(m, cs * clean[0, pl.ds(r, T), :] + sn * noise[0, pl.ds(r, T), :], 0.0)
        inp[0, pl.ds(r, T), :] = x
        g = jnp.where(m, cot[0, pl.ds(r, T), :], 0.0)
        outlow[0, pl.ds(r, T), :] = g.astype(BF16)
        return (s0 + fold8(x), s1 + fold8(g))

    s0, s1 = lax.fori_loop(0, POS // T, first, (zero, zero))
    mean = group_sums(s0) * inv_n

    def second(i, s):
        r = pl.multiple_of(i * T, T)
        m = row_iota(r, T) < rows
        d = jnp.where(m, inp[0, pl.ds(r, T), :] - mean, 0.0)
        return s + fold8(d * d)

    s2 = lax.fori_loop(0, POS // T, second, zero)
    rstd = lax.rsqrt(group_sums(s2) * inv_n + eps)
    stats[0] = jnp.concatenate([mean, rstd, jnp.zeros((6, CH), F32)], axis=0)
    obias[0] = s1


def pre(frames, trig, clean, noise, cot):
    n = clean.shape[0]
    big = pl.BlockSpec((1, POS, CH), lambda c, *_: (c, 0, 0))
    small = pl.BlockSpec((1, 8, CH), lambda c, *_: (c, 0, 0))
    return pl.pallas_call(
        pre_kernel,
        out_shape=(
            jax.ShapeDtypeStruct((n, POS, CH), F32),
            jax.ShapeDtypeStruct((n, POS, CH), BF16),
            jax.ShapeDtypeStruct((n, 8, CH), F32),
            jax.ShapeDtypeStruct((n, 8, CH), F32),
        ),
        grid_spec=pltpu.PrefetchScalarGridSpec(
            num_scalar_prefetch=2, grid=(n,), in_specs=[big, big, big], out_specs=[big, big, small, small]
        ),
        compiler_params=pltpu.CompilerParams(vmem_limit_bytes=VMEM_LIMIT),
        cost_estimate=SMALL,
        name="inputs_stats",
    )(frames, trig, clean, noise, cot)


def acts_kernel(frames_s, inp, stats, *refs):
    pieces, (e_ref, o_ref, params_ref, pad) = refs[:-4], refs[-4:]
    c = pl.program_id(0)
    rows = frames_s[c] * BINS
    T = 64
    total = None
    for piece in pieces:
        for j in range(piece.shape[0]):
            got = piece[j].astype(F32).reshape(CH // BS, 8, BS)
            total = got if total is None else total + got
    params = jnp.concatenate([total[j] for j in range(CH // BS)], axis=1)
    params_ref[...] = params
    mean, rstd = stats[0, 0:1], stats[0, 1:2]
    scale = rstd * params[0:1]
    shift = params[1:2]
    pad[0:8, :] = jnp.zeros((8, CH), F32)
    pad[8 + POS :, :] = jnp.zeros((8, CH), F32)

    def body(i, carry):
        r = pl.multiple_of(i * T, T)
        m = row_iota(r, T) < rows
        y = (inp[0, pl.ds(r, T), :] - mean) * scale + shift
        a = jnp.where(m, y * jax.nn.sigmoid(y), 0.0)
        pad[pl.ds(r + 8, T), :] = a
        return carry

    lax.fori_loop(0, POS // T, body, 0)
    write_windows(pad, e_ref, o_ref, 1)


def acts_windows(frames, inp, stats, pieces):
    n = inp.shape[0]
    row_share = pieces[0].shape[2]
    slots = CH // BS * 8 // row_share
    return pl.pallas_call(
        acts_kernel,
        out_shape=(
            jax.ShapeDtypeStruct((n, 3, POS, CH), BF16),
            jax.ShapeDtypeStruct((n, 3, POS + 16, CH), BF16),
            jax.ShapeDtypeStruct((8, CH), F32),
        ),
        grid_spec=pltpu.PrefetchScalarGridSpec(
            num_scalar_prefetch=1,
            grid=(n,),
            in_specs=[
                pl.BlockSpec((1, POS, CH), lambda c, *_: (c, 0, 0)),
                pl.BlockSpec((1, 8, CH), lambda c, *_: (c, 0, 0)),
            ]
            + [
                pl.BlockSpec((p.shape[0], slots, row_share, BS), lambda c, *_: (0, 0, 0, 0))
                for p in pieces
            ],
            out_specs=[
                pl.BlockSpec((1, 3, POS, CH), lambda c, *_: (c, 0, 0, 0)),
                pl.BlockSpec((1, 3, POS + 16, CH), lambda c, *_: (c, 0, 0, 0)),
                pl.BlockSpec((8, CH), lambda c, *_: (0, 0)),
            ],
            scratch_shapes=[pltpu.VMEM((POS + 16, CH), F32)],
        ),
        compiler_params=pltpu.CompilerParams(vmem_limit_bytes=VMEM_LIMIT),
        cost_estimate=SMALL,
        name="acts",
    )(frames, inp, stats, *pieces)


def conv_kernel(chunks, frames_s, dest_s, e_ref, o_ref, inp, emb, params, *refs):
    pieces, (res, normed, stats, w_out, w, sem, sem_out) = refs[: -7], refs[-7:]
    c = pl.program_id(0)
    per_chunk = len(pieces) // len(chunks)
    row_share = pieces[0].shape[2]

    @pl.when(c == 0)
    def _():
        copies = []
        for j, (skip, start, count) in enumerate(chunks):
            for a in range(per_chunk):
                ref = pieces[j * per_chunk + a]
                for p in range(ref.shape[0]):
                    i = a * ref.shape[0] + p
                    first = dest_s[0, i] + start
                    row = pl.multiple_of(dest_s[1, i], row_share)
                    copies.append(
                        pltpu.make_async_copy(
                            ref.at[p, pl.ds(skip, count)],
                            w.at[pl.ds(first, count), pl.ds(row, row_share), :],
                            sem.at[len(copies)],
                        )
                    )
        for copy in copies:
            copy.start()
        for copy in copies:
            copy.wait()
        pltpu.make_async_copy(w, w_out, sem_out).start()

    rows = frames_s[c] * BINS
    R = 256
    T = 64
    zero = jnp.zeros((8, CH), F32)
    inv_n = 1.0 / (rows * (CH // GROUPS)).astype(F32)
    temb = nn(emb[0], mat(w, TEMB0, 4, 4))[0:1] * INV_WIDTH
    add = temb + params[2:3]

    def tile(i, s):
        r = pl.multiple_of(i * R, R)
        acc = jnp.zeros((R, CH), F32)
        for t in range(9):
            df, db = divmod(t, 3)
            acc = acc + nn(window(e_ref, o_ref, df, db, r, R), mat(w, t * SQ, 4, 4))
        v = inp[0, pl.ds(r, R), :] + acc * CONV_SCALE + add
        res[0, pl.ds(r, R), :] = v
        return s + fold8(jnp.where(row_iota(r, R) < rows, v, 0.0))

    s = lax.fori_loop(0, POS // R, tile, zero)
    mean = group_sums(s) * inv_n

    def second(i, s):
        r = pl.multiple_of(i * T, T)
        d = jnp.where(row_iota(r, T) < rows, res[0, pl.ds(r, T), :] - mean, 0.0)
        return s + fold8(d * d)

    s2 = lax.fori_loop(0, POS // T, second, zero)
    rstd = lax.rsqrt(group_sums(s2) * inv_n + eps)
    scale = rstd * params[3:4]
    shift = params[4:5]

    def third(i, carry):
        r = pl.multiple_of(i * T, T)
        normed[0, pl.ds(r, T), :] = ((res[0, pl.ds(r, T), :] - mean) * scale + shift).astype(BF16)
        return carry

    lax.fori_loop(0, POS // T, third, 0)
    stats[0] = jnp.concatenate([mean, rstd, jnp.zeros((6, CH), F32)], axis=0)

    @pl.when(c == pl.num_programs(0) - 1)
    def _():
        pltpu.make_async_copy(w, w_out, sem_out).wait()


def whole(shape):
    return pl.BlockSpec(shape, lambda *_: (0,) * len(shape), pipeline_mode=pl.Buffered(1))


def per_clip(shape):
    return pl.BlockSpec((1,) + shape, lambda c, *_: (c,) + (0,) * len(shape))


def conv_forward(frames, dest, e, o, inp, emb, params, pieces, chunks):
    n = inp.shape[0]
    copies = sum(p.shape[0] for p in pieces)
    return pl.pallas_call(
        functools.partial(conv_kernel, chunks),
        out_shape=(
            jax.ShapeDtypeStruct((n, POS, CH), F32),
            jax.ShapeDtypeStruct((n, POS, CH), BF16),
            jax.ShapeDtypeStruct((n, 8, CH), F32),
            jax.ShapeDtypeStruct((NBLK, BS, BS), BF16),
        ),
        grid_spec=pltpu.PrefetchScalarGridSpec(
            num_scalar_prefetch=2,
            grid=(n,),
            in_specs=[
                per_clip((3, POS, CH)),
                per_clip((3, POS + 16, CH)),
                per_clip((POS, CH)),
                per_clip((16, CH)),
                whole((8, CH)),
            ]
            + [pl.BlockSpec(memory_space=pl.ANY)] * len(pieces),
            out_specs=[
                per_clip((POS, CH)),
                per_clip((POS, CH)),
                per_clip((8, CH)),
                pl.BlockSpec(memory_space=pl.ANY),
            ],
            scratch_shapes=[
                pltpu.VMEM((NBLK, BS, BS), BF16),
                pltpu.SemaphoreType.DMA((copies,)),
                pltpu.SemaphoreType.DMA(()),
            ],
        ),
        compiler_params=pltpu.CompilerParams(vmem_limit_bytes=VMEM_LIMIT),
        cost_estimate=pl.CostEstimate(
            flops=n * POS * CH * CH * 18, bytes_accessed=n * POS * CH * 22 + 5000000, transcendentals=0
        ),
        name="conv_forward",
    )(frames, dest, e, o, inp, emb, params, *pieces)


def attn_kernel(
    frames_s, normed, tokens, tok_t, kmask, outlow, res, params, w,
    block_out, dq_ref, dw_ref,
    q_s, do_s, qt_s, dot_s, mixed_s, dkt_s, dvt_s, dkv_acc, km_s, s_s, dp_s, pb_s, ds_s, odq_s, dw_s,
):
    c = pl.program_id(0)
    rows = frames_s[c] * BINS
    R = 256
    C = 32
    def project(i, carry):
        r = pl.multiple_of(i * R, R)
        q = (nn(normed[0, pl.ds(r, R), :], mat(w, SQ, 4, 4)) * INV_WIDTH).astype(BF16)
        q_s[pl.ds(r, R), :] = q
        qt_s[:, pl.ds(r, R)] = q.T
        d = (nt(outlow[0, pl.ds(r, R), :], mat(w, 2 * SQ, 4, 4)) * OUT_SCALE).astype(BF16)
        do_s[pl.ds(r, R), :] = d
        dot_s[:, pl.ds(r, R)] = d.T
        return carry

    lax.fori_loop(0, POS // R, project, 0)
    lane = lax.broadcasted_iota(jnp.int32, (1, BS), 1)
    first = lane < HEADDIM
    keys = ((nn(tokens[0], mat(w, 3 * SQ, CTX // BS, 4)) * INV_CTX).astype(BF16).astype(F32) * ATT_SCALE).astype(BF16)
    values = (nn(tokens[0], mat(w, 3 * SQ + KV, CTX // BS, 4)) * INV_CTX).astype(BF16)
    for slab in range(HEADS // 2):
        for j, side in enumerate((keys, values)):
            two = side[:, slab * BS : (slab + 1) * BS]
            none = jnp.zeros_like(two)
            km_s[slab, 2 * j] = jnp.where(first, two, none)
            km_s[slab, 2 * j + 1] = jnp.where(first, none, two)
    dkv_acc[...] = jnp.zeros_like(dkv_acc)
    pb_s[1] = jnp.zeros(pb_s.shape[1:], BF16)
    ds_s[1] = jnp.zeros(ds_s.shape[1:], BF16)
    valid = kmask[0, 0:1, :] > 0.0
    RA = s_s.shape[1]
    tiles = POS // RA
    steps = HEADS // 2 * tiles

    def place(i):
        slab = i // tiles
        return slab, pl.ds(pl.multiple_of(slab * BS, BS), BS), pl.ds(pl.multiple_of(i % tiles * RA, RA), RA)

    def scores(i, h):
        slab, cols, at = place(i)
        s_s[h] = nt(q_s[at, cols], km_s[slab, h])
        dp_s[h] = nt(do_s[at, cols], km_s[slab, 2 + h])

    def soften(h):
        for j in range(RA // C):
            part = slice(j * C, (j + 1) * C)
            s = jnp.where(valid, s_s[h, part, :], -1000000000.0)
            e = jnp.exp(s - jnp.max(s, axis=-1, keepdims=True))
            p = e * (1.0 / jnp.sum(e, axis=-1, keepdims=True))
            pb_s[h, part, :] = p.astype(BF16)
            dp = dp_s[h, part, :]
            delta = jnp.sum(p * dp, axis=-1, keepdims=True)
            ds_s[h, part, :] = (p * (dp - delta)).astype(BF16)

    def back(i, h):
        slab, cols, at = place(i)
        half = pl.ds(pl.multiple_of(slab * BS + h * HEADDIM, HEADDIM), HEADDIM)
        mine = slice(h * HEADDIM, (h + 1) * HEADDIM)
        pb, ds = pb_s[h], ds_s[h]
        dkv_acc[slab, 0, mine, :] += nn(qt_s[half, at], ds)
        dkv_acc[slab, 1, mine, :] += nn(dot_s[half, at], pb)
        o, dq = nn(pb, km_s[slab, 2 + h]), nn(ds, km_s[slab, h])
        if h == 0:
            odq_s[0] = o
            odq_s[1] = dq
        else:
            mixed_s[at, cols] = (odq_s[0] + o).astype(BF16)
            dq_ref[0, at, cols] = (odq_s[1] + dq).astype(BF16)

    scores(0, 0)

    def step(i, carry):
        back(jnp.maximum(i - 1, 0), 1)
        scores(i, 1)
        soften(0)
        back(i, 0)
        scores(jnp.minimum(i + 1, steps - 1), 0)
        soften(1)
        return carry

    odq_s[...] = jnp.zeros_like(odq_s)
    lax.fori_loop(0, steps, step, 0)
    back(steps - 1, 1)
    for slab in range(HEADS // 2):
        cols = slice(slab * BS, (slab + 1) * BS)
        dkt_s[cols, :] = (dkv_acc[slab, 0] * ATT_SCALE).astype(BF16)
        dvt_s[cols, :] = dkv_acc[slab, 1].astype(BF16)

    def project_out(i, carry):
        r = pl.multiple_of(i * R, R)
        proj = nn(mixed_s[pl.ds(r, R), :], mat(w, 2 * SQ, 4, 4)) * OUT_SCALE + params[5:6]
        m = row_iota(r, R) < rows
        block_out[0, pl.ds(r, R), :] = jnp.where(m, res[0, pl.ds(r, R), :] + proj, 0.0)
        return carry

    lax.fori_loop(0, POS // R, project_out, 0)

    @pl.when(c == 0)
    def _():
        dw_s[...] = jnp.zeros_like(dw_s)

    dw_s[0:CH, :] += nn(normed[0].T, dq_ref[0])
    dw_s[CH : 2 * CH, :] += nn(mixed_s[...].T, outlow[0])
    dw_s[2 * CH : 2 * CH + CTX, :] += nt(tok_t[0], dkt_s[...])
    dw_s[2 * CH + CTX :, :] += nt(tok_t[0], dvt_s[...])

    @pl.when(c == pl.num_programs(0) - 1)
    def _():
        def cut(i, carry):
            r = pl.multiple_of(i * BS, BS)
            scale = jnp.where(i < CH // BS, INV_WIDTH, jnp.where(i < 2 * CH // BS, OUT_SCALE, INV_CTX))
            low = (dw_s[pl.ds(r, BS), :] * scale).astype(BF16)
            for b in range(CH // BS):
                dw_ref[i * (CH // BS) + b] = low[:, b * BS : (b + 1) * BS]
            return carry

        lax.fori_loop(0, dw_s.shape[0] // BS, cut, 0)


def attention(frames, normed, tokens, tok_t, kmask, outlow, res, params, w):
    n = normed.shape[0]
    ctx_len = tokens.shape[1]
    amount = SQ + SQ + SQ + KV + KV
    return pl.pallas_call(
        attn_kernel,
        out_shape=(
            jax.ShapeDtypeStruct((n, POS, CH), F32),
            jax.ShapeDtypeStruct((n, POS, CH), BF16),
            jax.ShapeDtypeStruct((NBLK - QUERY0, BS, BS), BF16),
        ),
        grid_spec=pltpu.PrefetchScalarGridSpec(
            num_scalar_prefetch=1,
            grid=(n,),
            in_specs=[
                per_clip((POS, CH)),
                per_clip((ctx_len, CTX)),
                per_clip((CTX, ctx_len)),
                per_clip((8, ctx_len)),
                per_clip((POS, CH)),
                per_clip((POS, CH)),
                whole((8, CH)),
                pl.BlockSpec(
                    (pl.Element(amount), pl.Element(BS), pl.Element(BS)),
                    lambda *_: (TEMB0, 0, 0),
                    pipeline_mode=pl.Buffered(1),
                ),
            ],
            out_specs=[
                per_clip((POS, CH)),
                per_clip((POS, CH)),
                pl.BlockSpec((NBLK - QUERY0, BS, BS), lambda *_: (0, 0, 0)),
            ],
            scratch_shapes=[
                pltpu.VMEM((POS, CH), BF16),
                pltpu.VMEM((POS, CH), BF16),
                pltpu.VMEM((CH, POS), BF16),
                pltpu.VMEM((CH, POS), BF16),
                pltpu.VMEM((POS, CH), BF16),
                pltpu.VMEM((CH, ctx_len), BF16),
                pltpu.VMEM((CH, ctx_len), BF16),
                pltpu.VMEM((HEADS // 2, 2, BS, ctx_len), F32),
                pltpu.VMEM((HEADS // 2, 4, ctx_len, BS), BF16),
                pltpu.VMEM((2, 256, ctx_len), F32),
                pltpu.VMEM((2, 256, ctx_len), F32),
                pltpu.VMEM((2, 256, ctx_len), BF16),
                pltpu.VMEM((2, 256, ctx_len), BF16),
                pltpu.VMEM((2, 256, BS), F32),
                pltpu.VMEM((2 * CH + 2 * CTX, CH), F32),
            ],
        ),
        compiler_params=pltpu.CompilerParams(vmem_limit_bytes=VMEM_LIMIT),
        cost_estimate=pl.CostEstimate(
            flops=n * POS * CH * (6 * CH * 2 + 24 * ctx_len),
            bytes_accessed=n * POS * CH * 16,
            transcendentals=n * POS * HEADS * ctx_len,
        ),
        name="attention",
    )(frames, normed, tokens, tok_t, kmask, outlow, res, params, w)


def taps_kernel(
    counts, frames_s, slots_s, owned_s, dq_ref, res, stats, cot, params, w, at, emb, dw_att,
    rgrad, sums, e_out, o_out, *refs,
):
    outs, refs = refs[: len(counts)], refs[len(counts) :]
    ng_s, pad, e_ref, o_ref, blocks, sem, sem_w = refs
    n = e_ref.shape[0]
    step = pl.program_id(0)
    T = 64

    @pl.when(step == 0)
    def _():
        blocks[NBLK] = jnp.zeros((BS, BS), BF16)
        pltpu.make_async_copy(dw_att, blocks.at[pl.ds(QUERY0, NBLK - QUERY0)], sem.at[0]).start()

    @pl.when(step < n)
    def _():
        rows = frames_s[step] * BINS
        R = 256
        zero = jnp.zeros((8, CH), F32)
        inv_n = 1.0 / (rows * (CH // GROUPS)).astype(F32)
        mean, rstd = stats[0, 0:1], stats[0, 1:2]
        gain = params[3:4]

        def first(i, carry):
            s0, s1 = carry
            r = pl.multiple_of(i * R, R)
            ng = nt(dq_ref[0, pl.ds(r, R), :], mat(w, 0, 4, 4)) * INV_WIDTH
            m = row_iota(r, R) < rows
            ng = jnp.where(m, ng, 0.0)
            ng_s[pl.ds(r, R), :] = ng
            x = jnp.where(m, (res[0, pl.ds(r, R), :] - mean) * rstd, 0.0)
            return (s0 + fold8(ng), s1 + fold8(ng * x))

        s0, s1 = lax.fori_loop(0, POS // R, first, (zero, zero))
        mh, mhx = group_sums(s0 * gain, s1 * gain)
        scale, mh, mhx = rstd * gain, rstd * mh * inv_n, rstd * mhx * inv_n
        pad[0:8, :] = zero
        pad[8 + POS :, :] = zero

        def second(i, s):
            r = pl.multiple_of(i * T, T)
            m = row_iota(r, T) < rows
            x = (res[0, pl.ds(r, T), :] - mean) * rstd
            d = scale * ng_s[pl.ds(r, T), :] - mh - x * mhx
            g = jnp.where(m, cot[0, pl.ds(r, T), :] + d, 0.0)
            rgrad[0, pl.ds(r, T), :] = g
            pad[pl.ds(r + 8, T), :] = g
            return s + fold8(g)

        s2 = lax.fori_loop(0, POS // T, second, zero)
        sums[pl.ds(step, 1)] = jnp.concatenate([s2, s1, s0], axis=0)[None]
        write_windows(pad, e_ref, o_ref, -1, step)
        pltpu.make_async_copy(e_ref.at[step], e_out.at[step], sem_w.at[2 * step]).start()
        pltpu.make_async_copy(o_ref.at[step], o_out.at[step], sem_w.at[2 * step + 1]).start()

    def cut(value, first):
        low = value.astype(BF16)
        for a in range(4):
            for b in range(4):
                blocks[first + a * 4 + b] = low[a * BS : (a + 1) * BS, b * BS : (b + 1) * BS]

    @pl.when(step >= n)
    def _():
        d = step - n
        for df in range(3):
            acc = None
            for c in range(n):
                g = window(e_ref, o_ref, 2 - df, d, 0, POS, (c,))
                part = nn(at[:, c * POS : (c + 1) * POS], g)
                acc = part if acc is None else acc + part
            cut(acc * CONV_SCALE, (3 * df + d) * SQ)

    @pl.when(step == pl.num_programs(0) - 1)
    def _():
        rows = [jnp.sum(sums[c, 0:8], axis=0, keepdims=True) for c in range(n)]
        grad = jnp.concatenate(rows + [jnp.zeros((16 - n, CH), F32)], axis=0).astype(BF16)
        outer = lax.dot_general(emb[...], grad, (((0,), (0,)), ((), ())), preferred_element_type=F32)
        cut(outer * INV_WIDTH, TEMB0)
        pltpu.make_async_copy(dw_att, blocks.at[pl.ds(QUERY0, NBLK - QUERY0)], sem.at[0]).wait()
        start = sum(counts)
        for q in reversed(range(len(counts))):
            start -= counts[q]

            def send(i, carry, q=q, start=start):
                for u in range(8):
                    t = i * 8 + u
                    src = owned_s[slots_s[start + t]]
                    pltpu.make_async_copy(blocks.at[src], outs[q].at[t], sem.at[1 + q]).start()
                return carry

            lax.fori_loop(0, counts[q] // 8, send, 0)
        for c in range(n):
            pltpu.make_async_copy(e_ref.at[c], e_out.at[c], sem_w.at[2 * c]).wait()
            pltpu.make_async_copy(o_ref.at[c], o_out.at[c], sem_w.at[2 * c + 1]).wait()
        for q, out in enumerate(outs):
            pltpu.make_async_copy(out, out, sem.at[1 + q]).wait()


def tap_gradients(frames, slots, owned, dq, res, stats, cot, params, w, at, emb, dw_att, counts):
    n = dq.shape[0]

    def of_clip(shape):
        return pl.BlockSpec((1,) + shape, lambda i, *_: (jnp.minimum(i, n - 1),) + (0,) * len(shape))

    any_space = pl.BlockSpec(memory_space=pl.ANY)
    return pl.pallas_call(
        functools.partial(taps_kernel, counts),
        out_shape=(
            jax.ShapeDtypeStruct((n, POS, CH), F32),
            jax.ShapeDtypeStruct((n, 24, CH), F32),
            jax.ShapeDtypeStruct((n, 3, POS, CH), BF16),
            jax.ShapeDtypeStruct((n, 3, POS + 16, CH), BF16),
        )
        + tuple(jax.ShapeDtypeStruct((s, BS, BS), BF16) for s in counts),
        grid_spec=pltpu.PrefetchScalarGridSpec(
            num_scalar_prefetch=3,
            grid=(n + 3,),
            in_specs=[
                of_clip((POS, CH)),
                of_clip((POS, CH)),
                of_clip((8, CH)),
                of_clip((POS, CH)),
                whole((8, CH)),
                pl.BlockSpec((SQ, BS, BS), lambda *_: (QUERY0 // SQ, 0, 0), pipeline_mode=pl.Buffered(1)),
                whole((CH, n * POS)),
                whole((16, CH)),
                any_space,
            ],
            out_specs=[of_clip((POS, CH)), pl.BlockSpec((n, 24, CH), lambda *_: (0, 0, 0)), any_space, any_space]
            + [any_space] * len(counts),
            scratch_shapes=[
                pltpu.VMEM((POS, CH), F32),
                pltpu.VMEM((POS + 16, CH), F32),
                pltpu.VMEM((n, 3, POS, CH), BF16),
                pltpu.VMEM((n, 3, POS + 16, CH), BF16),
                pltpu.VMEM((NBLK + 1, BS, BS), BF16),
                pltpu.SemaphoreType.DMA((1 + len(counts),)),
                pltpu.SemaphoreType.DMA((2 * n,)),
            ],
        ),
        compiler_params=pltpu.CompilerParams(vmem_limit_bytes=VMEM_LIMIT),
        cost_estimate=pl.CostEstimate(
            flops=n * POS * CH * CH * 20, bytes_accessed=n * POS * CH * 30 + 20000000, transcendentals=0
        ),
        name="tap_gradients",
    )(frames, slots, owned, dq, res, stats, cot, params, w, at, emb, dw_att)


def transposed_conv(e_ref, o_ref, w, out):
    R = 256

    def conv(i, carry):
        r = pl.multiple_of(i * R, R)
        acc = jnp.zeros((R, CH), F32)
        for t in range(9):
            df, db = divmod(t, 3)
            acc = acc + nt(window(e_ref, o_ref, 2 - df, db, r, R), mat(w, t * SQ, 4, 4))
        out[pl.ds(r, R), :] = acc * CONV_SCALE
        return carry

    lax.fori_loop(0, POS // R, conv, 0)


def acts_grad_kernel(e_ref, o_ref, w, out):
    transposed_conv(e_ref, o_ref, w, out)


def acts_gradient(clip, e, o, w):
    def of_clip(shape):
        return pl.BlockSpec(
            (1,) + shape, lambda *_: (clip,) + (0,) * len(shape), pipeline_mode=pl.Buffered(1)
        )

    return pl.pallas_call(
        acts_grad_kernel,
        out_shape=jax.ShapeDtypeStruct((POS, CH), F32),
        grid=(1,),
        in_specs=[
            of_clip((3, POS, CH)),
            of_clip((3, POS + 16, CH)),
            pl.BlockSpec((TEMB0, BS, BS), lambda *_: (0, 0, 0), pipeline_mode=pl.Buffered(1)),
        ],
        out_specs=pl.BlockSpec((POS, CH), lambda *_: (0, 0)),
        compiler_params=pltpu.CompilerParams(vmem_limit_bytes=VMEM_LIMIT),
        cost_estimate=pl.CostEstimate(flops=POS * CH * CH * 18, bytes_accessed=POS * CH * 24, transcendentals=0),
        name="acts_gradient",
    )(e, o, w)


def input_kernel(clip, frames_s, ag, inp, stats, rgrad, params, *refs):
    out, sums, dy_s = refs[-3:]
    norm1_backward(clip, frames_s, ag, inp, stats, rgrad, params, out, sums, dy_s)


def clip_kernel(clip, frames_s, e_ref, o_ref, w, inp, stats, rgrad, params, *refs):
    out, sums, dy_s = refs[-3:]
    transposed_conv(e_ref, o_ref, w, dy_s)
    norm1_backward(clip, frames_s, dy_s, inp, stats, rgrad, params, out, sums, dy_s)


def norm1_backward(clip, frames_s, ag, inp, stats, rgrad, params, out, sums, dy_s):
    rows = frames_s[clip] * BINS
    T = 64
    zero = jnp.zeros((8, CH), F32)
    inv_n = 1.0 / (rows * (CH // GROUPS)).astype(F32)
    mean, rstd = stats[0, 0:1], stats[0, 1:2]
    gain, shift = params[0:1], params[1:2]

    def first(i, carry):
        s0, s1 = carry
        r = pl.multiple_of(i * T, T)
        m = row_iota(r, T) < rows
        x = (inp[0, pl.ds(r, T), :] - mean) * rstd
        y = x * gain + shift
        sg = jax.nn.sigmoid(y)
        dy = jnp.where(m, ag[pl.ds(r, T), :] * (sg * (1.0 + y * (1.0 - sg))), 0.0)
        dy_s[pl.ds(r, T), :] = dy
        return (s0 + fold8(dy), s1 + fold8(dy * x))

    s0, s1 = lax.fori_loop(0, POS // T, first, (zero, zero))
    mh, mhx = group_sums(s0 * gain, s1 * gain)
    scale, mh, mhx = rstd * gain, rstd * mh * inv_n, rstd * mhx * inv_n

    def second(i, carry):
        r = pl.multiple_of(i * T, T)
        m = row_iota(r, T) < rows
        x = (inp[0, pl.ds(r, T), :] - mean) * rstd
        d = scale * dy_s[pl.ds(r, T), :] - mh - x * mhx
        out[0, pl.ds(r, T), :] = jnp.where(m, rgrad[0, pl.ds(r, T), :] + d, 0.0)
        return carry

    lax.fori_loop(0, POS // T, second, 0)
    sums[0, 0:8] = s1
    sums[0, 8:16] = s0


def input_backward(clip, frames, ag, inp, stats, rgrad, params, before=None):
    n = inp.shape[0]

    def of_clip(shape):
        return pl.BlockSpec((1,) + shape, lambda *_: (clip,) + (0,) * len(shape))

    before = () if before is None else (before,)
    return pl.pallas_call(
        functools.partial(input_kernel, clip),
        out_shape=(
            jax.ShapeDtypeStruct((n, POS, CH), F32),
            jax.ShapeDtypeStruct((1, 16, CH), F32),
        ),
        grid_spec=pltpu.PrefetchScalarGridSpec(
            num_scalar_prefetch=1,
            grid=(1,),
            in_specs=[whole((POS, CH)), of_clip((POS, CH)), of_clip((8, CH)), of_clip((POS, CH)), whole((8, CH))]
            + [pl.BlockSpec(memory_space=pl.ANY)] * len(before),
            out_specs=[of_clip((POS, CH)), pl.BlockSpec((1, 16, CH), lambda *_: (0, 0, 0))],
            scratch_shapes=[pltpu.VMEM((POS, CH), F32)],
        ),
        input_output_aliases={6: 0} if before else {},
        compiler_params=pltpu.CompilerParams(vmem_limit_bytes=VMEM_LIMIT),
        cost_estimate=pl.CostEstimate(flops=POS * CH * 30, bytes_accessed=POS * CH * 20, transcendentals=POS * CH),
        name="input_backward",
    )(frames, ag, inp, stats, rgrad, params, *before)


def whole_backward(clip, frames, e, o, w, inp, stats, rgrad, params, before):
    n = inp.shape[0]

    def of_clip(shape, **mode):
        return pl.BlockSpec((1,) + shape, lambda *_: (clip,) + (0,) * len(shape), **mode)

    once = {"pipeline_mode": pl.Buffered(1)}
    return pl.pallas_call(
        functools.partial(clip_kernel, clip),
        out_shape=(
            jax.ShapeDtypeStruct((n, POS, CH), F32),
            jax.ShapeDtypeStruct((1, 16, CH), F32),
        ),
        grid_spec=pltpu.PrefetchScalarGridSpec(
            num_scalar_prefetch=1,
            grid=(1,),
            in_specs=[
                of_clip((3, POS, CH), **once),
                of_clip((3, POS + 16, CH), **once),
                pl.BlockSpec((TEMB0, BS, BS), lambda *_: (0, 0, 0), pipeline_mode=pl.Buffered(1)),
                of_clip((POS, CH)),
                of_clip((8, CH)),
                of_clip((POS, CH)),
                whole((8, CH)),
                pl.BlockSpec(memory_space=pl.ANY),
            ],
            out_specs=[of_clip((POS, CH)), pl.BlockSpec((1, 16, CH), lambda *_: (0, 0, 0))],
            scratch_shapes=[pltpu.VMEM((POS, CH), F32)],
        ),
        input_output_aliases={8: 0},
        compiler_params=pltpu.CompilerParams(vmem_limit_bytes=VMEM_LIMIT),
        cost_estimate=pl.CostEstimate(
            flops=POS * CH * CH * 18, bytes_accessed=POS * CH * 24, transcendentals=POS * CH
        ),
        name="whole_backward",
    )(frames, e, o, w, inp, stats, rgrad, params, before)


def norm_grads_kernel(me_s, obias, sums2, *refs):
    sums1, keep, send = refs[:-2], refs[-2], refs[-1]
    nx, n_data = keep.shape[0], keep.shape[1]
    width = CH // (2 * nx * n_data)
    total = lambda v: jnp.sum(v, axis=0, keepdims=True)
    first = sums1[0][0]
    for v in sums1[1:]:
        first = first + v[0]
    second, bias = sums2[0], obias[0]
    for i in range(1, sums2.shape[0]):
        second, bias = second + sums2[i], bias + obias[i]
    grads = jnp.concatenate(
        [
            total(first[0:8]), total(first[8:16]), total(second[0:8]), total(second[8:16]),
            total(second[16:24]), total(bias), jnp.zeros((2, CH), F32),
        ],
        axis=0,
    )
    lane = lax.broadcasted_iota(jnp.int32, (8, BS), 1)
    for x in range(nx):
        far = lax.rem(x - me_s[0] + nx, nx)
        for c in range(2):
            tiles = []
            for d in range(n_data):
                at = (d * 2 * nx + x * 2 + c) * width
                tile = grads[:, at // BS * BS : (at // BS + 1) * BS]
                tile = pltpu.roll(tile, (BS - at % BS) % BS, 1)
                tiles.append(jnp.where(lane < width, tile, 0.0)[None])
            tiles = jnp.concatenate(tiles, axis=0)

            @pl.when(me_s[1] == c)
            def _():
                keep[far] = tiles

            @pl.when(me_s[1] != c)
            def _():
                send[far] = tiles


def norm_grad_tiles(n_data, me, obias, sums2, sums1, n_model):
    vm = pl.BlockSpec(memory_space=pltpu.VMEM)
    shape = jax.ShapeDtypeStruct((n_model // 2, n_data, 8, BS), F32)
    return pl.pallas_call(
        norm_grads_kernel,
        out_shape=(shape, shape),
        in_specs=[pl.BlockSpec(memory_space=pltpu.SMEM)] + [vm] * (2 + len(sums1)),
        out_specs=[vm, vm],
        cost_estimate=SMALL,
        name="norm_grads",
    )(me, obias, sums2, *sums1)


def sinusoid(timesteps):
    half_width = CH // 2
    freqs = jnp.exp(-math.log(10000.0) * jnp.arange(half_width, dtype=F32) / half_width)
    angles = timesteps.astype(F32)[:, None] * freqs[None, :]
    return jnp.concatenate([jnp.sin(angles), jnp.cos(angles)], axis=-1)


def step_kernel(split, dp_s, *refs):
    first, second = refs[: split[0]], refs[split[0] : split[0] + split[1]]
    left_root, right_root, step, stats = refs[sum(split) :]
    k0, k1 = first[0].shape[0], second[0].shape[0]
    n_data, row_share = step.shape[0], step.shape[2]
    offset = dp_s[1]
    for i in range(k0 + k1):
        parts = [r[i] for r in first] if i < k0 else [r[i - k0] for r in second]
        g = add_low(*parts)
        low = g.astype(BF16)
        root = jnp.minimum(i + offset, left_root.shape[0] - 1)
        left = nt(low, low)
        right = lax.dot_general(low, low, (((0,), (0,)), ((), ())), preferred_element_type=F32)
        side = nn(left_root[root].astype(BF16), low)
        update = nn(side.astype(BF16), right_root[root].astype(BF16))
        rate = learn_rate * lax.rsqrt(jnp.sum(update * update, keepdims=True) * (1.0 / (BS * BS)) + 1e-06)
        step[:, i] = (update * rate).reshape(n_data, row_share, BS).astype(BF16)
        for j, value in enumerate((g, left, right)):
            stats[:, 3 * i + j] = value.reshape(n_data, row_share, BS).astype(BF16)
    for j in range(16 // row_share):
        stats[:, 3 * (k0 + k1) + j] = jnp.zeros((n_data, row_share, BS), BF16)


def owner_step(dp, first, second, left_root, right_root, row_share):
    first = [v.reshape(-1, BS, BS) for v in first]
    second = [v.reshape(-1, BS, BS) for v in second]
    k = first[0].shape[0] + second[0].shape[0]
    n_data = BS // row_share
    entries = 3 * k + 16 // row_share
    start = jnp.minimum(dp * k, left_root.shape[0] - k)
    where = jnp.concatenate([start, dp * k - start])
    root = pl.BlockSpec((pl.Element(k), pl.Element(BS), pl.Element(BS)), lambda i, w: (w[0], 0, 0))
    full = lambda shape: pl.BlockSpec(shape, lambda i, w: (0,) * len(shape))
    return pl.pallas_call(
        functools.partial(step_kernel, (len(first), len(second))),
        out_shape=(
            jax.ShapeDtypeStruct((n_data, k, row_share, BS), BF16),
            jax.ShapeDtypeStruct((n_data, entries, row_share, BS), BF16),
        ),
        grid_spec=pltpu.PrefetchScalarGridSpec(
            num_scalar_prefetch=1,
            grid=(1,),
            in_specs=[full(v.shape) for v in first + second] + [root, root],
            out_specs=[full((n_data, k, row_share, BS)), full((n_data, entries, row_share, BS))],
        ),
        cost_estimate=pl.CostEstimate(flops=k * 8 * BS**3, bytes_accessed=k * BS * BS * 20, transcendentals=0),
        name="owner_step",
    )(where, *first, *second, left_root, right_root)


def add_tiles_kernel(*refs):
    tiles, (_, stats, pair, sem) = refs[:-4], refs[-4:]
    tile = add_low(*[t[...] for t in tiles])
    high = tile.astype(BF16)
    both = jnp.concatenate([high, (tile - high.astype(F32)).astype(BF16)], axis=1)
    count, row_share = pair.shape[1], pair.shape[2]
    for j in range(count):
        pair[:, j] = both[:, j * row_share : (j + 1) * row_share]
    copy = pltpu.make_async_copy(pair, stats.at[:, pl.ds(stats.shape[1] - count, count)], sem)
    copy.start()
    copy.wait()


def add_tiles(tiles, stats):
    vm = pl.BlockSpec(memory_space=pltpu.VMEM)
    any_space = pl.BlockSpec(memory_space=pl.ANY)
    n_data, _, row_share, _ = stats.shape
    return pl.pallas_call(
        add_tiles_kernel,
        out_shape=jax.ShapeDtypeStruct(stats.shape, BF16),
        in_specs=[vm] * len(tiles) + [any_space],
        out_specs=any_space,
        scratch_shapes=[pltpu.VMEM((n_data, 16 // row_share, row_share, BS), BF16), pltpu.SemaphoreType.DMA(())],
        input_output_aliases={len(tiles): 0},
        cost_estimate=SMALL,
        name="add_tiles",
    )(*tiles, stats)


def master_kernel(where_s, master, near, far, new, low, steps):
    half = near.shape[0]
    steps[0:half] = near[...].astype(F32)
    steps[half:] = far[...].astype(F32)

    def one(j, carry):
        value = master[j] - steps[where_s[j]]
        new[j] = value
        low[j] = value.astype(BF16)
        return carry

    lax.fori_loop(0, master.shape[0], one, 0)


def update_master(where, master, near, far):
    vm = pl.BlockSpec(memory_space=pltpu.VMEM)
    return pl.pallas_call(
        master_kernel,
        out_shape=(
            jax.ShapeDtypeStruct(master.shape, F32),
            jax.ShapeDtypeStruct(master.shape, BF16),
        ),
        in_specs=[pl.BlockSpec(memory_space=pltpu.SMEM), vm, vm, vm],
        out_specs=[vm, vm],
        scratch_shapes=[pltpu.VMEM((2 * near.shape[0],) + near.shape[1:], F32)],
        cost_estimate=pl.CostEstimate(flops=300000, bytes_accessed=3000000, transcendentals=0),
        name="update_master",
    )(where, master, near, far)


class Grid:
    def __init__(self, n_data, n_model):
        self.nd, self.nm = n_data, n_model
        self.nx = n_model // 2
        self.ny = 1
        while self.ny * self.ny * 4 <= n_data:
            self.ny *= 2
        self.nz = n_data // self.ny
        self.split = self.nx == self.ny
        self.sizes = (self.ny, self.ny) if self.split else (self.ny, self.nx)
        dp, mp = lax.axis_index("dp"), lax.axis_index("mp")
        self.z, self.y, self.x, self.c = dp // self.ny, dp % self.ny, mp // 2, mp % 2

    def permute(self, value, fn):
        pairs = []
        for src in range(self.nd * self.nm):
            dp, mp = divmod(src, self.nm)
            z, y, x, c = fn(dp // self.ny, dp % self.ny, mp // 2, mp % 2)
            dst = ((z % self.nz) * self.ny + y % self.ny) * self.nm + (x % self.nx) * 2 + c % 2
            pairs.append((src, dst))
        return lax.ppermute(value, ("dp", "mp"), pairs)

    def along_z(self, value, d):
        return self.permute(value, lambda z, y, x, c: (z + d, y, x, c))

    def along_plane(self, value, stage, d):
        def fn(z, y, x, c):
            on_y = (stage == 0) != (self.split and c == 1)
            return (z, y + d, x, c) if on_y else (z, y, x + d, c)

        return self.permute(value, fn)

    def along_core(self, value):
        return self.permute(value, lambda z, y, x, c: (z, y, x, c + 1))

    def place(self, core, d0, d1, dz):
        swap = (core == 1) if self.split else jnp.zeros_like(core == 1)
        dy, dx = jnp.where(swap, d1, d0), jnp.where(swap, d0, d1)
        zz, yy, xx = (self.z + dz) % self.nz, (self.y + dy) % self.ny, (self.x + dx) % self.nx
        return zz * self.ny + yy, xx * 2 + core


def after(value, *others):
    return lax.optimization_barrier((value,) + others)[0]


def after_all(values, *others):
    return list(lax.optimization_barrier(tuple(values) + others)[: len(values)])


def gather_z(grid, shard):
    return [shard] + [grid.along_z(shard, -d) for d in range(1, grid.nz)]


def gather_plane(grid, stack, stage):
    return [stack] + [grid.along_plane(stack, stage, -d) for d in range(1, grid.sizes[stage])]


def gather_core(grid, got):
    return got + [grid.along_core(v) for v in got]


def gather_places(grid):
    dps, mps = [], []
    for rel in range(2):
        core = (grid.c + rel) % 2
        for d1 in range(grid.sizes[1]):
            for d0 in range(grid.sizes[0]):
                for dz in range(grid.nz):
                    dp, mp = grid.place(core, d0, d1, dz)
                    dps.append(dp)
                    mps.append(mp)
    return jnp.stack(dps), jnp.stack(mps)


def add_low(*parts):
    total = parts[0].astype(F32)
    for p in parts[1:]:
        total = total + p.astype(F32)
    return total


def scatter_core(grid, keep, send):
    return add_low(keep, grid.along_core(send)).astype(BF16)


def send_plane(grid, value, stage):
    value = value.reshape(grid.sizes[stage], -1, BS, BS)
    return [value[0]] + [grid.along_plane(value[d], stage, d) for d in range(1, value.shape[0])]


def send_z(grid, value):
    value = value.reshape(grid.nz, -1, BS, BS)
    return [value[0]] + [grid.along_z(value[d], d) for d in range(1, value.shape[0])]


def body(
    clean_latent, noise_latent, codec_tokens, codec_mask, frames, timesteps, out_cotangent,
    master_blocks, norm_params, owned_block, left_stats, right_stats, left_root, right_root,
):
    n_data = lax.axis_size("dp")
    n_model = lax.axis_size("mp")
    total_devices = n_data * n_model
    clip_count = clean_latent.shape[0]
    ctx_len = codec_tokens.shape[1]
    slot_count, row_share = (master_blocks.shape[0], master_blocks.shape[1])
    param_rows, width = norm_params.shape
    grid = Grid(n_data, n_model)
    dp, mp = lax.axis_index("dp"), lax.axis_index("mp")
    me = dp * n_model + mp

    own_params = lax.dynamic_update_slice(
        jnp.zeros((8, CH), BF16), norm_params.astype(BF16), (0, me * width)
    )
    param_tiles = own_params.reshape(8, CH // BS, BS).transpose(1, 0, 2).reshape(-1, row_share, BS)
    skip = param_tiles.shape[0]
    master_low = master_blocks.astype(BF16)
    cut = slot_count * 3 // 10
    chunks = ((skip, 0, cut), (0, cut, slot_count - cut))
    ring0 = gather_z(grid, jnp.concatenate([param_tiles, master_low[:cut]]))
    ring1 = gather_z(grid, master_low[cut:])
    place_dp, place_mp = gather_places(grid)
    dest = jnp.stack([place_mp * slot_count, place_dp * row_share])

    phases = timesteps.astype(F32) * (0.5 * math.pi / TSTEPS)
    trig = jnp.stack([jnp.cos(phases), jnp.sin(phases)])
    embedding = jax.nn.silu(sinusoid(timesteps)).astype(BF16)
    emb_rows = jnp.broadcast_to(embedding[:, None, :], (clip_count, 16, CH))
    emb_pad = jnp.pad(embedding, ((0, 16 - clip_count), (0, 0)))
    kmask = jnp.broadcast_to(codec_mask.astype(F32)[:, None, :], (clip_count, 8, ctx_len))
    tok_t = codec_tokens.transpose(0, 2, 1)

    k = slot_count // n_data + 1
    padded = n_data * k
    k0 = max(1, k // 8)

    planes = grid.sizes[0] * grid.sizes[1]
    half = n_model * padded // 2
    counts, slot_list = [], []
    for rel in range(2):
        core = (grid.c + rel) % 2
        for part, kk in ((0, k0), (1, k - k0)):
            t = jnp.arange(half // k * kk, dtype=jnp.int32)
            group, k_id = t // kk, t % kk + part * k0
            if part == 1:
                plane, dz = group // grid.nz, group % grid.nz
            else:
                plane, dz = group % planes, group // planes
            to_dp, to_mp = grid.place(core, plane % grid.sizes[0], plane // grid.sizes[0], dz)
            to_slot = to_dp * k + k_id
            slot_list.append(jnp.where(to_slot < slot_count, to_mp * slot_count + to_slot, NBLK))
            counts.append(half // k * kk)
    slots = jnp.concatenate(slot_list)
    owned = jnp.concatenate([owned_block, jnp.full((1,), NBLK, jnp.int32)])
    counts = tuple(counts)
    block_ids = jnp.arange(NBLK, dtype=jnp.int32)
    slot_of_block = jnp.sum(
        jnp.where(owned_block[None, :] == block_ids[:, None], block_ids[None, :], 0), axis=1
    )
    my_slots = lax.dynamic_slice_in_dim(slot_of_block, mp * slot_count, slot_count)
    from_mp = my_slots // slot_count
    where = (
        ((from_mp + grid.c) % 2 * grid.nx + (from_mp // 2 - grid.x) % grid.nx) * padded + my_slots % slot_count
    )

    stack0 = jnp.stack(ring0)
    got0 = jnp.concatenate(gather_plane(grid, stack0, 0))
    stack1 = jnp.stack(after_all(ring1, got0))
    got0 = gather_plane(grid, got0, 1)
    pieces = gather_core(grid, got0)
    got1 = jnp.concatenate(gather_plane(grid, stack1, 0))
    inp, outlow, stats1, obias = pre(after(frames, stack1), trig, clean_latent, noise_latent, out_cotangent)
    got1 = after(got1, stats1, *got0[1:])
    ready = after(frames, slots, owned, where, dest, kmask, emb_rows, emb_pad, tok_t)
    e1, o1, params = acts_windows(ready, inp, stats1, pieces)
    at = e1[:, 1].reshape(-1, CH).T
    got1 = gather_plane(grid, got1, 1)
    got1 = [got1[0]] + [after(v, e1) for v in got1[1:]]
    later = gather_core(grid, got1)
    e1 = after(e1, at)
    res, normed, stats2, blocks = conv_forward(
        frames, dest, e1, o1, inp, emb_rows, params, pieces + later, chunks
    )
    block_output, dq, dw_att = attention(
        frames, normed, codec_tokens, tok_t, kmask, outlow, res, params, blocks
    )
    rgrad, sums2, e2, o2, keep0, keep1, send0, send1 = tap_gradients(
        frames, slots, owned, dq, res, stats2, out_cotangent, params, blocks, at, emb_pad, dw_att, counts
    )

    value0 = scatter_core(grid, keep0, send0)
    value1 = scatter_core(grid, keep1, send1)
    ready = after(e2, value0, value1)
    moved0 = send_z(grid, value0)
    moved1 = send_plane(grid, value1, 1)
    ag = acts_gradient(0, ready, o2, blocks)
    moved = after_all(moved1 + moved0, ag)
    moved1, moved0 = moved[: len(moved1)], moved[len(moved1) :]
    value1 = add_low(*moved1).astype(BF16)
    moved1 = send_plane(grid, value1, 0)
    value0 = add_low(*moved0).astype(BF16)
    moved0 = send_plane(grid, value0, 1)
    input_grad, part = input_backward(0, after(frames, value1, value0), ag, inp, stats1, rgrad, params)
    sums1 = [part]
    moved = after_all(moved1 + moved0, part)
    moved1, moved0 = moved[: len(moved1)], moved[len(moved1) :]
    value1 = add_low(*moved1).astype(BF16)
    moved1 = send_z(grid, value1)
    value0 = add_low(*moved0).astype(BF16)
    moved0 = send_plane(grid, value0, 0)
    ready = after(e2, value1, value0)
    for clip in range(1, clip_count):
        input_grad, part = whole_backward(
            clip, frames, ready, o2, blocks, inp, stats1, rgrad, params, input_grad
        )
        sums1.append(part)
    moved = after_all(moved1 + moved0, part)
    moved1, moved0 = moved[: len(moved1)], moved[len(moved1) :]
    tiles, tiles_sent = norm_grad_tiles(
        n_data, jnp.stack([grid.x, grid.c]), after(obias, *moved1), sums2, sums1, n_model
    )
    step, stats = owner_step(dp[None], moved0, moved1, left_root, right_root, row_share)
    tiles = tiles + after(grid.along_core(tiles_sent), step)
    tiles = [tiles[0]] + [
        grid.permute(tiles[d], lambda z, y, x, c, d=d: (z, y, x + d, c)) for d in range(1, grid.nx)
    ]
    step = lax.all_to_all(step, "dp", 0, 0, tiled=True).reshape(padded, row_share, BS)
    stats = add_tiles(after_all(tiles, step), stats)
    near = jnp.concatenate(
        [step] + [grid.permute(step, lambda z, y, x, c, d=d: (z, y, x - d, c)) for d in range(1, grid.nx)]
    )
    far = grid.along_core(near)
    stats = lax.all_to_all(stats, "dp", 0, 0, tiled=True)
    tiles = jnp.sum(stats[:, 3 * k :].astype(F32), axis=0).reshape(16, BS)
    norm_grads = (tiles[0:8] + tiles[8:16])[:param_rows, :width]
    stats = stats[:, : 3 * k].reshape(padded, 3, row_share, BS)
    new_master, master_copy = update_master(where, master_blocks, near, far)
    owned_rows = stats[:slot_count, 0].astype(F32)
    new_left = 0.5 * left_stats + 0.5 * stats[:slot_count, 1].astype(F32)
    new_right = 0.5 * right_stats + 0.5 * stats[:slot_count, 2].astype(F32)
    small_rate = 0.5 / math.sqrt(clip_count * total_devices * POS)
    new_norm = norm_params - small_rate * norm_grads
    return (
        block_output, input_grad, owned_rows, new_left, new_right, new_master, master_copy,
        norm_grads, new_norm,
    )


def solution(mesh):
    cells = P(("dp", "mp"), None, None)
    rows = P("mp", "dp", None)
    in_specs = (
        cells, cells, cells, P(("dp", "mp"), None), P(("dp", "mp")), P(("dp", "mp")), cells,
        rows, P(None, ("dp", "mp")), P(), rows, rows, P("mp", None, None), P("mp", None, None),
    )
    out_specs = (
        cells, cells, rows, rows, rows, rows, rows, P(None, ("dp", "mp")), P(None, ("dp", "mp")),
    )
    return jax.shard_map(body, mesh=mesh, in_specs=in_specs, out_specs=out_specs, check_vma=False)
```

```python
import functools
import math

import jax
import jax.numpy as jnp
from jax import lax
from jax.experimental import pallas as pl
from jax.experimental.pallas import tpu as pltpu
from jax.sharding import PartitionSpec as P

LATENT_CHANNELS = 512
GROUPS = 32
HEADS = 8
HEADDIM = 64
CTX = 768
BINS = 8
TSTEPS = 1000
BS = 128
POS = 1024
CH = LATENT_CHANNELS

highest = lax.Precision.HIGHEST
learn_rate = 0.5
out_gain = 8.0
eps = 1e-05

CONV_SCALE = 1.0 / math.sqrt(9 * CH)
INV_WIDTH = 1.0 / math.sqrt(CH)
INV_CTX = 1.0 / math.sqrt(CTX)
OUT_SCALE = out_gain / math.sqrt(CH)
ATT_SCALE = 1.0 / math.sqrt(HEADDIM)

SQ = (CH // BS) * (CH // BS)
KV = (CTX // BS) * (CH // BS)
TEMB0 = 9 * SQ
QUERY0 = TEMB0 + SQ
OUT0 = QUERY0 + SQ
KEY0 = OUT0 + SQ
VALUE0 = KEY0 + KV
NBLK = VALUE0 + KV

F32 = jnp.float32
BF16 = jnp.bfloat16
VMEM_LIMIT = 60 * 1024 * 1024
SMALL = pl.CostEstimate(flops=1000000, bytes_accessed=1000000, transcendentals=0)


def nt(a, b):
    return lax.dot_general(a, b, (((1,), (1,)), ((), ())), preferred_element_type=F32)


def nn(a, b):
    return lax.dot_general(a, b, (((1,), (0,)), ((), ())), preferred_element_type=F32)


def mat(ref, base, nr, nc):
    rows = [jnp.concatenate([ref[base + a * nc + b] for b in range(nc)], axis=1) for a in range(nr)]
    return jnp.concatenate(rows, axis=0)


def row_iota(start, count):
    return lax.broadcasted_iota(jnp.int32, (count, 1), 0) + start


def fold8(x):
    return jnp.sum(x.reshape(-1, 8, x.shape[-1]), axis=0)


def group_sums(*partials):
    i = lax.broadcasted_iota(jnp.int32, (CH, CH), 0) // (CH // GROUPS)
    j = lax.broadcasted_iota(jnp.int32, (CH, CH), 1) // (CH // GROUPS)
    gmat = jnp.where(i == j, 1.0, 0.0).astype(BF16)
    row = lax.broadcasted_iota(jnp.int32, (16, CH), 0)
    stack = jnp.zeros((16, CH), F32)
    for k, rows8 in enumerate(partials):
        rest = jnp.sum(rows8, axis=0, keepdims=True)
        for t in range(3):
            term = rest.astype(BF16).astype(F32)
            stack = jnp.where(row == 3 * k + t, term, stack)
            rest = rest - term
    out = nn(stack.astype(BF16), gmat)
    sums = [out[3 * k : 3 * k + 1] + out[3 * k + 1 : 3 * k + 2] + out[3 * k + 2 : 3 * k + 3] for k in range(len(partials))]
    return sums[0] if len(sums) == 1 else sums


def shift_bins(tile, step):
    if step == 0:
        return tile
    t = tile.reshape(-1, 8, tile.shape[-1])
    rolled = pltpu.roll(t, (8 - step) % 8, 1)
    b = lax.broadcasted_iota(jnp.int32, (1, 8, 1), 1) + step
    keep = (b >= 0) & (b < 8)
    return jnp.where(keep, rolled, 0.0).reshape(tile.shape)


def write_windows(pad, e_ref, o_ref, sign, lead=0):
    T = 64

    def body(i, carry):
        r = pl.multiple_of(i * T, T)
        mid = pad[pl.ds(r + 8, T), :]
        low = pad[pl.ds(r, T), :]
        for d in range(3):
            step = sign * (d - 1)
            e_ref[lead, d, pl.ds(r, T), :] = shift_bins(mid, step).astype(BF16)
            o_ref[lead, d, pl.ds(r, T), :] = shift_bins(low, step).astype(BF16)
        return carry

    lax.fori_loop(0, POS // T, body, 0)
    last = pad[POS : POS + 16, :]
    for d in range(3):
        o_ref[lead, d, POS : POS + 16, :] = shift_bins(last, sign * (d - 1)).astype(BF16)


def window(e_ref, o_ref, df, db, r, n, lead=(0,)):
    if df == 1:
        return e_ref[lead + (db, pl.ds(r, n), slice(None))]
    off = 0 if df == 0 else 16
    return o_ref[lead + (db, pl.ds(pl.multiple_of(r + off, 16), n), slice(None))]


def pre_kernel(frames_s, trig_s, clean, noise, cot, inp, outlow, stats, obias):
    c = pl.program_id(0)
    rows = frames_s[c] * BINS
    cs, sn = trig_s[0, c], trig_s[1, c]
    T = 64
    zero = jnp.zeros((8, CH), F32)
    inv_n = 1.0 / (rows * (CH // GROUPS)).astype(F32)

    def first(i, carry):
        s0, s1 = carry
        r = pl.multiple_of(i * T, T)
        m = row_iota(r, T) < rows
        x = jnp.where(m, cs * clean[0, pl.ds(r, T), :] + sn * noise[0, pl.ds(r, T), :], 0.0)
        inp[0, pl.ds(r, T), :] = x
        g = jnp.where(m, cot[0, pl.ds(r, T), :], 0.0)
        outlow[0, pl.ds(r, T), :] = g.astype(BF16)
        return (s0 + fold8(x), s1 + fold8(g))

    s0, s1 = lax.fori_loop(0, POS // T, first, (zero, zero))
    mean = group_sums(s0) * inv_n

    def second(i, s):
        r = pl.multiple_of(i * T, T)
        m = row_iota(r, T) < rows
        d = jnp.where(m, inp[0, pl.ds(r, T), :] - mean, 0.0)
        return s + fold8(d * d)

    s2 = lax.fori_loop(0, POS // T, second, zero)
    rstd = lax.rsqrt(group_sums(s2) * inv_n + eps)
    stats[0] = jnp.concatenate([mean, rstd, jnp.zeros((6, CH), F32)], axis=0)
    obias[0] = s1


def pre(frames, trig, clean, noise, cot):
    n = clean.shape[0]
    big = pl.BlockSpec((1, POS, CH), lambda c, *_: (c, 0, 0))
    small = pl.BlockSpec((1, 8, CH), lambda c, *_: (c, 0, 0))
    return pl.pallas_call(
        pre_kernel,
        out_shape=(
            jax.ShapeDtypeStruct((n, POS, CH), F32),
            jax.ShapeDtypeStruct((n, POS, CH), BF16),
            jax.ShapeDtypeStruct((n, 8, CH), F32),
            jax.ShapeDtypeStruct((n, 8, CH), F32),
        ),
        grid_spec=pltpu.PrefetchScalarGridSpec(
            num_scalar_prefetch=2, grid=(n,), in_specs=[big, big, big], out_specs=[big, big, small, small]
        ),
        compiler_params=pltpu.CompilerParams(vmem_limit_bytes=VMEM_LIMIT),
        cost_estimate=SMALL,
        name="inputs_stats",
    )(frames, trig, clean, noise, cot)


def acts_kernel(frames_s, inp, stats, *refs):
    pieces, (e_ref, o_ref, params_ref, pad) = refs[:-4], refs[-4:]
    c = pl.program_id(0)
    rows = frames_s[c] * BINS
    T = 64
    total = None
    for piece in pieces:
        for j in range(piece.shape[0]):
            got = piece[j].astype(F32).reshape(CH // BS, 8, BS)
            total = got if total is None else total + got
    params = jnp.concatenate([total[j] for j in range(CH // BS)], axis=1)
    params_ref[...] = params
    mean, rstd = stats[0, 0:1], stats[0, 1:2]
    scale = rstd * params[0:1]
    shift = params[1:2]
    pad[0:8, :] = jnp.zeros((8, CH), F32)
    pad[8 + POS :, :] = jnp.zeros((8, CH), F32)

    def body(i, carry):
        r = pl.multiple_of(i * T, T)
        m = row_iota(r, T) < rows
        y = (inp[0, pl.ds(r, T), :] - mean) * scale + shift
        a = jnp.where(m, y * jax.nn.sigmoid(y), 0.0)
        pad[pl.ds(r + 8, T), :] = a
        return carry

    lax.fori_loop(0, POS // T, body, 0)
    write_windows(pad, e_ref, o_ref, 1)


def acts_windows(frames, inp, stats, pieces):
    n = inp.shape[0]
    row_share = pieces[0].shape[2]
    slots = CH // BS * 8 // row_share
    return pl.pallas_call(
        acts_kernel,
        out_shape=(
            jax.ShapeDtypeStruct((n, 3, POS, CH), BF16),
            jax.ShapeDtypeStruct((n, 3, POS + 16, CH), BF16),
            jax.ShapeDtypeStruct((8, CH), F32),
        ),
        grid_spec=pltpu.PrefetchScalarGridSpec(
            num_scalar_prefetch=1,
            grid=(n,),
            in_specs=[
                pl.BlockSpec((1, POS, CH), lambda c, *_: (c, 0, 0)),
                pl.BlockSpec((1, 8, CH), lambda c, *_: (c, 0, 0)),
            ]
            + [
                pl.BlockSpec((p.shape[0], slots, row_share, BS), lambda c, *_: (0, 0, 0, 0))
                for p in pieces
            ],
            out_specs=[
                pl.BlockSpec((1, 3, POS, CH), lambda c, *_: (c, 0, 0, 0)),
                pl.BlockSpec((1, 3, POS + 16, CH), lambda c, *_: (c, 0, 0, 0)),
                pl.BlockSpec((8, CH), lambda c, *_: (0, 0)),
            ],
            scratch_shapes=[pltpu.VMEM((POS + 16, CH), F32)],
        ),
        compiler_params=pltpu.CompilerParams(vmem_limit_bytes=VMEM_LIMIT),
        cost_estimate=SMALL,
        name="acts",
    )(frames, inp, stats, *pieces)


def conv_kernel(chunks, frames_s, dest_s, e_hbm, o_hbm, inp_hbm, emb, params, *refs):
    pieces, (res, normed, stats, w_out, w, e_ref, o_ref, inp, sem, sem_in, sem_out) = refs[:-11], refs[-11:]
    c = pl.program_id(0)
    n = e_ref.shape[0]
    per_chunk = len(pieces) // len(chunks)
    row_share = pieces[0].shape[2]
    copies = []
    for j, (skip, start, count) in enumerate(chunks):
        for a in range(per_chunk):
            ref = pieces[j * per_chunk + a]
            for p in range(ref.shape[0]):
                i = a * ref.shape[0] + p
                row = pl.multiple_of(dest_s[1, i], row_share)
                where = w.at[pl.ds(dest_s[0, i] + start, count), pl.ds(row, row_share), :]
                copies.append((i, pltpu.make_async_copy(ref.at[p, pl.ds(skip, count)], where, sem.at[len(copies)])))
    clips = [
        [
            pltpu.make_async_copy(src.at[k], dst.at[k], sem_in.at[3 * k + j])
            for j, (src, dst) in enumerate(((e_hbm, e_ref), (o_hbm, o_ref), (inp_hbm, inp)))
        ]
        for k in range(n)
    ]

    def weights(now, act):
        for i, copy in copies:
            pl.when((dest_s[0, i] < QUERY0) == now)(functools.partial(act, copy))

    @pl.when(c == 0)
    def _():
        weights(True, lambda copy: copy.start())
        for copy in clips[0]:
            copy.start()
        weights(False, lambda copy: copy.start())
        for k in range(1, n):
            for copy in clips[k]:
                copy.start()
        weights(True, lambda copy: copy.wait())

    for k in range(n):
        @pl.when(c == k)
        def _(k=k):
            for copy in clips[k]:
                copy.wait()

    rows = frames_s[c] * BINS
    R = 512
    T = 64
    zero = jnp.zeros((8, CH), F32)
    inv_n = 1.0 / (rows * (CH // GROUPS)).astype(F32)
    temb = nn(emb[0], mat(w, TEMB0, 4, 4))[0:1] * INV_WIDTH
    add = temb + params[2:3]

    def tile(i, s):
        r = pl.multiple_of(i * R, R)
        acc = jnp.zeros((R, CH), F32)
        for t in range(9):
            df, db = divmod(t, 3)
            acc = acc + nn(window(e_ref, o_ref, df, db, r, R, (c,)), mat(w, t * SQ, 4, 4))
        v = inp[c, pl.ds(r, R), :] + acc * CONV_SCALE + add
        res[0, pl.ds(r, R), :] = v
        return s + fold8(jnp.where(row_iota(r, R) < rows, v, 0.0))

    s = lax.fori_loop(0, POS // R, tile, zero)

    @pl.when(c == 0)
    def _():
        weights(False, lambda copy: copy.wait())
        pltpu.make_async_copy(w, w_out, sem_out).start()

    mean = group_sums(s) * inv_n

    def second(i, s):
        r = pl.multiple_of(i * T, T)
        d = jnp.where(row_iota(r, T) < rows, res[0, pl.ds(r, T), :] - mean, 0.0)
        return s + fold8(d * d)

    s2 = lax.fori_loop(0, POS // T, second, zero)
    rstd = lax.rsqrt(group_sums(s2) * inv_n + eps)
    scale = rstd * params[3:4]
    shift = params[4:5]

    def third(i, carry):
        r = pl.multiple_of(i * T, T)
        normed[0, pl.ds(r, T), :] = ((res[0, pl.ds(r, T), :] - mean) * scale + shift).astype(BF16)
        return carry

    lax.fori_loop(0, POS // T, third, 0)
    stats[0] = jnp.concatenate([mean, rstd, jnp.zeros((6, CH), F32)], axis=0)

    @pl.when(c == pl.num_programs(0) - 1)
    def _():
        pltpu.make_async_copy(w, w_out, sem_out).wait()


def whole(shape):
    return pl.BlockSpec(shape, lambda *_: (0,) * len(shape), pipeline_mode=pl.Buffered(1))


def per_clip(shape):
    return pl.BlockSpec((1,) + shape, lambda c, *_: (c,) + (0,) * len(shape))


def conv_forward(frames, dest, e, o, inp, emb, params, pieces, chunks):
    n = inp.shape[0]
    copies = sum(p.shape[0] for p in pieces)
    return pl.pallas_call(
        functools.partial(conv_kernel, chunks),
        out_shape=(
            jax.ShapeDtypeStruct((n, POS, CH), F32),
            jax.ShapeDtypeStruct((n, POS, CH), BF16),
            jax.ShapeDtypeStruct((n, 8, CH), F32),
            jax.ShapeDtypeStruct((NBLK, BS, BS), BF16),
        ),
        grid_spec=pltpu.PrefetchScalarGridSpec(
            num_scalar_prefetch=2,
            grid=(n,),
            in_specs=[
                pl.BlockSpec(memory_space=pl.ANY),
                pl.BlockSpec(memory_space=pl.ANY),
                pl.BlockSpec(memory_space=pl.ANY),
                per_clip((16, CH)),
                whole((8, CH)),
            ]
            + [pl.BlockSpec(memory_space=pl.ANY)] * len(pieces),
            out_specs=[
                per_clip((POS, CH)),
                per_clip((POS, CH)),
                per_clip((8, CH)),
                pl.BlockSpec(memory_space=pl.ANY),
            ],
            scratch_shapes=[
                pltpu.VMEM((NBLK, BS, BS), BF16),
                pltpu.VMEM((n, 3, POS, CH), BF16),
                pltpu.VMEM((n, 3, POS + 16, CH), BF16),
                pltpu.VMEM((n, POS, CH), F32),
                pltpu.SemaphoreType.DMA((copies,)),
                pltpu.SemaphoreType.DMA((3 * n,)),
                pltpu.SemaphoreType.DMA(()),
            ],
        ),
        compiler_params=pltpu.CompilerParams(vmem_limit_bytes=VMEM_LIMIT),
        cost_estimate=pl.CostEstimate(
            flops=n * POS * CH * CH * 18, bytes_accessed=n * POS * CH * 22 + 5000000, transcendentals=0
        ),
        name="conv_forward",
    )(frames, dest, e, o, inp, emb, params, *pieces)


def attn_kernel(
    frames_s, normed, tokens, tok_t, kmask, outlow, res, params, w,
    block_out, dq_ref, dw_ref,
    q_s, do_s, qt_s, dot_s, mixed_s, dkt_s, dvt_s, dkv_acc, km_s, s_s, dp_s, pb_s, ds_s, odq_s, dw_s,
):
    c = pl.program_id(0)
    rows = frames_s[c] * BINS
    R = 256
    C = 32
    def project(i, carry):
        r = pl.multiple_of(i * R, R)
        q = (nn(normed[0, pl.ds(r, R), :], mat(w, SQ, 4, 4)) * INV_WIDTH).astype(BF16)
        q_s[pl.ds(r, R), :] = q
        qt_s[:, pl.ds(r, R)] = q.T
        d = (nt(outlow[0, pl.ds(r, R), :], mat(w, 2 * SQ, 4, 4)) * OUT_SCALE).astype(BF16)
        do_s[pl.ds(r, R), :] = d
        dot_s[:, pl.ds(r, R)] = d.T
        return carry

    lax.fori_loop(0, POS // R, project, 0)
    lane = lax.broadcasted_iota(jnp.int32, (1, BS), 1)
    first = lane < HEADDIM
    keys = ((nn(tokens[0], mat(w, 3 * SQ, CTX // BS, 4)) * INV_CTX).astype(BF16).astype(F32) * ATT_SCALE).astype(BF16)
    values = (nn(tokens[0], mat(w, 3 * SQ + KV, CTX // BS, 4)) * INV_CTX).astype(BF16)
    for slab in range(HEADS // 2):
        for j, side in enumerate((keys, values)):
            two = side[:, slab * BS : (slab + 1) * BS]
            none = jnp.zeros_like(two)
            km_s[slab, 2 * j] = jnp.where(first, two, none)
            km_s[slab, 2 * j + 1] = jnp.where(first, none, two)
    dkv_acc[...] = jnp.zeros_like(dkv_acc)
    pb_s[1] = jnp.zeros(pb_s.shape[1:], BF16)
    ds_s[1] = jnp.zeros(ds_s.shape[1:], BF16)
    valid = kmask[0, 0:1, :] > 0.0
    RA = s_s.shape[1]
    tiles = POS // RA
    steps = HEADS // 2 * tiles

    def place(i):
        slab = i // tiles
        return slab, pl.ds(pl.multiple_of(slab * BS, BS), BS), pl.ds(pl.multiple_of(i % tiles * RA, RA), RA)

    def scores(i, h):
        slab, cols, at = place(i)
        s_s[h] = nt(q_s[at, cols], km_s[slab, h])
        dp_s[h] = nt(do_s[at, cols], km_s[slab, 2 + h])

    def soften(h):
        for j in range(RA // C):
            part = slice(j * C, (j + 1) * C)
            s = jnp.where(valid, s_s[h, part, :], -1000000000.0)
            e = jnp.exp(s - jnp.max(s, axis=-1, keepdims=True))
            p = e * (1.0 / jnp.sum(e, axis=-1, keepdims=True))
            pb_s[h, part, :] = p.astype(BF16)
            dp = dp_s[h, part, :]
            delta = jnp.sum(p * dp, axis=-1, keepdims=True)
            ds_s[h, part, :] = (p * (dp - delta)).astype(BF16)

    def back(i, h):
        slab, cols, at = place(i)
        half = pl.ds(pl.multiple_of(slab * BS + h * HEADDIM, HEADDIM), HEADDIM)
        mine = slice(h * HEADDIM, (h + 1) * HEADDIM)
        pb, ds = pb_s[h], ds_s[h]
        dkv_acc[slab, 0, mine, :] += nn(qt_s[half, at], ds)
        dkv_acc[slab, 1, mine, :] += nn(dot_s[half, at], pb)
        o, dq = nn(pb, km_s[slab, 2 + h]), nn(ds, km_s[slab, h])
        if h == 0:
            odq_s[0] = o
            odq_s[1] = dq
        else:
            mixed_s[at, cols] = (odq_s[0] + o).astype(BF16)
            dq_ref[0, at, cols] = (odq_s[1] + dq).astype(BF16)

    scores(0, 0)

    def step(i, carry):
        back(jnp.maximum(i - 1, 0), 1)
        scores(i, 1)
        soften(0)
        back(i, 0)
        scores(jnp.minimum(i + 1, steps - 1), 0)
        soften(1)
        return carry

    odq_s[...] = jnp.zeros_like(odq_s)
    def four(i, carry):
        for u in range(4):
            carry = step(4 * i + u, carry)
        return carry

    lax.fori_loop(0, steps // 4, four, 0)
    back(steps - 1, 1)
    for slab in range(HEADS // 2):
        cols = slice(slab * BS, (slab + 1) * BS)
        dkt_s[cols, :] = (dkv_acc[slab, 0] * ATT_SCALE).astype(BF16)
        dvt_s[cols, :] = dkv_acc[slab, 1].astype(BF16)

    def project_out(i, carry):
        r = pl.multiple_of(i * R, R)
        proj = nn(mixed_s[pl.ds(r, R), :], mat(w, 2 * SQ, 4, 4)) * OUT_SCALE + params[5:6]
        m = row_iota(r, R) < rows
        block_out[0, pl.ds(r, R), :] = jnp.where(m, res[0, pl.ds(r, R), :] + proj, 0.0)
        return carry

    lax.fori_loop(0, POS // R, project_out, 0)

    @pl.when(c == 0)
    def _():
        dw_s[...] = jnp.zeros_like(dw_s)

    dw_s[0:CH, :] += nn(normed[0].T, dq_ref[0])
    dw_s[CH : 2 * CH, :] += nn(mixed_s[...].T, outlow[0])
    dw_s[2 * CH : 2 * CH + CTX, :] += nt(tok_t[0], dkt_s[...])
    dw_s[2 * CH + CTX :, :] += nt(tok_t[0], dvt_s[...])

    @pl.when(c == pl.num_programs(0) - 1)
    def _():
        def cut(i, carry):
            r = pl.multiple_of(i * BS, BS)
            scale = jnp.where(i < CH // BS, INV_WIDTH, jnp.where(i < 2 * CH // BS, OUT_SCALE, INV_CTX))
            low = (dw_s[pl.ds(r, BS), :] * scale).astype(BF16)
            for b in range(CH // BS):
                dw_ref[i * (CH // BS) + b] = low[:, b * BS : (b + 1) * BS]
            return carry

        lax.fori_loop(0, dw_s.shape[0] // BS, cut, 0)


def attention(frames, normed, tokens, tok_t, kmask, outlow, res, params, w):
    n = normed.shape[0]
    ctx_len = tokens.shape[1]
    amount = SQ + SQ + SQ + KV + KV
    return pl.pallas_call(
        attn_kernel,
        out_shape=(
            jax.ShapeDtypeStruct((n, POS, CH), F32),
            jax.ShapeDtypeStruct((n, POS, CH), BF16),
            jax.ShapeDtypeStruct((NBLK - QUERY0, BS, BS), BF16),
        ),
        grid_spec=pltpu.PrefetchScalarGridSpec(
            num_scalar_prefetch=1,
            grid=(n,),
            in_specs=[
                per_clip((POS, CH)),
                per_clip((ctx_len, CTX)),
                per_clip((CTX, ctx_len)),
                per_clip((8, ctx_len)),
                per_clip((POS, CH)),
                per_clip((POS, CH)),
                whole((8, CH)),
                pl.BlockSpec(
                    (pl.Element(amount), pl.Element(BS), pl.Element(BS)),
                    lambda *_: (TEMB0, 0, 0),
                    pipeline_mode=pl.Buffered(1),
                ),
            ],
            out_specs=[
                per_clip((POS, CH)),
                per_clip((POS, CH)),
                pl.BlockSpec((NBLK - QUERY0, BS, BS), lambda *_: (0, 0, 0)),
            ],
            scratch_shapes=[
                pltpu.VMEM((POS, CH), BF16),
                pltpu.VMEM((POS, CH), BF16),
                pltpu.VMEM((CH, POS), BF16),
                pltpu.VMEM((CH, POS), BF16),
                pltpu.VMEM((POS, CH), BF16),
                pltpu.VMEM((CH, ctx_len), BF16),
                pltpu.VMEM((CH, ctx_len), BF16),
                pltpu.VMEM((HEADS // 2, 2, BS, ctx_len), F32),
                pltpu.VMEM((HEADS // 2, 4, ctx_len, BS), BF16),
                pltpu.VMEM((2, 256, ctx_len), F32),
                pltpu.VMEM((2, 256, ctx_len), F32),
                pltpu.VMEM((2, 256, ctx_len), BF16),
                pltpu.VMEM((2, 256, ctx_len), BF16),
                pltpu.VMEM((2, 256, BS), F32),
                pltpu.VMEM((2 * CH + 2 * CTX, CH), F32),
            ],
        ),
        compiler_params=pltpu.CompilerParams(vmem_limit_bytes=VMEM_LIMIT),
        cost_estimate=pl.CostEstimate(
            flops=n * POS * CH * (6 * CH * 2 + 24 * ctx_len),
            bytes_accessed=n * POS * CH * 16,
            transcendentals=n * POS * HEADS * ctx_len,
        ),
        name="attention",
    )(frames, normed, tokens, tok_t, kmask, outlow, res, params, w)


def taps_kernel(
    counts, frames_s, slots_s, owned_s, dq_ref, res, stats, cot, params, w, at, emb, dw_att,
    rgrad, sums, e_out, o_out, *refs,
):
    outs, refs = refs[: len(counts)], refs[len(counts) :]
    ng_s, pad, e_ref, o_ref, blocks, sem, sem_w = refs
    n = e_ref.shape[0]
    step = pl.program_id(0)
    T = 64

    @pl.when(step == 0)
    def _():
        blocks[NBLK] = jnp.zeros((BS, BS), BF16)
        pltpu.make_async_copy(dw_att, blocks.at[pl.ds(QUERY0, NBLK - QUERY0)], sem.at[0]).start()

    @pl.when(step < n)
    def _():
        rows = frames_s[step] * BINS
        R = 256
        zero = jnp.zeros((8, CH), F32)
        inv_n = 1.0 / (rows * (CH // GROUPS)).astype(F32)
        mean, rstd = stats[0, 0:1], stats[0, 1:2]
        gain = params[3:4]

        def first(i, carry):
            s0, s1 = carry
            r = pl.multiple_of(i * R, R)
            ng = nt(dq_ref[0, pl.ds(r, R), :], mat(w, 0, 4, 4)) * INV_WIDTH
            m = row_iota(r, R) < rows
            ng = jnp.where(m, ng, 0.0)
            ng_s[pl.ds(r, R), :] = ng
            x = jnp.where(m, (res[0, pl.ds(r, R), :] - mean) * rstd, 0.0)
            return (s0 + fold8(ng), s1 + fold8(ng * x))

        s0, s1 = lax.fori_loop(0, POS // R, first, (zero, zero))
        mh, mhx = group_sums(s0 * gain, s1 * gain)
        scale, mh, mhx = rstd * gain, rstd * mh * inv_n, rstd * mhx * inv_n
        pad[0:8, :] = zero
        pad[8 + POS :, :] = zero

        def second(i, s):
            r = pl.multiple_of(i * T, T)
            m = row_iota(r, T) < rows
            x = (res[0, pl.ds(r, T), :] - mean) * rstd
            d = scale * ng_s[pl.ds(r, T), :] - mh - x * mhx
            g = jnp.where(m, cot[0, pl.ds(r, T), :] + d, 0.0)
            rgrad[0, pl.ds(r, T), :] = g
            pad[pl.ds(r + 8, T), :] = g
            return s + fold8(g)

        s2 = lax.fori_loop(0, POS // T, second, zero)
        sums[pl.ds(step, 1)] = jnp.concatenate([s2, s1, s0], axis=0)[None]
        write_windows(pad, e_ref, o_ref, -1, step)
        pltpu.make_async_copy(e_ref.at[step], e_out.at[step], sem_w.at[2 * step]).start()
        pltpu.make_async_copy(o_ref.at[step], o_out.at[step], sem_w.at[2 * step + 1]).start()

    def cut(value, first):
        low = value.astype(BF16)
        for a in range(4):
            for b in range(4):
                blocks[first + a * 4 + b] = low[a * BS : (a + 1) * BS, b * BS : (b + 1) * BS]

    @pl.when(step >= n)
    def _():
        d = step - n
        for df in range(3):
            acc = None
            for c in range(n):
                g = window(e_ref, o_ref, 2 - df, d, 0, POS, (c,))
                part = nn(at[:, c * POS : (c + 1) * POS], g)
                acc = part if acc is None else acc + part
            cut(acc * CONV_SCALE, (3 * df + d) * SQ)

    @pl.when(step == pl.num_programs(0) - 1)
    def _():
        rows = [jnp.sum(sums[c, 0:8], axis=0, keepdims=True) for c in range(n)]
        grad = jnp.concatenate(rows + [jnp.zeros((16 - n, CH), F32)], axis=0).astype(BF16)
        outer = lax.dot_general(emb[...], grad, (((0,), (0,)), ((), ())), preferred_element_type=F32)
        cut(outer * INV_WIDTH, TEMB0)
        pltpu.make_async_copy(dw_att, blocks.at[pl.ds(QUERY0, NBLK - QUERY0)], sem.at[0]).wait()
        start = sum(counts)
        for q in reversed(range(len(counts))):
            start -= counts[q]

            def send(i, carry, q=q, start=start):
                for u in range(8):
                    t = i * 8 + u
                    src = owned_s[slots_s[start + t]]
                    pltpu.make_async_copy(blocks.at[src], outs[q].at[t], sem.at[1 + q]).start()
                return carry

            lax.fori_loop(0, counts[q] // 8, send, 0)
        for c in range(n):
            pltpu.make_async_copy(e_ref.at[c], e_out.at[c], sem_w.at[2 * c]).wait()
            pltpu.make_async_copy(o_ref.at[c], o_out.at[c], sem_w.at[2 * c + 1]).wait()
        for q, out in enumerate(outs):
            pltpu.make_async_copy(out, out, sem.at[1 + q]).wait()


def tap_gradients(frames, slots, owned, dq, res, stats, cot, params, w, at, emb, dw_att, counts):
    n = dq.shape[0]

    def of_clip(shape):
        return pl.BlockSpec((1,) + shape, lambda i, *_: (jnp.minimum(i, n - 1),) + (0,) * len(shape))

    any_space = pl.BlockSpec(memory_space=pl.ANY)
    return pl.pallas_call(
        functools.partial(taps_kernel, counts),
        out_shape=(
            jax.ShapeDtypeStruct((n, POS, CH), F32),
            jax.ShapeDtypeStruct((n, 24, CH), F32),
            jax.ShapeDtypeStruct((n, 3, POS, CH), BF16),
            jax.ShapeDtypeStruct((n, 3, POS + 16, CH), BF16),
        )
        + tuple(jax.ShapeDtypeStruct((s, BS, BS), BF16) for s in counts),
        grid_spec=pltpu.PrefetchScalarGridSpec(
            num_scalar_prefetch=3,
            grid=(n + 3,),
            in_specs=[
                of_clip((POS, CH)),
                of_clip((POS, CH)),
                of_clip((8, CH)),
                of_clip((POS, CH)),
                whole((8, CH)),
                pl.BlockSpec((SQ, BS, BS), lambda *_: (QUERY0 // SQ, 0, 0), pipeline_mode=pl.Buffered(1)),
                whole((CH, n * POS)),
                whole((16, CH)),
                any_space,
            ],
            out_specs=[of_clip((POS, CH)), pl.BlockSpec((n, 24, CH), lambda *_: (0, 0, 0)), any_space, any_space]
            + [any_space] * len(counts),
            scratch_shapes=[
                pltpu.VMEM((POS, CH), F32),
                pltpu.VMEM((POS + 16, CH), F32),
                pltpu.VMEM((n, 3, POS, CH), BF16),
                pltpu.VMEM((n, 3, POS + 16, CH), BF16),
                pltpu.VMEM((NBLK + 1, BS, BS), BF16),
                pltpu.SemaphoreType.DMA((1 + len(counts),)),
                pltpu.SemaphoreType.DMA((2 * n,)),
            ],
        ),
        compiler_params=pltpu.CompilerParams(vmem_limit_bytes=VMEM_LIMIT),
        cost_estimate=pl.CostEstimate(
            flops=n * POS * CH * CH * 20, bytes_accessed=n * POS * CH * 30 + 20000000, transcendentals=0
        ),
        name="tap_gradients",
    )(frames, slots, owned, dq, res, stats, cot, params, w, at, emb, dw_att)


def transposed_conv(e_ref, o_ref, w, out):
    R = 512

    def conv(i, carry):
        r = pl.multiple_of(i * R, R)
        acc = jnp.zeros((R, CH), F32)
        for t in range(9):
            df, db = divmod(t, 3)
            acc = acc + nt(window(e_ref, o_ref, 2 - df, db, r, R), mat(w, t * SQ, 4, 4))
        out[pl.ds(r, R), :] = acc * CONV_SCALE
        return carry

    lax.fori_loop(0, POS // R, conv, 0)


def acts_grad_kernel(e_ref, o_ref, w, out):
    transposed_conv(e_ref, o_ref, w, out)


def acts_gradient(clip, e, o, w):
    def of_clip(shape):
        return pl.BlockSpec(
            (1,) + shape, lambda *_: (clip,) + (0,) * len(shape), pipeline_mode=pl.Buffered(1)
        )

    return pl.pallas_call(
        acts_grad_kernel,
        out_shape=jax.ShapeDtypeStruct((POS, CH), F32),
        grid=(1,),
        in_specs=[
            of_clip((3, POS, CH)),
            of_clip((3, POS + 16, CH)),
            pl.BlockSpec((TEMB0, BS, BS), lambda *_: (0, 0, 0), pipeline_mode=pl.Buffered(1)),
        ],
        out_specs=pl.BlockSpec((POS, CH), lambda *_: (0, 0)),
        compiler_params=pltpu.CompilerParams(vmem_limit_bytes=VMEM_LIMIT),
        cost_estimate=pl.CostEstimate(flops=POS * CH * CH * 18, bytes_accessed=POS * CH * 24, transcendentals=0),
        name="acts_gradient",
    )(e, o, w)


def input_kernel(clip, frames_s, ag, inp, stats, rgrad, params, *refs):
    out, sums, dy_s = refs[-3:]
    norm1_backward(clip, frames_s, ag, inp, stats, rgrad, params, out, sums, dy_s)


def clip_kernel(clip, frames_s, e_ref, o_ref, w, inp, stats, rgrad, params, *refs):
    out, sums, dy_s = refs[-3:]
    transposed_conv(e_ref, o_ref, w, dy_s)
    norm1_backward(clip, frames_s, dy_s, inp, stats, rgrad, params, out, sums, dy_s)


def norm1_backward(clip, frames_s, ag, inp, stats, rgrad, params, out, sums, dy_s):
    rows = frames_s[clip] * BINS
    T = 64
    zero = jnp.zeros((8, CH), F32)
    inv_n = 1.0 / (rows * (CH // GROUPS)).astype(F32)
    mean, rstd = stats[0, 0:1], stats[0, 1:2]
    gain, shift = params[0:1], params[1:2]

    def first(i, carry):
        s0, s1 = carry
        r = pl.multiple_of(i * T, T)
        m = row_iota(r, T) < rows
        x = (inp[0, pl.ds(r, T), :] - mean) * rstd
        y = x * gain + shift
        sg = jax.nn.sigmoid(y)
        dy = jnp.where(m, ag[pl.ds(r, T), :] * (sg * (1.0 + y * (1.0 - sg))), 0.0)
        dy_s[pl.ds(r, T), :] = dy
        return (s0 + fold8(dy), s1 + fold8(dy * x))

    s0, s1 = lax.fori_loop(0, POS // T, first, (zero, zero))
    mh, mhx = group_sums(s0 * gain, s1 * gain)
    scale, mh, mhx = rstd * gain, rstd * mh * inv_n, rstd * mhx * inv_n

    def second(i, carry):
        r = pl.multiple_of(i * T, T)
        m = row_iota(r, T) < rows
        x = (inp[0, pl.ds(r, T), :] - mean) * rstd
        d = scale * dy_s[pl.ds(r, T), :] - mh - x * mhx
        out[0, pl.ds(r, T), :] = jnp.where(m, rgrad[0, pl.ds(r, T), :] + d, 0.0)
        return carry

    lax.fori_loop(0, POS // T, second, 0)
    sums[0, 0:8] = s1
    sums[0, 8:16] = s0


def input_backward(clip, frames, ag, inp, stats, rgrad, params, before=None):
    n = inp.shape[0]

    def of_clip(shape):
        return pl.BlockSpec((1,) + shape, lambda *_: (clip,) + (0,) * len(shape))

    before = () if before is None else (before,)
    return pl.pallas_call(
        functools.partial(input_kernel, clip),
        out_shape=(
            jax.ShapeDtypeStruct((n, POS, CH), F32),
            jax.ShapeDtypeStruct((1, 16, CH), F32),
        ),
        grid_spec=pltpu.PrefetchScalarGridSpec(
            num_scalar_prefetch=1,
            grid=(1,),
            in_specs=[whole((POS, CH)), of_clip((POS, CH)), of_clip((8, CH)), of_clip((POS, CH)), whole((8, CH))]
            + [pl.BlockSpec(memory_space=pl.ANY)] * len(before),
            out_specs=[of_clip((POS, CH)), pl.BlockSpec((1, 16, CH), lambda *_: (0, 0, 0))],
            scratch_shapes=[pltpu.VMEM((POS, CH), F32)],
        ),
        input_output_aliases={6: 0} if before else {},
        compiler_params=pltpu.CompilerParams(vmem_limit_bytes=VMEM_LIMIT),
        cost_estimate=pl.CostEstimate(flops=POS * CH * 30, bytes_accessed=POS * CH * 20, transcendentals=POS * CH),
        name="input_backward",
    )(frames, ag, inp, stats, rgrad, params, *before)


def whole_backward(clip, frames, e, o, w, inp, stats, rgrad, params, before):
    n = inp.shape[0]

    def of_clip(shape, **mode):
        return pl.BlockSpec((1,) + shape, lambda *_: (clip,) + (0,) * len(shape), **mode)

    once = {"pipeline_mode": pl.Buffered(1)}
    return pl.pallas_call(
        functools.partial(clip_kernel, clip),
        out_shape=(
            jax.ShapeDtypeStruct((n, POS, CH), F32),
            jax.ShapeDtypeStruct((1, 16, CH), F32),
        ),
        grid_spec=pltpu.PrefetchScalarGridSpec(
            num_scalar_prefetch=1,
            grid=(1,),
            in_specs=[
                of_clip((3, POS, CH), **once),
                of_clip((3, POS + 16, CH), **once),
                pl.BlockSpec((TEMB0, BS, BS), lambda *_: (0, 0, 0), pipeline_mode=pl.Buffered(1)),
                of_clip((POS, CH)),
                of_clip((8, CH)),
                of_clip((POS, CH)),
                whole((8, CH)),
                pl.BlockSpec(memory_space=pl.ANY),
            ],
            out_specs=[of_clip((POS, CH)), pl.BlockSpec((1, 16, CH), lambda *_: (0, 0, 0))],
            scratch_shapes=[pltpu.VMEM((POS, CH), F32)],
        ),
        input_output_aliases={8: 0},
        compiler_params=pltpu.CompilerParams(vmem_limit_bytes=VMEM_LIMIT),
        cost_estimate=pl.CostEstimate(
            flops=POS * CH * CH * 18, bytes_accessed=POS * CH * 24, transcendentals=POS * CH
        ),
        name="whole_backward",
    )(frames, e, o, w, inp, stats, rgrad, params, before)


def norm_grads_kernel(me_s, obias, sums2, *refs):
    sums1, keep, send = refs[:-2], refs[-2], refs[-1]
    nx, n_data = keep.shape[0], keep.shape[1]
    width = CH // (2 * nx * n_data)
    total = lambda v: jnp.sum(v, axis=0, keepdims=True)
    first = sums1[0][0]
    for v in sums1[1:]:
        first = first + v[0]
    second, bias = sums2[0], obias[0]
    for i in range(1, sums2.shape[0]):
        second, bias = second + sums2[i], bias + obias[i]
    grads = jnp.concatenate(
        [
            total(first[0:8]), total(first[8:16]), total(second[0:8]), total(second[8:16]),
            total(second[16:24]), total(bias), jnp.zeros((2, CH), F32),
        ],
        axis=0,
    )
    lane = lax.broadcasted_iota(jnp.int32, (8, BS), 1)
    for x in range(nx):
        far = lax.rem(x - me_s[0] + nx, nx)
        for c in range(2):
            tiles = []
            for d in range(n_data):
                at = (d * 2 * nx + x * 2 + c) * width
                tile = grads[:, at // BS * BS : (at // BS + 1) * BS]
                tile = pltpu.roll(tile, (BS - at % BS) % BS, 1)
                tiles.append(jnp.where(lane < width, tile, 0.0)[None])
            tiles = jnp.concatenate(tiles, axis=0)

            @pl.when(me_s[1] == c)
            def _():
                keep[far] = tiles

            @pl.when(me_s[1] != c)
            def _():
                send[far] = tiles


def norm_grad_tiles(n_data, me, obias, sums2, sums1, n_model):
    vm = pl.BlockSpec(memory_space=pltpu.VMEM)
    shape = jax.ShapeDtypeStruct((n_model // 2, n_data, 8, BS), F32)
    return pl.pallas_call(
        norm_grads_kernel,
        out_shape=(shape, shape),
        in_specs=[pl.BlockSpec(memory_space=pltpu.SMEM)] + [vm] * (2 + len(sums1)),
        out_specs=[vm, vm],
        cost_estimate=SMALL,
        name="norm_grads",
    )(me, obias, sums2, *sums1)


def sinusoid(timesteps):
    half_width = CH // 2
    freqs = jnp.exp(-math.log(10000.0) * jnp.arange(half_width, dtype=F32) / half_width)
    angles = timesteps.astype(F32)[:, None] * freqs[None, :]
    return jnp.concatenate([jnp.sin(angles), jnp.cos(angles)], axis=-1)


def step_kernel(split, dp_s, *refs):
    first, second = refs[: split[0]], refs[split[0] : split[0] + split[1]]
    left_root, right_root, step, stats = refs[sum(split) :]
    k0, k1 = first[0].shape[0], second[0].shape[0]
    n_data, row_share = step.shape[0], step.shape[2]
    offset = dp_s[1]
    for i in range(k0 + k1):
        parts = [r[i] for r in first] if i < k0 else [r[i - k0] for r in second]
        g = add_low(*parts)
        low = g.astype(BF16)
        root = jnp.minimum(i + offset, left_root.shape[0] - 1)
        left = nt(low, low)
        right = lax.dot_general(low, low, (((0,), (0,)), ((), ())), preferred_element_type=F32)
        side = nn(left_root[root].astype(BF16), low)
        update = nn(side.astype(BF16), right_root[root].astype(BF16))
        rate = learn_rate * lax.rsqrt(jnp.sum(update * update, keepdims=True) * (1.0 / (BS * BS)) + 1e-06)
        step[:, i] = (update * rate).reshape(n_data, row_share, BS).astype(BF16)
        for j, value in enumerate((g, left, right)):
            stats[:, 3 * i + j] = value.reshape(n_data, row_share, BS).astype(BF16)
    for j in range(16 // row_share):
        stats[:, 3 * (k0 + k1) + j] = jnp.zeros((n_data, row_share, BS), BF16)


def owner_step(dp, first, second, left_root, right_root, row_share):
    first = [v.reshape(-1, BS, BS) for v in first]
    second = [v.reshape(-1, BS, BS) for v in second]
    k = first[0].shape[0] + second[0].shape[0]
    n_data = BS // row_share
    entries = 3 * k + 16 // row_share
    start = jnp.minimum(dp * k, left_root.shape[0] - k)
    where = jnp.concatenate([start, dp * k - start])
    root = pl.BlockSpec((pl.Element(k), pl.Element(BS), pl.Element(BS)), lambda i, w: (w[0], 0, 0))
    full = lambda shape: pl.BlockSpec(shape, lambda i, w: (0,) * len(shape))
    return pl.pallas_call(
        functools.partial(step_kernel, (len(first), len(second))),
        out_shape=(
            jax.ShapeDtypeStruct((n_data, k, row_share, BS), BF16),
            jax.ShapeDtypeStruct((n_data, entries, row_share, BS), BF16),
        ),
        grid_spec=pltpu.PrefetchScalarGridSpec(
            num_scalar_prefetch=1,
            grid=(1,),
            in_specs=[full(v.shape) for v in first + second] + [root, root],
            out_specs=[full((n_data, k, row_share, BS)), full((n_data, entries, row_share, BS))],
        ),
        cost_estimate=pl.CostEstimate(flops=k * 8 * BS**3, bytes_accessed=k * BS * BS * 20, transcendentals=0),
        name="owner_step",
    )(where, *first, *second, left_root, right_root)


def add_tiles_kernel(*refs):
    tiles, (_, stats, pair, sem) = refs[:-4], refs[-4:]
    tile = add_low(*[t[...] for t in tiles])
    high = tile.astype(BF16)
    both = jnp.concatenate([high, (tile - high.astype(F32)).astype(BF16)], axis=1)
    count, row_share = pair.shape[1], pair.shape[2]
    for j in range(count):
        pair[:, j] = both[:, j * row_share : (j + 1) * row_share]
    copy = pltpu.make_async_copy(pair, stats.at[:, pl.ds(stats.shape[1] - count, count)], sem)
    copy.start()
    copy.wait()


def add_tiles(tiles, stats):
    vm = pl.BlockSpec(memory_space=pltpu.VMEM)
    any_space = pl.BlockSpec(memory_space=pl.ANY)
    n_data, _, row_share, _ = stats.shape
    return pl.pallas_call(
        add_tiles_kernel,
        out_shape=jax.ShapeDtypeStruct(stats.shape, BF16),
        in_specs=[vm] * len(tiles) + [any_space],
        out_specs=any_space,
        scratch_shapes=[pltpu.VMEM((n_data, 16 // row_share, row_share, BS), BF16), pltpu.SemaphoreType.DMA(())],
        input_output_aliases={len(tiles): 0},
        cost_estimate=SMALL,
        name="add_tiles",
    )(*tiles, stats)


def master_kernel(where_s, master, near, far, new, low, steps):
    half = near.shape[0]
    steps[0:half] = near[...].astype(F32)
    steps[half:] = far[...].astype(F32)

    def one(j, carry):
        value = master[j] - steps[where_s[j]]
        new[j] = value
        low[j] = value.astype(BF16)
        return carry

    lax.fori_loop(0, master.shape[0], one, 0)


def update_master(where, master, near, far):
    vm = pl.BlockSpec(memory_space=pltpu.VMEM)
    return pl.pallas_call(
        master_kernel,
        out_shape=(
            jax.ShapeDtypeStruct(master.shape, F32),
            jax.ShapeDtypeStruct(master.shape, BF16),
        ),
        in_specs=[pl.BlockSpec(memory_space=pltpu.SMEM), vm, vm, vm],
        out_specs=[vm, vm],
        scratch_shapes=[pltpu.VMEM((2 * near.shape[0],) + near.shape[1:], F32)],
        cost_estimate=pl.CostEstimate(flops=300000, bytes_accessed=3000000, transcendentals=0),
        name="update_master",
    )(where, master, near, far)


class Grid:
    def __init__(self, n_data, n_model):
        self.nd, self.nm = n_data, n_model
        self.nx = n_model // 2
        self.ny = 1
        while self.ny * self.ny * 4 <= n_data:
            self.ny *= 2
        self.nz = n_data // self.ny
        self.split = self.nx == self.ny
        self.sizes = (self.ny, self.ny) if self.split else (self.ny, self.nx)
        dp, mp = lax.axis_index("dp"), lax.axis_index("mp")
        self.z, self.y, self.x, self.c = dp // self.ny, dp % self.ny, mp // 2, mp % 2

    def permute(self, value, fn):
        pairs = []
        for src in range(self.nd * self.nm):
            dp, mp = divmod(src, self.nm)
            z, y, x, c = fn(dp // self.ny, dp % self.ny, mp // 2, mp % 2)
            dst = ((z % self.nz) * self.ny + y % self.ny) * self.nm + (x % self.nx) * 2 + c % 2
            pairs.append((src, dst))
        return lax.ppermute(value, ("dp", "mp"), pairs)

    def along_z(self, value, d):
        return self.permute(value, lambda z, y, x, c: (z + d, y, x, c))

    def along_plane(self, value, stage, d):
        def fn(z, y, x, c):
            on_y = (stage == 0) != (self.split and c == 1)
            return (z, y + d, x, c) if on_y else (z, y, x + d, c)

        return self.permute(value, fn)

    def along_core(self, value):
        return self.permute(value, lambda z, y, x, c: (z, y, x, c + 1))

    def place(self, core, d0, d1, dz):
        swap = (core == 1) if self.split else jnp.zeros_like(core == 1)
        dy, dx = jnp.where(swap, d1, d0), jnp.where(swap, d0, d1)
        zz, yy, xx = (self.z + dz) % self.nz, (self.y + dy) % self.ny, (self.x + dx) % self.nx
        return zz * self.ny + yy, xx * 2 + core


def after(value, *others):
    return lax.optimization_barrier((value,) + others)[0]


def after_all(values, *others):
    return list(lax.optimization_barrier(tuple(values) + others)[: len(values)])


def gather_z(grid, shard):
    return [shard] + [grid.along_z(shard, -d) for d in range(1, grid.nz)]


def gather_plane(grid, stack, stage):
    return [stack] + [grid.along_plane(stack, stage, -d) for d in range(1, grid.sizes[stage])]


def gather_core(grid, got):
    return got + [grid.along_core(v) for v in got]


def gather_places(grid):
    dps, mps = [], []
    for rel in range(2):
        core = (grid.c + rel) % 2
        for d1 in range(grid.sizes[1]):
            for d0 in range(grid.sizes[0]):
                for dz in range(grid.nz):
                    dp, mp = grid.place(core, d0, d1, dz)
                    dps.append(dp)
                    mps.append(mp)
    return jnp.stack(dps), jnp.stack(mps)


def add_low(*parts):
    total = parts[0].astype(F32)
    for p in parts[1:]:
        total = total + p.astype(F32)
    return total


def scatter_core(grid, keep, send):
    return add_low(keep, grid.along_core(send)).astype(BF16)


def send_plane(grid, value, stage):
    value = value.reshape(grid.sizes[stage], -1, BS, BS)
    return [value[0]] + [grid.along_plane(value[d], stage, d) for d in range(1, value.shape[0])]


def send_z(grid, value):
    value = value.reshape(grid.nz, -1, BS, BS)
    return [value[0]] + [grid.along_z(value[d], d) for d in range(1, value.shape[0])]


def body(
    clean_latent, noise_latent, codec_tokens, codec_mask, frames, timesteps, out_cotangent,
    master_blocks, norm_params, owned_block, left_stats, right_stats, left_root, right_root,
):
    n_data = lax.axis_size("dp")
    n_model = lax.axis_size("mp")
    total_devices = n_data * n_model
    clip_count = clean_latent.shape[0]
    ctx_len = codec_tokens.shape[1]
    slot_count, row_share = (master_blocks.shape[0], master_blocks.shape[1])
    param_rows, width = norm_params.shape
    grid = Grid(n_data, n_model)
    dp, mp = lax.axis_index("dp"), lax.axis_index("mp")
    me = dp * n_model + mp

    own_params = lax.dynamic_update_slice(
        jnp.zeros((8, CH), BF16), norm_params.astype(BF16), (0, me * width)
    )
    param_tiles = own_params.reshape(8, CH // BS, BS).transpose(1, 0, 2).reshape(-1, row_share, BS)
    skip = param_tiles.shape[0]
    master_low = master_blocks.astype(BF16)
    cut = slot_count * 3 // 10
    chunks = ((skip, 0, cut), (0, cut, slot_count - cut))
    ring0 = gather_z(grid, jnp.concatenate([param_tiles, master_low[:cut]]))
    ring1 = gather_z(grid, master_low[cut:])
    place_dp, place_mp = gather_places(grid)
    dest = jnp.stack([place_mp * slot_count, place_dp * row_share])

    phases = timesteps.astype(F32) * (0.5 * math.pi / TSTEPS)
    trig = jnp.stack([jnp.cos(phases), jnp.sin(phases)])
    embedding = jax.nn.silu(sinusoid(timesteps)).astype(BF16)
    emb_rows = jnp.broadcast_to(embedding[:, None, :], (clip_count, 16, CH))
    emb_pad = jnp.pad(embedding, ((0, 16 - clip_count), (0, 0)))
    kmask = jnp.broadcast_to(codec_mask.astype(F32)[:, None, :], (clip_count, 8, ctx_len))
    tok_t = codec_tokens.transpose(0, 2, 1)

    k = slot_count // n_data + 1
    padded = n_data * k
    k0 = max(1, k // 8)

    planes = grid.sizes[0] * grid.sizes[1]
    half = n_model * padded // 2
    counts, slot_list = [], []
    for rel in range(2):
        core = (grid.c + rel) % 2
        for part, kk in ((0, k0), (1, k - k0)):
            t = jnp.arange(half // k * kk, dtype=jnp.int32)
            group, k_id = t // kk, t % kk + part * k0
            if part == 1:
                plane, dz = group // grid.nz, group % grid.nz
            else:
                plane, dz = group % planes, group // planes
            to_dp, to_mp = grid.place(core, plane % grid.sizes[0], plane // grid.sizes[0], dz)
            to_slot = to_dp * k + k_id
            slot_list.append(jnp.where(to_slot < slot_count, to_mp * slot_count + to_slot, NBLK))
            counts.append(half // k * kk)
    slots = jnp.concatenate(slot_list)
    owned = jnp.concatenate([owned_block, jnp.full((1,), NBLK, jnp.int32)])
    counts = tuple(counts)
    block_ids = jnp.arange(NBLK, dtype=jnp.int32)
    slot_of_block = jnp.sum(
        jnp.where(owned_block[None, :] == block_ids[:, None], block_ids[None, :], 0), axis=1
    )
    my_slots = lax.dynamic_slice_in_dim(slot_of_block, mp * slot_count, slot_count)
    from_mp = my_slots // slot_count
    where = (
        ((from_mp + grid.c) % 2 * grid.nx + (from_mp // 2 - grid.x) % grid.nx) * padded + my_slots % slot_count
    )

    stack0 = jnp.stack(ring0)
    got0 = jnp.concatenate(gather_plane(grid, stack0, 0))
    stack1 = jnp.stack(after_all(ring1, got0))
    got0 = gather_plane(grid, got0, 1)
    pieces = gather_core(grid, got0)
    got1 = jnp.concatenate(gather_plane(grid, stack1, 0))
    inp, outlow, stats1, obias = pre(after(frames, stack1), trig, clean_latent, noise_latent, out_cotangent)
    got1 = after(got1, stats1, *got0[1:])
    ready = after(frames, slots, owned, where, dest, kmask, emb_rows, emb_pad, tok_t)
    e1, o1, params = acts_windows(ready, inp, stats1, pieces)
    at = e1[:, 1].reshape(-1, CH).T
    got1 = gather_plane(grid, got1, 1)
    got1 = [got1[0]] + [after(v, e1) for v in got1[1:]]
    later = gather_core(grid, got1)
    e1 = after(e1, at)
    res, normed, stats2, blocks = conv_forward(
        frames, dest, e1, o1, inp, emb_rows, params, pieces + later, chunks
    )
    block_output, dq, dw_att = attention(
        frames, normed, codec_tokens, tok_t, kmask, outlow, res, params, blocks
    )
    rgrad, sums2, e2, o2, keep0, keep1, send0, send1 = tap_gradients(
        frames, slots, owned, dq, res, stats2, out_cotangent, params, blocks, at, emb_pad, dw_att, counts
    )

    value0 = scatter_core(grid, keep0, send0)
    value1 = scatter_core(grid, keep1, send1)
    ready = after(e2, value0, value1)
    moved0 = send_z(grid, value0)
    moved1 = send_plane(grid, value1, 1)
    ag = acts_gradient(0, ready, o2, blocks)
    moved = after_all(moved1 + moved0, ag)
    moved1, moved0 = moved[: len(moved1)], moved[len(moved1) :]
    value1 = add_low(*moved1).astype(BF16)
    moved1 = send_plane(grid, value1, 0)
    value0 = add_low(*moved0).astype(BF16)
    moved0 = send_plane(grid, value0, 1)
    input_grad, part = input_backward(0, after(frames, value1, value0), ag, inp, stats1, rgrad, params)
    sums1 = [part]
    moved = after_all(moved1 + moved0, part)
    moved1, moved0 = moved[: len(moved1)], moved[len(moved1) :]
    value1 = add_low(*moved1).astype(BF16)
    moved1 = send_z(grid, value1)
    value0 = add_low(*moved0).astype(BF16)
    moved0 = send_plane(grid, value0, 0)
    ready = after(e2, value1, value0)
    for clip in range(1, clip_count):
        input_grad, part = whole_backward(
            clip, frames, ready, o2, blocks, inp, stats1, rgrad, params, input_grad
        )
        sums1.append(part)
    moved = after_all(moved1 + moved0, part)
    moved1, moved0 = moved[: len(moved1)], moved[len(moved1) :]
    tiles, tiles_sent = norm_grad_tiles(
        n_data, jnp.stack([grid.x, grid.c]), after(obias, *moved1), sums2, sums1, n_model
    )
    step, stats = owner_step(dp[None], moved0, moved1, left_root, right_root, row_share)
    tiles = tiles + after(grid.along_core(tiles_sent), step)
    tiles = [tiles[0]] + [
        grid.permute(tiles[d], lambda z, y, x, c, d=d: (z, y, x + d, c)) for d in range(1, grid.nx)
    ]
    step = lax.all_to_all(step, "dp", 0, 0, tiled=True).reshape(padded, row_share, BS)
    stats = add_tiles(after_all(tiles, step), stats)
    near = jnp.concatenate(
        [step] + [grid.permute(step, lambda z, y, x, c, d=d: (z, y, x - d, c)) for d in range(1, grid.nx)]
    )
    far = grid.along_core(near)
    stats = lax.all_to_all(stats, "dp", 0, 0, tiled=True)
    tiles = jnp.sum(stats[:, 3 * k :].astype(F32), axis=0).reshape(16, BS)
    norm_grads = (tiles[0:8] + tiles[8:16])[:param_rows, :width]
    stats = stats[:, : 3 * k].reshape(padded, 3, row_share, BS)
    new_master, master_copy = update_master(where, master_blocks, near, far)
    owned_rows = stats[:slot_count, 0].astype(F32)
    new_left = 0.5 * left_stats + 0.5 * stats[:slot_count, 1].astype(F32)
    new_right = 0.5 * right_stats + 0.5 * stats[:slot_count, 2].astype(F32)
    small_rate = 0.5 / math.sqrt(clip_count * total_devices * POS)
    new_norm = norm_params - small_rate * norm_grads
    return (
        block_output, input_grad, owned_rows, new_left, new_right, new_master, master_copy,
        norm_grads, new_norm,
    )


def solution(mesh):
    cells = P(("dp", "mp"), None, None)
    rows = P("mp", "dp", None)
    in_specs = (
        cells, cells, cells, P(("dp", "mp"), None), P(("dp", "mp")), P(("dp", "mp")), cells,
        rows, P(None, ("dp", "mp")), P(), rows, rows, P("mp", None, None), P("mp", None, None),
    )
    out_specs = (
        cells, cells, rows, rows, rows, rows, rows, P(None, ("dp", "mp")), P(None, ("dp", "mp")),
    )
    return jax.shard_map(body, mesh=mesh, in_specs=in_specs, out_specs=out_specs, check_vma=False)
```
